32 devices in a mesh: row: 4 (over x, core), col: 8 (over z, y).
Axes of the slice: x: 2, y: 2, z: 4, core: 2. Of those that a mesh axis runs over, the one named last changes fastest.
Arguments:
- block_input: bfloat16 [8, 1024, 1024], P('col', 'row'), may hold values from -6 to 6
- state_start: bfloat16 [8, 512, 1024], P('col'), may hold values from -6 to 6
- teacher: bfloat16 [8, 1024, 1024], P('col', 'row'), may hold values from -6 to 6
- valid_mask: int32 [8, 1024], replicated, may hold values 0 or 1
- segment: int32 [8, 1024], P('col'), may hold values from 0 to 3, never falling along the last dimension, each value on 1 to 512 neighbouring positions
- image_offset: int32 [8, 2], P('col'), may hold values from 0 to 256
- retain: float32 [1024], replicated, may hold values from 0.55 to 0.995
- to_query: bfloat16 [1024, 1024], P('col', 'row'), may hold values from -0.1875 to 0.1875
- to_key: bfloat16 [1024, 1024], P('col', 'row'), may hold values from -0.1875 to 0.1875
- to_value: bfloat16 [1024, 1024], P('col', 'row'), may hold values from -0.1875 to 0.1875
- to_output: bfloat16 [1024, 1024], P('row', 'col'), may hold values from -4 to 4
- to_hidden: bfloat16 [1024, 4096], P('col'), may hold values from -0.1875 to 0.1875
- to_model: bfloat16 [4096, 1024], P(None, 'col'), may hold values from -0.09375 to 0.09375
- state_query: bfloat16 [1024, 1024], P('col', 'row'), may hold values from -0.1875 to 0.1875
- state_key: bfloat16 [1024, 1024], P('col', 'row'), may hold values from -0.1875 to 0.1875
- state_value: bfloat16 [1024, 1024], P('col', 'row'), may hold values from -0.1875 to 0.1875
- state_write: bfloat16 [1024, 1024], P(None, 'col'), may hold values from -4 to 4
- first_gain: float32 [1024], replicated, may hold values from 0.5 to 1.5
- second_gain: float32 [1024], replicated, may hold values from 0.5 to 1.5
- state_gain: float32 [1024], replicated, may hold values from 0.5 to 1.5
Outputs:
- total_loss: float32 [], replicated
- final_state: float32 [8, 512, 1024], P('col')
- input_grad: float32 [8, 1024, 1024], P('col', 'row')
- state_grad: float32 [8, 512, 1024], P('col')
- query_grad: float32 [1024, 1024], P('col', 'row')
- key_grad: float32 [1024, 1024], P('col', 'row')
- value_grad: float32 [1024, 1024], P('col', 'row')
- output_grad: float32 [1024, 1024], P('row', 'col')
- hidden_grad: float32 [1024, 4096], P('col', 'row')
- model_grad: float32 [4096, 1024], P('row', 'col')
- state_query_grad: float32 [1024, 1024], P('col', 'row')
- state_key_grad: float32 [1024, 1024], P('col', 'row')
- state_value_grad: float32 [1024, 1024], P('col', 'row')
- state_write_grad: float32 [1024, 1024], P('row', 'col')
- first_gain_grad: float32 [1024], replicated
- second_gain_grad: float32 [1024], replicated
- state_gain_grad: float32 [1024], replicated
The draws below stay inside these ranges and needn't reach their ends.
Inputs may be any that keep to these rules, and one draw needn't show every extreme that they name: `image_offset`: each block's image piece starts at this offset from the block's first token and ends inside the block. `segment`: document numbers never fall along a sequence; every one of the 4 numbers appears in each sequence.
All inputs are finite; a program needn't handle non-finite values.
Results may differ from the reference program's by a relative error of at most 0.02.
Values may be sent and summed in bfloat16 or wider, within the bound.
No kernel may reach another device: no remote copies, remote signals or barrier semaphores. Data moves between devices by JAX's collectives and lax.ppermute only.
A program may use at most 192 MiB of HBM per device.

```python
import math
import jax
import jax.numpy as jnp
import numpy as np
from jax import lax

D = 1024
HEADS = 8
HEAD = 128
FF = 4096
BLOCK = 512
NS = 512
PIECE = 256
LENGTH = 1024
SEQS = 8
NBLK = 2


def touch_ends(values, own_key, least, largest):
    shape = values.shape
    spot = [jax.random.randint(jax.random.fold_in(own_key, axis), (), 0, shape[axis]) for axis in range(len(shape))]
    values = values.at[tuple(spot)].set(least)
    longest = shape.index(max(shape))
    spot[longest] = (spot[longest] + 1) % shape[longest]
    return values.at[tuple(spot)].set(largest)


def level_of(key, dims, cuts, low, largest):
    def one(dim, parts):
        draws = jax.random.uniform(jax.random.fold_in(jax.random.fold_in(key, 6), dim), (parts,), jnp.float32, low / len(cuts), largest / len(cuts))
        return jnp.repeat(jnp.exp(draws), dims[dim] // parts).reshape((-1,) + (1,) * (len(dims) - dim - 1))

    loudness = one(*cuts[0])
    for cut in cuts[1:]:
        loudness = loudness * one(*cut)
    return loudness


def profile(amount, total, limit, lean):
    portions = [(1 << 20) // math.isqrt(rank ** lean) + 1 for rank in range(2, amount + 1)]
    surplus, holding = total - limit - (amount - 1), [1] * (amount - 1)
    while surplus > 0:
        free = [i for i in range(amount - 1) if holding[i] < limit]
        pool, remaining = sum([portions[i] for i in free]), surplus
        for i in free:
            more = min(limit - holding[i], max(1, remaining * portions[i] // pool), surplus)
            holding[i] = holding[i] + more
            surplus = surplus - more
    return np.array([limit] + holding)


def ragged_sizes(rng, number_of, total, most, slope):
    if number_of == 2:
        one = jax.random.randint(rng, (), max(1, total - most), min(most, total - 1) + 1)
        return jnp.stack([one, total - one])
    sizes = jnp.asarray(profile(number_of, total, most, slope), jnp.int32)
    twos = (number_of - 1) // 2
    donor, taker = sizes[1:1 + 2 * twos:2], sizes[2:2 + 2 * twos:2]
    room = jnp.minimum(donor - 1, most - taker)
    passed = jax.random.randint(jax.random.fold_in(rng, 1), (twos,), 0, 1 << 20) % (room + 1)
    sizes = sizes.at[1:1 + 2 * twos:2].set(donor - passed).at[2:2 + 2 * twos:2].set(taker + passed)
    return sizes[jax.random.permutation(jax.random.fold_in(rng, 2), number_of)]


def centred(stream_key, shape, spread, reach, split=(), kind=jnp.bfloat16):
    factor_of = level_of(stream_key, shape, split, -0.22, 0.18) if split else 1.0
    drawn = jax.random.normal(stream_key, shape, jnp.float32) * spread * factor_of
    return jnp.minimum(jnp.maximum(drawn, -reach), reach).astype(kind)


def setup_inputs(seed: int = 0) -> dict:
    key_list = jax.random.split(jax.random.key(seed), 21)
    block_input = centred(key_list[0], (SEQS, LENGTH, D), 1.0, 6.0, ((0, 8), (1, 4)))
    state_start = centred(key_list[1], (SEQS, NS, D), 1.0, 6.0, ((0, 8),))
    teacher = centred(key_list[2], (SEQS, LENGTH, D), 1.0, 6.0, ((0, 8), (1, 4)))
    valid_mask = touch_ends((jax.random.randint(key_list[3], (SEQS, LENGTH), 0, 16) < 15).astype(jnp.int32), jax.random.fold_in(key_list[3], 1), 0, 1)
    segment = jax.vmap(lambda own: jnp.searchsorted(jnp.cumsum(ragged_sizes(own, 4, LENGTH, LENGTH // 2, 0)), jnp.arange(LENGTH), side="right"))(jax.random.split(key_list[4], SEQS)).reshape((SEQS, LENGTH)).astype(jnp.int32)
    image_offset = touch_ends(jax.random.randint(key_list[5], (SEQS, NBLK), 0, BLOCK - PIECE + 1), jax.random.fold_in(key_list[5], 1), 0, BLOCK - PIECE).astype(jnp.int32)
    retain = jnp.clip(jax.random.uniform(key_list[6], (D,), jnp.float32, 0.55, 0.995), 0.55, 0.995)
    to_query = centred(key_list[7], (D, D), D ** -0.5, 0.1875, ((0, 8), (1, 4)))
    to_key = centred(key_list[8], (D, D), D ** -0.5, 0.1875, ((0, 8), (1, 4)))
    to_value = centred(key_list[9], (D, D), D ** -0.5, 0.1875, ((0, 8), (1, 4)))
    to_output = centred(key_list[10], (D, D), (max(D // 512, 1)) ** -0.5, 4.0, ((0, 4), (1, 8)))
    to_hidden = centred(key_list[11], (D, FF), D ** -0.5, 0.1875, ((0, 8),))
    to_model = centred(key_list[12], (FF, D), FF ** -0.5, 0.09375, ((1, 8),))
    state_query = centred(key_list[13], (D, D), D ** -0.5, 0.1875, ((0, 8), (1, 4)))
    state_key = centred(key_list[14], (D, D), D ** -0.5, 0.1875, ((0, 8), (1, 4)))
    state_value = centred(key_list[15], (D, D), D ** -0.5, 0.1875, ((0, 8), (1, 4)))
    state_write = centred(key_list[16], (D, D), (max(D // 512, 1)) ** -0.5, 4.0, ((1, 8),))
    first_gain = jnp.clip(1.0 + 0.1 * jax.random.normal(key_list[17], (D,), jnp.float32), 0.5, 1.5)
    second_gain = jnp.clip(1.0 + 0.1 * jax.random.normal(key_list[18], (D,), jnp.float32), 0.5, 1.5)
    state_gain = jnp.clip(1.0 + 0.1 * jax.random.normal(key_list[19], (D,), jnp.float32), 0.5, 1.5)
    return {"block_input": block_input, "state_start": state_start, "teacher": teacher, "valid_mask": valid_mask, "segment": segment, "image_offset": image_offset, "retain": retain, "to_query": to_query, "to_key": to_key, "to_value": to_value, "to_output": to_output, "to_hidden": to_hidden, "to_model": to_model, "state_query": state_query, "state_key": state_key, "state_value": state_value, "state_write": state_write, "first_gain": first_gain, "second_gain": second_gain, "state_gain": state_gain}


epsilon = 1e-06
highest = lax.Precision.HIGHEST
masked_value = -1e+30

@jax.custom_vjp
def low(v):
    return lax.optimization_barrier(v.astype(jnp.bfloat16)).astype(jnp.float32)

@jax.custom_vjp
def low_back(v):
    return v

def low_keep(v):
    return (low(v), None)

def low_pass(kept, grad):
    return (grad,)

def back_keep(v):
    return (v, None)

def back_low(kept, grad):
    return (low(grad),)
low.defvjp(low_keep, low_pass)
low_back.defvjp(back_keep, back_low)

def narrow_both(values):
    return low(low_back(values))

def product(former, latter):
    return jnp.dot(former, latter, precision=highest, preferred_element_type=jnp.float32)

def norm_rows(values, scaling):
    return values * lax.rsqrt(lax.optimization_barrier(jnp.mean(values * values, axis=-1, keepdims=True)) + epsilon) * scaling

def piece_number(offsets, length):
    numbers = jnp.arange(offsets.shape[0], dtype=jnp.int32)
    places = jnp.arange(length, dtype=jnp.int32)[:, None]
    starts = (numbers * BLOCK + offsets.astype(jnp.int32))[None, :]
    inside = (places >= starts) & (places < starts + PIECE)
    return (lax.optimization_barrier(jnp.sum(jnp.where(inside, numbers[None, :] + 1, 0), axis=1)) - 1).astype(jnp.int32)

def token_mask(number, valid_pad, segment_pad, piece_pad):
    first_row = (number * BLOCK).astype(jnp.int32)
    row_places = first_row + jnp.arange(BLOCK, dtype=jnp.int32)
    col_places = first_row - BLOCK + jnp.arange(2 * BLOCK, dtype=jnp.int32)
    row_segment = lax.dynamic_slice_in_dim(segment_pad, first_row + BLOCK, BLOCK)
    row_piece = lax.dynamic_slice_in_dim(piece_pad, first_row + BLOCK, BLOCK)
    col_segment = lax.dynamic_slice_in_dim(segment_pad, first_row, 2 * BLOCK)
    col_piece = lax.dynamic_slice_in_dim(piece_pad, first_row, 2 * BLOCK)
    col_valid = lax.dynamic_slice_in_dim(valid_pad, first_row, 2 * BLOCK)
    nearby = row_places[:, None] - col_places[None, :] < BLOCK
    earlier = col_places[None, :] <= row_places[:, None]
    same_piece = (row_piece[:, None] == col_piece[None, :]) & (row_piece[:, None] >= 0)
    allowed = (col_valid[None, :] > 0) & (row_segment[:, None] == col_segment[None, :]) & nearby & (earlier | same_piece)
    return jnp.concatenate([allowed, jnp.full((BLOCK, NS), True)], axis=1)

def state_mask(number, valid_row):
    col_valid = lax.dynamic_slice_in_dim(valid_row, (number * BLOCK).astype(jnp.int32), BLOCK) > 0
    joined = jnp.concatenate([col_valid, jnp.full((NS,), True)])
    return jnp.broadcast_to(joined[None, :], (NS, BLOCK + NS))

def attention(query_rows, key_rows, value_rows, allowed):
    logits = jnp.einsum('rhe,khe->hrk', query_rows, key_rows, precision=highest) * HEAD ** (-0.5)
    logits = jnp.where(allowed[None], low_back(logits), masked_value)
    chances = jax.nn.softmax(logits, axis=-1)
    mixture = jnp.einsum('hrk,khe->rhe', low(chances), value_rows, precision=highest)
    return narrow_both(mixture.reshape(mixture.shape[0], -1))

def sequence_loss(params, tokens, initial, target, valid_row, segment_row, offsets, retain):
    to_query, to_key, to_value, to_output, to_hidden, to_model, state_query, state_key, state_value, state_write, first_gain, second_gain, state_gain = params
    length = tokens.shape[0]
    nblocks = length // BLOCK
    blocks = jnp.arange(nblocks, dtype=jnp.int32)
    pieces = piece_number(offsets, length)
    valid_pad = jnp.pad(valid_row, (BLOCK, 0))
    segment_pad = jnp.pad(segment_row, (BLOCK, 0), constant_values=-1)
    piece_pad = jnp.pad(pieces, (BLOCK, 0), constant_values=-1)
    first_low = low(norm_rows(tokens, first_gain))
    query_all = narrow_both(product(first_low, to_query)).reshape(length, HEADS, HEAD)
    key_all = narrow_both(product(first_low, to_key)).reshape(length, HEADS, HEAD)
    value_all = narrow_both(product(first_low, to_value)).reshape(length, HEADS, HEAD)

    def chain_step(current, number):
        state_normed = low(norm_rows(current, state_gain))
        state_queries = narrow_both(product(state_normed, state_query)).reshape(NS, HEADS, HEAD)
        state_keys = narrow_both(product(state_normed, state_key)).reshape(NS, HEADS, HEAD)
        state_values = narrow_both(product(state_normed, state_value)).reshape(NS, HEADS, HEAD)
        first_row = (number * BLOCK).astype(jnp.int32)
        block_keys = lax.dynamic_slice_in_dim(key_all, first_row, BLOCK)
        block_values = lax.dynamic_slice_in_dim(value_all, first_row, BLOCK)
        mixture = attention(state_queries, jnp.concatenate([block_keys, state_keys]), jnp.concatenate([block_values, state_values]), state_mask(number, valid_row))
        update = low_back(product(mixture, state_write))
        return (retain * current + (1.0 - retain) * update, (state_keys, state_values))
    final_state, (key_stack, value_stack) = lax.scan(jax.checkpoint(chain_step), initial, blocks)
    key_pad = jnp.pad(key_all, ((BLOCK, 0), (0, 0), (0, 0)))
    value_pad = jnp.pad(value_all, ((BLOCK, 0), (0, 0), (0, 0)))

    def token_block(element):
        number, state_keys, state_values = element
        first_row = (number * BLOCK).astype(jnp.int32)
        query_rows = lax.dynamic_slice_in_dim(query_all, first_row, BLOCK)
        key_rows = jnp.concatenate([lax.dynamic_slice_in_dim(key_pad, first_row, 2 * BLOCK), state_keys])
        value_rows = jnp.concatenate([lax.dynamic_slice_in_dim(value_pad, first_row, 2 * BLOCK), state_values])
        return attention(query_rows, key_rows, value_rows, token_mask(number, valid_pad, segment_pad, piece_pad))
    mixture_all = lax.map(jax.checkpoint(token_block), (blocks, key_stack, value_stack)).reshape(length, HEADS * HEAD)
    after_attend = tokens + low_back(product(mixture_all, to_output))
    second_low = low(norm_rows(after_attend, second_gain))
    pre_gelu = low_back(product(second_low, to_hidden))
    hidden_low = low(jax.nn.gelu(pre_gelu))
    block_out = after_attend + low_back(product(hidden_low, to_model))
    errors = block_out - target
    return (jnp.sum(valid_row.astype(jnp.float32)[:, None] * errors * errors), final_state)

def reference(block_input, state_start, teacher, valid_mask, segment, image_offset, retain, to_query, to_key, to_value, to_output, to_hidden, to_model, state_query, state_key, state_value, state_write, first_gain, second_gain, state_gain):
    weights = tuple((array.astype(jnp.float32) for array in (to_query, to_key, to_value, to_output, to_hidden, to_model, state_query, state_key, state_value, state_write, first_gain, second_gain, state_gain)))
    tokens = block_input.astype(jnp.float32)
    initial = state_start.astype(jnp.float32)
    targets = teacher.astype(jnp.float32)
    valid_count = jnp.sum(valid_mask.astype(jnp.float32))

    def everything(params, inputs, starts):

        def sequence_step(running, sequence):
            seq_tokens, seq_state, seq_target, seq_valid, seq_segment, seq_offsets = sequence
            partial_sum, seq_final = sequence_loss(params, seq_tokens, seq_state, seq_target, seq_valid, seq_segment, seq_offsets, retain)
            return (running + partial_sum, seq_final)
        return lax.scan(jax.checkpoint(sequence_step), jnp.zeros((), jnp.float32), (inputs, starts, targets, valid_mask, segment, image_offset))
    (squared_sum, final_states), pull_back = jax.vjp(everything, weights, tokens, initial)
    scale_factor = SEQS * LENGTH / (2.0 * valid_count)
    weight_grads, input_grad, state_grad = pull_back((scale_factor, jnp.zeros_like(final_states)))
    return (squared_sum / (2.0 * valid_count), final_states, input_grad, state_grad, weight_grads[0], weight_grads[1], weight_grads[2], weight_grads[3], weight_grads[4], weight_grads[5], weight_grads[6], weight_grads[7], weight_grads[8], weight_grads[9], weight_grads[10], weight_grads[11], weight_grads[12])
```

```python
import functools

import jax
import jax.numpy as jnp
from jax import lax
from jax.experimental import pallas as pl
from jax.experimental.pallas import tpu as pltpu
from jax.sharding import PartitionSpec as P

HEAD = 128
BLOCK = 512
HALF = 256
NS = 512
PIECE = 256

epsilon = 1e-06
masked_value = -1e30
score_scale = HEAD ** (-0.5)
log2_scale = score_scale * 1.4426950408889634
f32 = jnp.float32
bf16 = jnp.bfloat16


def dot_nn(a, b):
    return lax.dot_general(a, b, (((1,), (0,)), ((), ())), preferred_element_type=f32)


def dot_nt(a, b):
    return lax.dot_general(a, b, (((1,), (1,)), ((), ())), preferred_element_type=f32)


def dot_tn(a, b):
    return lax.dot_general(a, b, (((0,), (0,)), ((), ())), preferred_element_type=f32)


def half_of(i, s):
    return lax.rem(i + 1 + s[1], 2)


def launch(body, grid, idx, inputs, outputs, scratch=(), flops=0, vmem=40, name=None):
    arrays = [a for a, unused in inputs]
    nbytes = sum(a.size * a.dtype.itemsize for a in arrays)
    nbytes += sum(o.size * o.dtype.itemsize for o, unused in outputs)
    return pl.pallas_call(
        body,
        grid_spec=pltpu.PrefetchScalarGridSpec(
            num_scalar_prefetch=1,
            grid=grid,
            in_specs=[spec for unused, spec in inputs],
            out_specs=[spec for unused, spec in outputs],
            scratch_shapes=list(scratch),
        ),
        out_shape=[o for o, unused in outputs],
        compiler_params=pltpu.CompilerParams(
            dimension_semantics=("arbitrary",) * len(grid), vmem_limit_bytes=vmem << 20
        ),
        cost_estimate=pl.CostEstimate(flops=flops, bytes_accessed=nbytes, transcendentals=0),
        name=name,
    )(idx, *arrays)


def shaped(shape, dtype):
    return jax.ShapeDtypeStruct(shape, dtype)


def whole(shape, place=(0, 0)):
    return pl.BlockSpec(shape, lambda i, s: place, pipeline_mode=pl.Buffered(1))


def norm_project(idx, values, gain, weights, column, width, name):
    rows, features = values.shape

    def body(s, x_ref, g_ref, w_ref, n_ref, p_ref):
        x = x_ref[...].astype(f32)
        inverse = lax.rsqrt(jnp.mean(x * x, axis=-1, keepdims=True) + epsilon)
        normed = (x * inverse * g_ref[...]).astype(bf16)
        n_ref[...] = normed
        p_ref[...] = dot_nn(normed, w_ref[...]).astype(bf16)

    return launch(
        body,
        (rows // HALF,),
        idx,
        [
            (values, pl.BlockSpec((HALF, features), lambda i, s: (i, 0))),
            (gain, whole((1, features))),
            (weights, whole((features, width), (0, column))),
        ],
        [
            (shaped((rows, features), bf16), pl.BlockSpec((HALF, features), lambda i, s: (i, 0))),
            (shaped((rows, width), bf16), pl.BlockSpec((HALF, width), lambda i, s: (i, 0))),
        ],
        flops=2 * rows * features * width,
        name=name,
    )


def masked_scores(kind, keys, queries, katt, qatt):
    scores = dot_nt(keys, queries)
    if kind == "free":
        return scores
    if kind == "valid":
        return jnp.where(katt[:, 2:3] > 0, scores, masked_value)
    places = lax.broadcasted_iota(jnp.int32, scores.shape, 0)
    asking = lax.broadcasted_iota(jnp.int32, scores.shape, 1)
    same = katt[:, 0:1] == qatt[0:1, :]
    if kind == "prev":
        allowed = same & (places > asking)
    else:
        allowed = same & ((places <= asking) | (katt[:, 1:2] == qatt[1:2, :]))
    return jnp.where(allowed, scores, masked_value)


def attention_inputs(queries, segments, katt, qatt):
    q_arr, q_row, q_col = queries
    inputs = [(q_arr, pl.BlockSpec((BLOCK, HEAD), lambda h, s: (q_row, q_col + h)))]
    for kind, k_arr, row, k_col, v_col, att in segments:
        inputs.append(
            (k_arr, pl.BlockSpec((BLOCK, HEAD), lambda h, s, row=row, k_col=k_col: (row, k_col + h)))
        )
        inputs.append(
            (k_arr, pl.BlockSpec((BLOCK, HEAD), lambda h, s, row=row, v_col=v_col: (row, v_col + h)))
        )
        if att is not None:
            inputs.append((katt, pl.BlockSpec((BLOCK, 4), lambda h, s, att=att: (att, 0))))
    if qatt is not None:
        inputs.append((qatt, pl.BlockSpec((4, BLOCK), lambda h, s: (0, q_row))))
    return inputs


def take_attention(refs, segments, has_qatt):
    refs = list(refs)
    q = refs.pop(0)[...]
    parts = []
    for kind, unused_a, unused_b, unused_c, unused_d, att in segments:
        k = refs.pop(0)[...]
        v = refs.pop(0)[...]
        katt = refs.pop(0)[...] if att is not None else None
        parts.append((kind, k, v, katt))
    qatt = refs.pop(0)[...] if has_qatt else None
    return q, parts, qatt, refs


def attend(idx, queries, segments, katt, qatt, heads, name):
    inputs = attention_inputs(queries, segments, katt, qatt)

    def body(s, *refs):
        q, parts, qa, rest = take_attention(refs, segments, qatt is not None)
        o_ref, l_ref = rest
        scores = [masked_scores(kind, k, q, ka, qa) for kind, k, v, ka in parts]
        largest = functools.reduce(
            jnp.maximum, [jnp.max(x, axis=0, keepdims=True) for x in scores]
        )
        total = jnp.zeros_like(largest)
        mixed = jnp.zeros((HEAD, BLOCK), f32)
        for x, (kind, k, v, ka) in zip(scores, parts):
            raised = jnp.exp2((x - largest) * log2_scale)
            total = total + jnp.sum(raised, axis=0, keepdims=True)
            mixed = mixed + dot_tn(v, raised.astype(bf16))
        o_ref[...] = jnp.transpose(mixed * (1.0 / total)).astype(bf16)
        l_ref[0] = largest * log2_scale + jnp.log2(total)

    keys = BLOCK * len(segments)
    return launch(
        body,
        (heads,),
        idx,
        inputs,
        [
            (shaped((BLOCK, heads * HEAD), bf16), pl.BlockSpec((BLOCK, HEAD), lambda h, s: (0, h))),
            (shaped((heads, 1, BLOCK), f32), pl.BlockSpec((1, 1, BLOCK), lambda h, s: (h, 0, 0))),
        ],
        flops=4 * heads * BLOCK * keys * HEAD * 2,
        name=name,
    )


def attend_back(idx, queries, segments, katt, qatt, heads, logs, upstream, added, dtypes, name):
    inputs = attention_inputs(queries, segments, katt, qatt)
    inputs.append((logs, pl.BlockSpec((1, 1, BLOCK), lambda h, s: (h, 0, 0))))
    by_head = pl.BlockSpec((BLOCK, HEAD), lambda h, s: (0, h))
    inputs.append((upstream, by_head))
    for pair in added:
        if pair is not None:
            inputs.extend([(pair[0], by_head), (pair[1], by_head)])
    outputs = [(shaped((BLOCK, heads * HEAD), bf16), by_head)]
    for dtype in dtypes:
        outputs.extend([(shaped((BLOCK, heads * HEAD), dtype), by_head)] * 2)

    def body(s, *refs):
        q, parts, qa, rest = take_attention(refs, segments, qatt is not None)
        log_total = rest.pop(0)[0]
        go = rest.pop(0)[...]
        sums = []
        for pair in added:
            sums.append((rest.pop(0), rest.pop(0)) if pair is not None else None)
        gq_ref = rest.pop(0)
        chances, grads = [], []
        inner = jnp.zeros((1, BLOCK), f32)
        for kind, k, v, ka in parts:
            x = masked_scores(kind, k, q, ka, qa)
            chance = jnp.exp2(x * log2_scale - log_total)
            grad = dot_nt(v, go)
            inner = inner + jnp.sum(chance * grad, axis=0, keepdims=True)
            chances.append(chance)
            grads.append(grad)
        gq = jnp.zeros((HEAD, BLOCK), f32)
        for (kind, k, v, ka), chance, grad, pair, dtype in zip(parts, chances, grads, sums, dtypes):
            gl = (chance * (grad - inner)).astype(bf16)
            gk = dot_nn(gl, q) * score_scale
            gv = dot_nn(chance.astype(bf16), go)
            gq = gq + dot_tn(k, gl)
            if pair is not None:
                gk = gk + pair[0][...]
                gv = gv + pair[1][...]
            gk_ref, gv_ref = rest.pop(0), rest.pop(0)
            gk_ref[...] = gk.astype(dtype)
            gv_ref[...] = gv.astype(dtype)
        gq_ref[...] = jnp.transpose(gq * score_scale).astype(bf16)

    keys = BLOCK * len(segments)
    return launch(
        body,
        (heads,),
        idx,
        inputs,
        outputs,
        flops=10 * heads * BLOCK * keys * HEAD * 2,
        name=name,
    )


def state_update(idx, pieces, write_t, column, state, retain, gain, weights, w_col, width, name):
    rows, features = state.shape
    count, piece_width = len(pieces), pieces[0].shape[1]
    project = weights is not None

    def body(s, *refs):
        refs = list(refs)
        piece_refs = [refs.pop(0) for unused in range(count)]
        w_ref, s_ref, r_ref = refs[:3]
        refs = refs[3:]
        scr = refs.pop()
        for k, ref in enumerate(piece_refs):
            scr[s[0] ^ k] = ref[...]
        update = jnp.zeros((HALF, features), f32)
        for k in range(count):
            update = update + dot_nt(scr[k], w_ref[:, k * piece_width : (k + 1) * piece_width])
        keep = r_ref[...]
        following = keep * s_ref[...].astype(f32) + (1.0 - keep) * update
        if project:
            g_ref, p_ref, out_ref, n_ref, t_ref = refs
            inverse = lax.rsqrt(jnp.mean(following * following, axis=-1, keepdims=True) + epsilon)
            normed = (following * inverse * g_ref[...]).astype(bf16)
            n_ref[...] = normed
            t_ref[...] = dot_nn(normed, p_ref[...]).astype(bf16)
        else:
            (out_ref,) = refs
        out_ref[...] = following

    tile = lambda w: pl.BlockSpec((HALF, w), lambda i, s: (i, 0))
    inputs = [(p, tile(piece_width)) for p in pieces]
    inputs += [
        (write_t, whole((features, features), (0, column))),
        (state, tile(features)),
        (retain, whole((1, features))),
    ]
    outputs = [(shaped((rows, features), f32), tile(features))]
    if project:
        inputs += [(gain, whole((1, features))), (weights, whole((features, width), (0, w_col)))]
        outputs += [
            (shaped((rows, features), bf16), tile(features)),
            (shaped((rows, width), bf16), tile(width)),
        ]
    return launch(
        body,
        (rows // HALF,),
        idx,
        inputs,
        outputs,
        scratch=[pltpu.VMEM((count, HALF, piece_width), bf16)],
        flops=2 * rows * features * (features + (width if project else 0)),
        name=name,
    )


def take_sum(i, refs, total):
    mine, mine_other, theirs, theirs_other = refs

    @pl.when(i == 0)
    def _():
        total[...] = theirs[...].astype(f32) + theirs_other[...].astype(f32)

    @pl.when(i == 1)
    def _():
        total[...] = mine[...].astype(f32) + mine_other[...].astype(f32)

    return total[...]


def sum_inputs(sums):
    return [(a, whole(a.shape)) for a in sums]


def halves(features, row_block=0):
    return pl.BlockSpec((HALF, features), lambda i, s: (2 * row_block + half_of(i, s), 0))


def fixed(shape):
    return pl.BlockSpec(shape, lambda i, s: (0, 0))


def add_rows(i, ref, value):
    value = jnp.sum(value, axis=0, keepdims=True)

    @pl.when(i == 0)
    def _():
        ref[...] = value

    @pl.when(i != 0)
    def _():
        ref[...] = ref[...] + value


def put_half(i, theirs_ref, mine_ref, value):
    @pl.when(i == 0)
    def _():
        theirs_ref[...] = value

    @pl.when(i == 1)
    def _():
        mine_ref[...] = value


def project_back(idx, grads, weights, column, name):
    rows, width = grads[0].shape
    features = weights.shape[0]

    def body(s, *refs):
        i = pl.program_id(0)
        *g_refs, w_ref, theirs_ref, mine_ref = refs
        out = jnp.zeros((HALF, features), f32)
        for k, ref in enumerate(g_refs):
            out = out + dot_nt(ref[...], w_ref[:, k * width : (k + 1) * width])
        put_half(i, theirs_ref, mine_ref, out.astype(bf16))

    return launch(
        body,
        (2,),
        idx,
        [(g, halves(width)) for g in grads]
        + [(weights, whole((features, len(grads) * width), (0, column)))],
        [(shaped((HALF, features), bf16), fixed((HALF, features)))] * 2,
        flops=2 * rows * features * width * len(grads),
        name=name,
    )


def state_back(idx, sums, state, following, retain, gain, write_t, w_col, width, name):
    rows, features = state.shape
    before = write_t is not None

    def body(s, *refs):
        i = pl.program_id(0)
        refs = list(refs)
        total = refs.pop()
        up = take_sum(i, [refs.pop(0) for unused in range(4)], total)
        s_ref, r_ref, g_ref = refs[:3]
        refs = refs[3:]
        x = s_ref[...].astype(f32)
        inverse = lax.rsqrt(jnp.mean(x * x, axis=-1, keepdims=True) + epsilon)
        unit = x * inverse
        scaled = up * g_ref[...]
        inner = jnp.mean(scaled * unit, axis=-1, keepdims=True)
        out = inverse * (scaled - unit * inner)
        if following is not None:
            out = r_ref[...] * refs.pop(0)[...] + out
        if before:
            w_ref, gs_ref, gain_ref, gu_ref, gos_ref = refs
            gu = ((1.0 - r_ref[...]) * out).astype(bf16)
            gu_ref[...] = gu
            gos_ref[...] = dot_nn(gu, w_ref[...]).astype(bf16)
        else:
            gs_ref, gain_ref = refs
        gs_ref[...] = out
        add_rows(i, gain_ref, up * unit)

    inputs = sum_inputs(sums) + [
        (state, halves(features)),
        (retain, whole((1, features))),
        (gain, whole((1, features))),
    ]
    outputs = [
        (shaped((rows, features), f32), halves(features)),
        (shaped((1, features), f32), fixed((1, features))),
    ]
    if following is not None:
        inputs.append((following, halves(features)))
    if before:
        inputs.append(
            (
                write_t,
                pl.BlockSpec(
                    (features, width),
                    lambda i, s: (0, w_col + s[2]),
                    pipeline_mode=pl.Buffered(1),
                ),
            )
        )
        outputs += [
            (shaped((rows, features), bf16), halves(features)),
            (shaped((rows, width), bf16), halves(width)),
        ]
    return launch(
        body,
        (2,),
        idx,
        inputs,
        outputs,
        scratch=[pltpu.VMEM((HALF, features), f32)],
        flops=2 * rows * features * width if before else rows * features * 10,
        name=name,
    )


def gelu_both(a):
    root, cubic = 0.7978845608028654, 0.044715
    squared = a * a
    bent = jnp.tanh(root * (a + cubic * (squared * a)))
    rising = 0.5 * (1.0 + bent)
    slope = rising + (0.5 * root) * a * (1.0 - bent * bent) * (1.0 + (3.0 * cubic) * squared)
    return a * rising, slope


def dense_forward(idx, number, pieces, out_pieces, tokens, gain, dense, name):
    features = tokens.shape[1]
    hidden = features_of_hidden = dense[2]
    weights, modelt_col = dense[0], dense[1]
    count, width = len(pieces), pieces[0].shape[1]

    def body(s, *refs):
        i = pl.program_id(0)
        refs = list(refs)
        o_refs = [refs.pop(0) for unused in range(count)]
        w_refs = [refs.pop(0) for unused in range(count)]
        t_ref, g_ref, up_ref, down_ref = refs[:4]
        x1_ref, xn_ref, h_ref, d_ref, theirs_ref, mine_ref = refs[4:]
        x1 = t_ref[...].astype(f32)
        for o_ref, w_ref in zip(o_refs, w_refs):
            x1 = x1 + dot_nt(o_ref[...], w_ref[...])
        x1_ref[...] = x1
        inverse = lax.rsqrt(jnp.mean(x1 * x1, axis=-1, keepdims=True) + epsilon)
        normed = (x1 * inverse * g_ref[...]).astype(bf16)
        xn_ref[...] = normed
        h, slope = gelu_both(dot_nn(normed, up_ref[...]))
        h = h.astype(bf16)
        h_ref[...] = h
        d_ref[...] = slope.astype(bf16)
        put_half(i, theirs_ref, mine_ref, dot_nt(h, down_ref[...]).astype(bf16))

    return launch(
        body,
        (2,),
        idx,
        [(p, halves(width)) for p in pieces]
        + [(w, whole((features, width))) for w in out_pieces]
        + [
            (tokens, halves(features, number)),
            (gain, whole((1, features))),
            (weights, whole((features, hidden), (0, 0))),
            (weights, whole((features, hidden), (0, modelt_col))),
        ],
        [
            (shaped((BLOCK, features), f32), halves(features)),
            (shaped((BLOCK, features), bf16), halves(features)),
            (shaped((BLOCK, hidden), bf16), halves(hidden)),
            (shaped((BLOCK, hidden), bf16), halves(hidden)),
            (shaped((HALF, features), bf16), fixed((HALF, features))),
            (shaped((HALF, features), bf16), fixed((HALF, features))),
        ],
        flops=2 * BLOCK * features * (features + 2 * hidden),
        name=name,
    )


def dense_backward(idx, number, sums, x1, teacher, weight_of_row, slope, dense, name):
    features = x1.shape[1]
    weights, modelt_col, hidden = dense

    def body(s, *refs):
        i = pl.program_id(0)
        refs = list(refs)
        total = refs.pop()
        dense_sum = take_sum(i, [refs.pop(0) for unused in range(4)], total)
        x_ref, t_ref, v_ref, d_ref, up_ref, down_ref = refs[:6]
        gy_ref, gm_ref, ga_ref, loss_ref, theirs_ref, mine_ref = refs[6:]
        errors = x_ref[...] + dense_sum - t_ref[...].astype(f32)
        gy = v_ref[...] * errors
        gy_ref[...] = gy
        add_rows(i, loss_ref, gy * errors)
        gm = gy.astype(bf16)
        gm_ref[...] = gm
        ga = (dot_nn(gm, down_ref[...]) * d_ref[...].astype(f32)).astype(bf16)
        ga_ref[...] = ga
        put_half(i, theirs_ref, mine_ref, dot_nt(ga, up_ref[...]).astype(bf16))

    return launch(
        body,
        (2,),
        idx,
        sum_inputs(sums)
        + [
            (x1, halves(features)),
            (teacher, halves(features, number)),
            (weight_of_row, halves(1, number)),
            (slope, halves(hidden)),
            (weights, whole((features, hidden), (0, 0))),
            (weights, whole((features, hidden), (0, modelt_col))),
        ],
        [
            (shaped((BLOCK, features), f32), halves(features)),
            (shaped((BLOCK, features), bf16), halves(features)),
            (shaped((BLOCK, hidden), bf16), halves(hidden)),
            (shaped((1, features), f32), fixed((1, features))),
            (shaped((HALF, features), bf16), fixed((HALF, features))),
            (shaped((HALF, features), bf16), fixed((HALF, features))),
        ],
        scratch=[pltpu.VMEM((HALF, features), f32)],
        flops=4 * BLOCK * features * hidden,
        name=name,
    )


def output_backward(idx, sums, gy, x1, gain, out_own, name):
    features = x1.shape[1]
    width = out_own.shape[1]

    def body(s, *refs):
        i = pl.program_id(0)
        refs = list(refs)
        total = refs.pop()
        up = take_sum(i, [refs.pop(0) for unused in range(4)], total)
        gy_ref, x_ref, g_ref, w_ref, gx_ref, gp_ref, go_ref, gain_ref = refs
        x = x_ref[...]
        inverse = lax.rsqrt(jnp.mean(x * x, axis=-1, keepdims=True) + epsilon)
        unit = x * inverse
        scaled = up * g_ref[...]
        inner = jnp.mean(scaled * unit, axis=-1, keepdims=True)
        gx = gy_ref[...] + inverse * (scaled - unit * inner)
        gx_ref[...] = gx
        gp = gx.astype(bf16)
        gp_ref[...] = gp
        go_ref[...] = dot_nn(gp, w_ref[...]).astype(bf16)
        add_rows(i, gain_ref, up * unit)

    return launch(
        body,
        (2,),
        idx,
        sum_inputs(sums)
        + [
            (gy, halves(features)),
            (x1, halves(features)),
            (gain, whole((1, features))),
            (out_own, whole((features, width))),
        ],
        [
            (shaped((BLOCK, features), f32), halves(features)),
            (shaped((BLOCK, features), bf16), halves(features)),
            (shaped((BLOCK, width), bf16), halves(width)),
            (shaped((1, features), f32), fixed((1, features))),
        ],
        scratch=[pltpu.VMEM((HALF, features), f32)],
        flops=2 * BLOCK * features * width,
        name=name,
    )


def weight_grads(idx, groups, name):
    features = groups[0][0][0].shape[1]
    inputs, total = [], 0
    flops = 0
    for parts in groups:
        for left, right in parts:
            inputs.append((left, pl.BlockSpec((left.shape[0], HALF), lambda i, s: (0, i))))
            inputs.append((right, whole(right.shape)))
            flops += 2 * left.size * right.shape[1]
        total += parts[0][1].shape[1]

    def body(s, *refs):
        refs = list(refs)
        out_ref = refs.pop()
        at = 0
        for parts in groups:
            size = parts[0][1].shape[1]
            out = jnp.zeros((HALF, size), f32)
            for unused in parts:
                left, right = refs.pop(0), refs.pop(0)
                out = out + dot_tn(left[...], right[...])
            out_ref[:, at : at + size] = out.astype(bf16)
            at += size

    return launch(
        body,
        (features // HALF,),
        idx,
        inputs,
        [(shaped((features, total), bf16), pl.BlockSpec((HALF, total), lambda i, s: (i, 0)))],
        flops=flops,
        name=name,
    )[0]


def per_device(
    block_input,
    state_start,
    teacher,
    valid_mask,
    segment,
    image_offset,
    retain,
    to_query,
    to_key,
    to_value,
    to_output,
    to_hidden,
    to_model,
    state_query,
    state_key,
    state_value,
    state_write,
    first_gain,
    second_gain,
    state_gain,
):
    row_devices = lax.axis_size("row")
    col_devices = lax.axis_size("col")
    row_index = lax.axis_index("row")
    col_index = lax.axis_index("col")
    local_rows, features = block_input.shape[1:]
    length = local_rows * row_devices
    width = to_query.shape[1]
    heads = width // HEAD
    hidden = to_hidden.shape[1] // row_devices
    nblocks = length // BLOCK
    pairs = row_devices == 4 and 2 * local_rows == BLOCK
    core_pairs = [(k, k ^ 1) for k in range(row_devices)]
    chip_pairs = [(k, k ^ 2) for k in range(row_devices)] if pairs else None
    if pairs:
        idx = jnp.stack([row_index, row_index % 2, row_index]).astype(jnp.int32)
    else:
        idx = jnp.stack([0, 1, row_index]).astype(jnp.int32)

    def to_core(x):
        return lax.ppermute(x, "row", core_pairs)

    def to_chip(x):
        return lax.ppermute(x, "row", chip_pairs)

    def row_pieces(x):
        if not pairs:
            stacked = lax.all_gather(x, "row", axis=0, tiled=False)
            return [stacked[k] for k in range(row_devices)]
        near = to_core(x)
        far = to_chip(x)
        return [x, near, far, to_core(far)]

    def row_order(x):
        if not pairs:
            return lax.all_gather(x, "row", axis=0, tiled=True)
        out = jnp.zeros((row_devices,) + x.shape, x.dtype)
        for k, piece in enumerate(row_pieces(x)):
            out = lax.dynamic_update_index_in_dim(out, piece, row_index ^ k, 0)
        return out.reshape((-1,) + x.shape[1:])

    def chip_sum(theirs, mine):
        return (mine.astype(f32) + to_core(theirs).astype(f32)).astype(bf16)

    def row_sum(theirs, mine):
        if not pairs:
            both = lax.psum(jnp.concatenate([theirs, mine]), "row")
            none = jnp.zeros_like(mine)
            return [both[HALF:], none, both[:HALF], none]
        own = chip_sum(theirs, mine)
        far = to_chip(own)
        return [own, far, to_core(own), to_core(far)]

    def all_sum(x):
        for axis, size in (("row", row_devices), ("col", col_devices)):
            step = 1
            while step < size:
                x = x + lax.ppermute(x, axis, [(k, k ^ step) for k in range(size)])
                step *= 2
        return x

    near_weights = jnp.concatenate(
        [state_query, state_key, state_value, to_query, to_key, to_value], axis=1
    )
    near = lax.all_gather(near_weights, "col", axis=0, tiled=True)
    upper = lax.dynamic_slice_in_dim(to_hidden, row_index * hidden, hidden, 1)
    lower = lax.dynamic_slice_in_dim(to_model, row_index * hidden, hidden, 0)
    mid = lax.all_gather(
        jnp.concatenate([state_write.T, to_output.T], axis=1), "col", axis=0, tiled=True
    )
    far = lax.all_gather(jnp.concatenate([upper, lower.T], axis=1), "col", axis=0, tiled=True)
    dense = (far, 1, hidden)
    out_own = lax.slice_in_dim(mid, features, features + width, axis=1)
    out_pieces = row_pieces(out_own)

    valid_row = lax.dynamic_index_in_dim(valid_mask, col_index, 0, keepdims=False)
    segment_row = segment[0]
    numbers = jnp.arange(nblocks, dtype=jnp.int32)
    places = jnp.arange(length, dtype=jnp.int32)
    starts = numbers * BLOCK + image_offset[0]
    inside = (places[:, None] >= starts[None, :]) & (places[:, None] < starts[None, :] + PIECE)
    piece = jnp.sum(jnp.where(inside, numbers[None, :] + 1, 0), axis=1) - 1
    nothing = jnp.zeros_like(piece)
    katt = jnp.stack(
        [jnp.where(valid_row > 0, segment_row, -1), piece, valid_row, nothing], axis=1
    )
    qatt = jnp.stack([segment_row, jnp.where(piece >= 0, piece, -2), nothing, nothing], axis=0)
    valid_count = jnp.sum(valid_mask.astype(f32))
    total_tokens = f32(length * col_devices)
    weight_of_row = (total_tokens / valid_count * valid_row.astype(f32))[:, None]
    retain2 = retain[None]
    first_gain2, second_gain2, state_gain2 = first_gain[None], second_gain[None], state_gain[None]

    tokens = row_order(block_input[0])
    teacher_all = row_order(teacher[0])
    first_low, token_heads = norm_project(idx, tokens, first_gain2, near, 1, 3 * width, "token_proj")

    def token_segments(number, trio):
        found = []
        if number > 0:
            found.append(("prev", token_heads, number - 1, heads, 2 * heads, number - 1))
        found.append(("own", token_heads, number, heads, 2 * heads, number))
        found.append(("free", trio, 0, heads, 2 * heads, None))
        return found

    def state_segments(number, trio):
        return [
            ("valid", token_heads, number, heads, 2 * heads, number),
            ("free", trio, 0, heads, 2 * heads, None),
        ]

    current = state_start[0]
    state_low, trio = norm_project(idx, current, state_gain2, near, 0, 3 * width, "state_proj")
    states, lows, trios = [], [], []
    state_out, state_logs, token_out, token_logs = [], [], [], []
    x1s, second_lows, hiddens, slopes, dense_sums = [], [], [], [], []
    for b in range(nblocks):
        states.append(current)
        lows.append(state_low)
        trios.append(trio)
        mixed, logs = attend(
            idx, (trio, 0, 0), state_segments(b, trio), katt, None, heads, f"state_attend{b}"
        )
        state_out.append(mixed)
        state_logs.append(logs)
        pieces = row_pieces(mixed)
        mixed, logs = attend(
            idx, (token_heads, b, 0), token_segments(b, trio), katt, qatt, heads, f"token_attend{b}"
        )
        token_out.append(mixed)
        token_logs.append(logs)
        if b + 1 < nblocks:
            current, state_low, trio = state_update(
                idx, pieces, mid, 0, current, retain2, state_gain2, near, 0, 3 * width, f"update{b}"
            )
        else:
            (final_state,) = state_update(
                idx, pieces, mid, 0, current, retain2, None, None, 0, 0, f"update{b}"
            )
        x1, low, h, slope, theirs, mine = dense_forward(
            idx, b, row_pieces(mixed), out_pieces, tokens, second_gain2, dense, f"dense{b}"
        )
        x1s.append(x1)
        second_lows.append(low)
        hiddens.append(h)
        slopes.append(slope)
        dense_sums.append(row_sum(theirs, mine))

    gms, gas, losses, gx1s, gps, gos, second_sums = [], [], [], [], [], [], []
    for b in range(nblocks):
        gy, gm, ga, loss, theirs, mine = dense_backward(
            idx, b, dense_sums[b], x1s[b], teacher_all, weight_of_row, slopes[b], dense, f"back{b}"
        )
        gms.append(gm)
        gas.append(ga)
        losses.append(loss)
        gx1, gp, go, gain_sum = output_backward(
            idx, row_sum(theirs, mine), gy, x1s[b], second_gain2, out_own, f"out_back{b}"
        )
        gx1s.append(gx1)
        gps.append(gp)
        gos.append(go)
        second_sums.append(gain_sum)
    dense_grads = weight_grads(
        idx,
        [list(zip(second_lows, gas)), list(zip(gms, hiddens))],
        "dense_grads",
    )
    dense_grads = lax.psum_scatter(dense_grads, "col", scatter_dimension=0, tiled=True)

    grad_next = None
    key_part = None
    gain_sums = []
    gus = [None] * nblocks
    trio_grads = [None] * nblocks
    token_grads = [None] * nblocks
    first_halves = [None] * nblocks
    gu = ((1.0 - retain2) * jnp.zeros((NS, features), f32)).astype(bf16)
    write_own = lax.dynamic_slice_in_dim(mid, row_index * width, width, 1)
    gos_state = dot_nn(gu, write_own).astype(bf16)
    for b in reversed(range(nblocks)):
        gus[b] = gu
        last = b + 1 == nblocks

        def token_part(own, free, dtype):
            segments = token_segments(b, trios[b])
            added = ([None] if b > 0 else []) + [own, free]
            dtypes = ([f32] if b > 0 else []) + [dtype, dtype]
            return attend_back(
                idx,
                (token_heads, b, 0),
                segments,
                katt,
                qatt,
                heads,
                token_logs[b],
                gos[b],
                added,
                dtypes,
                f"token_back{b}",
            )

        def state_part(own, free, dtype):
            return attend_back(
                idx,
                (trios[b], 0, 0),
                state_segments(b, trios[b]),
                katt,
                None,
                heads,
                state_logs[b],
                gos_state,
                [own, free],
                [dtype, dtype],
                f"state_back{b}",
            )

        if last:
            gqs, gk, gv, gks, gvs = state_part(key_part, None, f32)
            found = token_part((gk, gv), (gks, gvs), bf16)
            gq, (gk, gv, gks, gvs) = found[0], found[-4:]
        else:
            found = token_part(key_part, None, f32)
            gq, (gk, gv, gks, gvs) = found[0], found[-4:]
            gqs, gk, gv, gks, gvs = state_part((gk, gv), (gks, gvs), bf16)
        key_part = (found[1], found[2]) if b > 0 else None
        trio_grads[b] = (gqs, gks, gvs)
        token_grads[b] = (gq, gk, gv)
        theirs, mine = project_back(idx, trio_grads[b], near, 0, f"trio_back{b}")
        sums = row_sum(theirs, mine)
        first_halves[b] = project_back(idx, token_grads[b], near, 1, f"first_back{b}")
        if b > 0:
            grad_next, gain_sum, gu, gos_state = state_back(
                idx,
                sums,
                states[b],
                grad_next,
                retain2,
                state_gain2,
                mid,
                0,
                width,
                f"chain_back{b}",
            )
        else:
            grad_next, gain_sum = state_back(
                idx, sums, states[b], grad_next, retain2, state_gain2, None, 0, width, "chain_back0"
            )
        gain_sums.append(gain_sum)

    late_grads = weight_grads(
        idx,
        [[(lows[b], trio_grads[b][k]) for b in range(nblocks)] for k in range(3)]
        + [
            [
                (lax.slice_in_dim(first_low, b * BLOCK, (b + 1) * BLOCK), token_grads[b][k])
                for b in range(nblocks)
            ]
            for k in range(3)
        ]
        + [list(zip(gps, token_out)), list(zip(gus, state_out))],
        "late_grads",
    )
    late_grads = lax.psum_scatter(late_grads, "col", scatter_dimension=0, tiled=True)

    if pairs:
        own_rows, arrived = [], []
        for b in range(nblocks):
            own = chip_sum(*first_halves[b])
            own_rows.append(own)
            senders = [(k, k ^ 2) for k in range(row_devices) if k // 2 != b]
            arrived.append(lax.ppermute(own, "row", senders))
        mine_first = row_index // 2 == 0
        grad_first = jnp.where(mine_first, own_rows[0], own_rows[1]).astype(f32) + jnp.where(
            mine_first, arrived[0], arrived[1]
        ).astype(f32)
        own_gx1 = jnp.where(mine_first, gx1s[0], gx1s[1])
        own_gx1 = lax.dynamic_slice_in_dim(own_gx1, row_index % 2 * HALF, HALF)
    else:
        both = jnp.concatenate([half for pair in first_halves for half in pair])
        grad_first = lax.psum_scatter(both, "row", scatter_dimension=0, tiled=True).astype(f32)
        own_gx1 = lax.dynamic_slice_in_dim(
            jnp.concatenate(gx1s), row_index * local_rows, local_rows
        )
    own_tokens = block_input[0].astype(f32)
    inverse = lax.rsqrt(jnp.mean(own_tokens * own_tokens, axis=-1, keepdims=True) + epsilon)
    unit = own_tokens * inverse
    scaled = grad_first * first_gain2
    inner = jnp.mean(scaled * unit, axis=-1, keepdims=True)
    input_grad = own_gx1 + inverse * (scaled - unit * inner)
    first_sum = jnp.sum(grad_first * unit, axis=0)

    share = 1.0 / row_devices
    summed = all_sum(
        jnp.stack(
            [
                sum(losses)[0] * share,
                first_sum,
                sum(second_sums)[0] * share,
                sum(gain_sums)[0] * share,
            ]
        )
    )
    total_loss = jnp.sum(summed[0]) / (2.0 * total_tokens)

    dense_grads = dense_grads.astype(f32)
    late = late_grads.astype(f32)

    def part(k):
        return lax.slice_in_dim(late, k * width, (k + 1) * width, axis=1)

    return (
        total_loss,
        final_state[None],
        input_grad[None],
        grad_next[None],
        part(3),
        part(4),
        part(5),
        part(6).T,
        dense_grads[:, :hidden],
        dense_grads[:, hidden:].T,
        part(0),
        part(1),
        part(2),
        part(7).T,
        summed[1],
        summed[2],
        summed[3],
    )


def solution(mesh):
    in_specs = (
        P("col", "row", None),
        P("col", None, None),
        P("col", "row", None),
        P(),
        P("col", None),
        P("col", None),
        P(),
        P("col", "row"),
        P("col", "row"),
        P("col", "row"),
        P("row", "col"),
        P("col", None),
        P(None, "col"),
        P("col", "row"),
        P("col", "row"),
        P("col", "row"),
        P(None, "col"),
        P(),
        P(),
        P(),
    )
    out_specs = (
        P(),
        P("col", None, None),
        P("col", "row", None),
        P("col", None, None),
        P("col", "row"),
        P("col", "row"),
        P("col", "row"),
        P("row", "col"),
        P("col", "row"),
        P("row", "col"),
        P("col", "row"),
        P("col", "row"),
        P("col", "row"),
        P("row", "col"),
        P(),
        P(),
        P(),
    )
    return jax.shard_map(
        per_device, mesh=mesh, in_specs=in_specs, out_specs=out_specs, check_vma=False
    )
```

```python
import functools

import jax
import jax.numpy as jnp
from jax import lax
from jax.experimental import pallas as pl
from jax.experimental.pallas import tpu as pltpu
from jax.sharding import PartitionSpec as P

HEAD = 128
BLOCK = 512
HALF = 256
NS = 512
PIECE = 256
COST = 8

epsilon = 1e-06
masked_value = -1e30
score_scale = HEAD ** (-0.5)
log2_scale = score_scale * 1.4426950408889634
f32 = jnp.float32
bf16 = jnp.bfloat16


def dot_nn(a, b):
    return lax.dot_general(a, b, (((1,), (0,)), ((), ())), preferred_element_type=f32)


def dot_nt(a, b):
    return lax.dot_general(a, b, (((1,), (1,)), ((), ())), preferred_element_type=f32)


def dot_tn(a, b):
    return lax.dot_general(a, b, (((0,), (0,)), ((), ())), preferred_element_type=f32)


def cost(flops, arrays):
    return pl.CostEstimate(flops=flops // COST, bytes_accessed=1024, transcendentals=0)


def after(x, *earlier):
    return lax.optimization_barrier((x,) + earlier)[0]


def shaped(shape, dtype):
    return jax.ShapeDtypeStruct(shape, dtype)


def launch(body, idx, inputs, outputs, scratch=(), flops=0, vmem=12, name=None):
    return pl.pallas_call(
        body,
        in_specs=[pl.BlockSpec(memory_space=pltpu.SMEM)]
        + [pl.BlockSpec(memory_space=pltpu.VMEM)] * len(inputs),
        out_specs=[pl.BlockSpec(memory_space=pltpu.VMEM)] * len(outputs),
        out_shape=list(outputs),
        scratch_shapes=list(scratch),
        compiler_params=pltpu.CompilerParams(vmem_limit_bytes=vmem << 20),
        cost_estimate=cost(flops, inputs),
        name=name,
    )(idx, *inputs)


def rows_of(i, base=0, size=HALF):
    return pl.ds(pl.multiple_of(base + i * size, size), size)


def half_of(i, s):
    return lax.rem(i + s[1], 2)


def unit_rows(x):
    inverse = lax.rsqrt(jnp.mean(x * x, axis=-1, keepdims=True) + epsilon)
    return x * inverse, inverse


def unit_back(up, unit, inverse, gain):
    scaled = up * gain
    inner = jnp.mean(scaled * unit, axis=-1, keepdims=True)
    return inverse * (scaled - unit * inner)


def norm_project(idx, values, gain, weights, column, width, name):
    rows, features = values.shape

    def body(s, x_ref, g_ref, w_ref, n_ref, p_ref):
        @pl.loop(0, rows // HALF)
        def _(i):
            at = rows_of(i)
            unit, unused = unit_rows(x_ref[at, :].astype(f32))
            normed = (unit * g_ref[...]).astype(bf16)
            n_ref[at, :] = normed
            p_ref[at, :] = dot_nn(normed, w_ref[:, column : column + width]).astype(bf16)

    return launch(
        body,
        idx,
        [values, gain, weights],
        [shaped((rows, features), bf16), shaped((rows, width), bf16)],
        flops=2 * rows * features * width,
        name=name,
    )


def masked_scores(kind, keys, queries, katt, qatt):
    scores = dot_nt(keys, queries)
    if kind == "free":
        return scores
    if kind == "valid":
        return jnp.where(katt[:, 2:3] > 0.0, scores, masked_value)
    places = lax.broadcasted_iota(jnp.int32, scores.shape, 0)
    asking = lax.broadcasted_iota(jnp.int32, scores.shape, 1)
    same = katt[:, 0:1] == qatt[0:1, :]
    if kind == "prev":
        allowed = same & (places > asking)
    else:
        allowed = same & ((places <= asking) | (katt[:, 1:2] == qatt[1:2, :]))
    return jnp.where(allowed, scores, masked_value)


def attention_inputs(queries, segments, katt, qatt):
    arrays = []

    def place(array):
        for k, known in enumerate(arrays):
            if known is array:
                return k
        arrays.append(array)
        return len(arrays) - 1

    use_q = place(queries[0])
    use_k = [place(segment[1]) for segment in segments]
    use_att = place(katt)
    use_qatt = place(qatt) if qatt is not None else None
    return arrays, use_q, use_k, use_att, use_qatt


def read_attention(refs, uses, queries, segments, head):
    use_q, use_k, use_att, use_qatt = uses
    unused, q_row, q_col = queries

    def take(ref, row, col):
        lanes = pl.ds(pl.multiple_of(col + head * HEAD, HEAD), HEAD)
        return ref[row * BLOCK : (row + 1) * BLOCK, lanes]

    q = take(refs[use_q], q_row, q_col)
    parts = []
    for (kind, unused, row, k_col, v_col, att), k in zip(segments, use_k):
        rows = None if att is None else refs[use_att][att * BLOCK : (att + 1) * BLOCK, :]
        parts.append((kind, take(refs[k], row, k_col), take(refs[k], row, v_col), rows))
    qa = None if use_qatt is None else refs[use_qatt][:, q_row * BLOCK : (q_row + 1) * BLOCK]
    return q, parts, qa


def attend(idx, queries, segments, katt, qatt, heads, name):
    arrays, *uses = attention_inputs(queries, segments, katt, qatt)
    count = len(arrays)

    def body(s, *refs):
        o_ref, l_ref = refs[count:]

        @pl.loop(0, heads)
        def _(head):
            q, parts, qa = read_attention(refs, uses, queries, segments, head)
            scores = [masked_scores(kind, k, q, ka, qa) for kind, k, v, ka in parts]
            largest = functools.reduce(
                jnp.maximum, [jnp.max(x, axis=0, keepdims=True) for x in scores]
            )
            total = jnp.zeros_like(largest)
            mixed = jnp.zeros((HEAD, BLOCK), f32)
            for x, (kind, k, v, ka) in zip(scores, parts):
                raised = jnp.exp2((x - largest) * log2_scale)
                total = total + jnp.sum(raised, axis=0, keepdims=True)
                mixed = mixed + dot_tn(v, raised.astype(bf16))
            lanes = pl.ds(pl.multiple_of(head * HEAD, HEAD), HEAD)
            o_ref[:, lanes] = jnp.transpose(mixed * (1.0 / total)).astype(bf16)
            l_ref[head] = largest * log2_scale + jnp.log2(total)

    keys = BLOCK * len(segments)
    return launch(
        body,
        idx,
        arrays,
        [shaped((BLOCK, heads * HEAD), bf16), shaped((heads, 1, BLOCK), f32)],
        flops=4 * heads * BLOCK * keys * HEAD * 2,
        name=name,
    )


def attend_back(idx, queries, segments, katt, qatt, heads, logs, upstream, added, dtypes, name):
    arrays, *uses = attention_inputs(queries, segments, katt, qatt)
    count = len(arrays)
    inputs = arrays + [logs, upstream]
    for pairs in added:
        for pair in pairs:
            inputs.extend(pair)
    wide = (BLOCK, heads * HEAD)
    outputs = [shaped(wide, bf16)]
    for dtype in dtypes:
        outputs.extend([shaped(wide, dtype)] * 2)

    def body(s, *refs):
        rest = list(refs[count:])
        l_ref, go_ref = rest.pop(0), rest.pop(0)
        sums = []
        for pairs in added:
            sums.append([(rest.pop(0), rest.pop(0)) for unused in pairs])
        gq_ref = rest.pop(0)
        outs = list(zip(rest[0::2], rest[1::2]))

        @pl.loop(0, heads)
        def _(head):
            q, parts, qa = read_attention(refs, uses, queries, segments, head)
            lanes = pl.ds(pl.multiple_of(head * HEAD, HEAD), HEAD)
            log_total = l_ref[head]
            go = go_ref[:, lanes]
            chances, grads = [], []
            inner = jnp.zeros((1, BLOCK), f32)
            for kind, k, v, ka in parts:
                x = masked_scores(kind, k, q, ka, qa)
                chance = jnp.exp2(x * log2_scale - log_total)
                grad = dot_nt(v, go)
                inner = inner + jnp.sum(chance * grad, axis=0, keepdims=True)
                chances.append(chance)
                grads.append(grad)
            gq = jnp.zeros((HEAD, BLOCK), f32)
            for (kind, k, v, ka), chance, grad, pairs, out in zip(
                parts, chances, grads, sums, outs
            ):
                gl = (chance * (grad - inner)).astype(bf16)
                gk = dot_nn(gl, q) * score_scale
                gv = dot_nn(chance.astype(bf16), go)
                gq = gq + dot_tn(k, gl)
                for more_k, more_v in pairs:
                    gk = gk + more_k[:, lanes]
                    gv = gv + more_v[:, lanes]
                out[0][:, lanes] = gk.astype(out[0].dtype)
                out[1][:, lanes] = gv.astype(out[1].dtype)
            gq_ref[:, lanes] = jnp.transpose(gq * score_scale).astype(bf16)

    keys = BLOCK * len(segments)
    return launch(
        body,
        idx,
        inputs,
        outputs,
        flops=10 * heads * BLOCK * keys * HEAD * 2,
        vmem=20,
        name=name,
    )


def state_update(idx, pieces, write_pieces, state, retain, gain, weights, width, name):
    rows, features = state.shape
    count = len(pieces)
    project = weights is not None

    def body(s, *refs):
        refs = list(refs)
        piece_refs = [refs.pop(0) for unused in range(count)]
        w_refs = [refs.pop(0) for unused in range(count)]
        s_ref, r_ref = refs[:2]
        refs = refs[2:]
        if project:
            g_ref, p_ref, out_ref, n_ref, t_ref = refs
        else:
            (out_ref,) = refs

        @pl.loop(0, rows // HALF)
        def _(i):
            at = rows_of(i)
            terms = [
                dot_nt(o_ref[at, :], w_ref[:, : o_ref.shape[1]])
                for o_ref, w_ref in zip(piece_refs, w_refs)
            ]
            while len(terms) > 1:
                terms = [a + b for a, b in zip(terms[0::2], terms[1::2])]
            update = terms[0]
            keep = r_ref[...]
            following = keep * s_ref[at, :].astype(f32) + (1.0 - keep) * update
            out_ref[at, :] = following
            if project:
                normed = (unit_rows(following)[0] * g_ref[...]).astype(bf16)
                n_ref[at, :] = normed
                t_ref[at, :] = dot_nn(normed, p_ref[:, :width]).astype(bf16)

    inputs = list(pieces) + list(write_pieces) + [state, retain]
    outputs = [shaped((rows, features), f32)]
    if project:
        inputs += [gain, weights]
        outputs += [shaped((rows, features), bf16), shaped((rows, width), bf16)]
    return launch(
        body,
        idx,
        inputs,
        outputs,
        flops=2 * rows * features * (features + (width if project else 0)),
        name=name,
    )


def take_sum(i, refs, at, total):
    chip_ref, *others = refs
    parts = len(others) // 2
    width = others[0].shape[1]

    def take(refs):
        for k, ref in enumerate(refs):
            to = slice(k * width, (k + 1) * width)
            total[:, to] = chip_ref[at, to].astype(f32) + ref[...].astype(f32)

    @pl.when(i == 0)
    def _():
        take(others[:parts])

    @pl.when(i == 1)
    def _():
        take(others[parts:])

    return total[...]


def chip_sum(idx, partial, other, parts, name):
    rows, features = partial.shape
    width = features // parts

    def body(s, a_ref, b_ref, sum_ref, *own_refs):
        sum_ref[...] = (a_ref[...].astype(f32) + b_ref[...].astype(f32)).astype(bf16)
        at = rows_of(s[1])
        for k, ref in enumerate(own_refs):
            ref[...] = sum_ref[at, k * width : (k + 1) * width]

    return launch(
        body,
        idx,
        [partial, other],
        [shaped((rows, features), bf16)] + [shaped((HALF, width), bf16)] * parts,
        name=name,
    )


def add_rows(i, ref, value):
    value = jnp.sum(value, axis=0, keepdims=True)

    @pl.when(i == 0)
    def _():
        ref[...] = value

    @pl.when(i != 0)
    def _():
        ref[...] = ref[...] + value


def project_back(idx, grads, weights, column, name):
    rows, width = grads[0].shape
    features = weights.shape[0]

    def body(s, *refs):
        *g_refs, w_ref, out_ref = refs

        @pl.loop(0, 2)
        def _(i):
            at = rows_of(i)
            out = jnp.zeros((HALF, features), f32)
            for k, ref in enumerate(g_refs):
                first = column + k * width
                out = out + dot_nt(ref[at, :], w_ref[:, first : first + width])
            out_ref[at, :] = out.astype(bf16)

    return launch(
        body,
        idx,
        list(grads) + [weights],
        [shaped((rows, features), bf16)],
        flops=2 * rows * features * width * len(grads),
        name=name,
    )[0]


def state_back(idx, sums, state, following, retain, gain, write_own, name):
    rows, features = state.shape
    before = write_own is not None
    width = write_own.shape[1] // 2 if before else 10

    def body(s, *refs):
        refs = list(refs)
        total = refs.pop()
        sum_refs = [refs.pop(0) for unused in range(len(sums))]
        s_ref, r_ref, g_ref = refs[:3]
        refs = refs[3:]
        following_ref = refs.pop(0) if following is not None else None
        if before:
            w_ref, gs_ref, gain_ref, gu_ref, gos_ref = refs
        else:
            gs_ref, gain_ref = refs

        @pl.loop(0, 2)
        def _(i):
            at = rows_of(half_of(i, s))
            up = take_sum(i, sum_refs, at, total)
            unit, inverse = unit_rows(s_ref[at, :].astype(f32))
            out = unit_back(up, unit, inverse, g_ref[...])
            if following is not None:
                out = r_ref[...] * following_ref[at, :] + out
            gs_ref[at, :] = out
            add_rows(i, gain_ref, up * unit)
            if before:
                gu = ((1.0 - r_ref[...]) * out).astype(bf16)
                gu_ref[at, :] = gu
                gos_ref[at, :] = dot_nn(gu, w_ref[:, :width]).astype(bf16)

    inputs = list(sums) + [state, retain, gain]
    outputs = [shaped((rows, features), f32), shaped((1, features), f32)]
    if following is not None:
        inputs.append(following)
    if before:
        inputs.append(write_own)
        outputs += [shaped((rows, features), bf16), shaped((rows, width), bf16)]
    return launch(
        body,
        idx,
        inputs,
        outputs,
        scratch=[pltpu.VMEM((HALF, features), f32)],
        flops=2 * rows * features * width,
        name=name,
    )


def last_update_back(idx, retain, write_own, rows, name):
    features, width = write_own.shape[0], write_own.shape[1] // 2

    def body(s, r_ref, w_ref, gu_ref, gos_ref):
        gu = ((1.0 - r_ref[...]) * jnp.zeros((rows, features), f32)).astype(bf16)
        gu_ref[...] = gu
        gos_ref[...] = dot_nn(gu, w_ref[:, :width]).astype(bf16)

    return launch(
        body,
        idx,
        [retain, write_own],
        [shaped((rows, features), bf16), shaped((rows, width), bf16)],
        name=name,
    )


def gelu_both(a):
    root, cubic = 0.7978845608028654, 0.044715
    squared = a * a
    bent = jnp.tanh(root * (a + cubic * (squared * a)))
    rising = 0.5 * (1.0 + bent)
    slope = rising + (0.5 * root) * a * (1.0 - bent * bent) * (1.0 + (3.0 * cubic) * squared)
    return a * rising, slope


def dense_forward(idx, number, pieces, out_pieces, tokens, gain, dense, name):
    features = tokens.shape[1]
    hidden = dense.shape[1] // 2
    count = len(pieces)

    def body(s, *refs):
        refs = list(refs)
        o_refs = [refs.pop(0) for unused in range(count)]
        w_refs = [refs.pop(0) for unused in range(count)]
        t_ref, g_ref, d_ref = refs[:3]
        x1_ref, xn_ref, h_ref, slope_ref, part_ref = refs[3:]

        @pl.loop(0, 2)
        def _(i):
            at = rows_of(i)
            x1 = t_ref[rows_of(i, number * BLOCK), :].astype(f32)
            for o_ref, w_ref in zip(o_refs, w_refs):
                x1 = x1 + dot_nt(o_ref[at, :], w_ref[:, o_ref.shape[1] :])
            x1_ref[at, :] = x1
            normed = (unit_rows(x1)[0] * g_ref[...]).astype(bf16)
            xn_ref[at, :] = normed
            h, slope = gelu_both(dot_nn(normed, d_ref[:, :hidden]))
            h = h.astype(bf16)
            h_ref[at, :] = h
            slope_ref[at, :] = slope.astype(bf16)
            part_ref[at, :] = dot_nt(h, d_ref[:, hidden:]).astype(bf16)

    return launch(
        body,
        idx,
        list(pieces) + list(out_pieces) + [tokens, gain, dense],
        [
            shaped((BLOCK, features), f32),
            shaped((BLOCK, features), bf16),
            shaped((BLOCK, hidden), bf16),
            shaped((BLOCK, hidden), bf16),
            shaped((BLOCK, features), bf16),
        ],
        flops=2 * BLOCK * features * (features + 2 * hidden),
        name=name,
    )


def dense_backward(idx, number, sums, x1, teacher, katt, slope, dense, name):
    features = x1.shape[1]
    hidden = dense.shape[1] // 2

    def body(s, *refs):
        refs = list(refs)
        total = refs.pop()
        sum_refs = [refs.pop(0) for unused in range(len(sums))]
        x_ref, t_ref, v_ref, slope_ref, d_ref = refs[:5]
        gy_ref, gm_ref, ga_ref, loss_ref, part_ref = refs[5:]

        @pl.loop(0, 2)
        def _(i):
            half = half_of(i, s)
            at, far = rows_of(half), rows_of(half, number * BLOCK)
            errors = x_ref[at, :] + take_sum(i, sum_refs, at, total) - t_ref[far, :].astype(f32)
            gy = v_ref[far, 2:3] * errors
            gy_ref[at, :] = gy
            add_rows(i, loss_ref, gy * errors)
            gm = gy.astype(bf16)
            gm_ref[at, :] = gm
            ga = (dot_nn(gm, d_ref[:, hidden:]) * slope_ref[at, :].astype(f32)).astype(bf16)
            ga_ref[at, :] = ga
            part_ref[at, :] = dot_nt(ga, d_ref[:, :hidden]).astype(bf16)

    return launch(
        body,
        idx,
        list(sums) + [x1, teacher, katt, slope, dense],
        [
            shaped((BLOCK, features), f32),
            shaped((BLOCK, features), bf16),
            shaped((BLOCK, hidden), bf16),
            shaped((1, features), f32),
            shaped((BLOCK, features), bf16),
        ],
        scratch=[pltpu.VMEM((HALF, features), f32)],
        flops=4 * BLOCK * features * hidden,
        name=name,
    )


def output_backward(idx, sums, gy, x1, gain, out_own, name):
    features = x1.shape[1]
    width = out_own.shape[1] // 2

    def body(s, *refs):
        refs = list(refs)
        total = refs.pop()
        sum_refs = [refs.pop(0) for unused in range(len(sums))]
        gy_ref, x_ref, g_ref, w_ref, gx_ref, gp_ref, go_ref, gain_ref = refs

        @pl.loop(0, 2)
        def _(i):
            at = rows_of(half_of(i, s))
            up = take_sum(i, sum_refs, at, total)
            unit, inverse = unit_rows(x_ref[at, :])
            gx = gy_ref[at, :] + unit_back(up, unit, inverse, g_ref[...])
            gx_ref[at, :] = gx
            gp = gx.astype(bf16)
            gp_ref[at, :] = gp
            go_ref[at, :] = dot_nn(gp, w_ref[:, width:]).astype(bf16)
            add_rows(i, gain_ref, up * unit)

    return launch(
        body,
        idx,
        list(sums) + [gy, x1, gain, out_own],
        [
            shaped((BLOCK, features), f32),
            shaped((BLOCK, features), bf16),
            shaped((BLOCK, width), bf16),
            shaped((1, features), f32),
        ],
        scratch=[pltpu.VMEM((HALF, features), f32)],
        flops=2 * BLOCK * features * width,
        name=name,
    )


def weight_grads(idx, groups, name):
    features = groups[0][0][0].shape[1]
    inputs, specs, total, flops = [], [], 0, 0
    for parts in groups:
        for left, block, right in parts:
            rows = right.shape[0]
            inputs += [left, right]
            specs.append(pl.BlockSpec((rows, HALF), lambda i, block=block: (block, i)))
            specs.append(
                pl.BlockSpec(right.shape, lambda i: (0, 0), pipeline_mode=pl.Buffered(1))
            )
            flops += 2 * rows * features * right.shape[1]
        total += parts[0][2].shape[1]

    def body(s, *refs):
        refs = list(refs)
        out_ref = refs.pop()
        at = 0
        for parts in groups:
            size = parts[0][2].shape[1]
            out = jnp.zeros((HALF, size), f32)
            for unused in parts:
                left, right = refs.pop(0), refs.pop(0)
                out = out + dot_tn(left[...], right[...])
            out_ref[:, at : at + size] = out.astype(bf16)
            at += size

    return pl.pallas_call(
        body,
        grid=(features // HALF,),
        in_specs=[pl.BlockSpec(memory_space=pltpu.SMEM)] + specs,
        out_specs=pl.BlockSpec((HALF, total), lambda i: (i, 0)),
        out_shape=pltpu.HBM((features, total), bf16),
        compiler_params=pltpu.CompilerParams(
            dimension_semantics=("arbitrary",), vmem_limit_bytes=20 << 20
        ),
        cost_estimate=cost(flops, inputs),
        name=name,
    )(idx, *inputs)


def unpack_grads(packed, widths, flipped, name):
    rows = packed.shape[0]

    def body(p_ref, *out_refs):
        at = 0
        for size, flip, out_ref in zip(widths, flipped, out_refs):
            values = p_ref[:, at : at + size].astype(f32)
            out_ref[...] = jnp.transpose(values) if flip else values
            at += size

    return pl.pallas_call(
        body,
        in_specs=[pl.BlockSpec(memory_space=pltpu.VMEM)],
        out_specs=[pl.BlockSpec(memory_space=pltpu.VMEM)] * len(widths),
        out_shape=[
            shaped((size, rows) if flip else (rows, size), f32)
            for size, flip in zip(widths, flipped)
        ],
        compiler_params=pltpu.CompilerParams(vmem_limit_bytes=8 << 20),
        cost_estimate=cost(0, [packed]),
        name=name,
    )(packed)


def arrange_rows(idx, pieces, count, name):
    rows, features = pieces[0].shape
    rows = rows // count

    def body(s, *refs):
        ins, outs = refs[: len(pieces)], refs[len(pieces) :]
        for k, ref in enumerate(ins):
            for j, out_ref in enumerate(outs):
                out_ref[rows_of(s[0] ^ k, 0, rows), :] = ref[j * rows : (j + 1) * rows, :]

    return launch(
        body,
        idx,
        pieces,
        [shaped((rows * len(pieces), features), pieces[0].dtype)] * count,
        name=name,
    )


def arrange_columns(idx, moved, widths, name):
    rows = moved[0].shape[0] // 2

    def body(s, *refs):
        ins, outs = refs[:6], refs[6:]
        z, y = s[3], s[4]
        middle = (z == 1) | (z == 2)
        source = jnp.where(z < 2, 2, 1)

        def put(level, side, ref):
            for k in range(2):
                at = 0
                for out_ref, width in zip(outs, widths):
                    place = rows_of(2 * (level ^ k) + side, 0, rows)
                    out_ref[place, :] = ref[k * rows : (k + 1) * rows, at : at + width]
                    at += width

        put(z, y, ins[0])
        put(z, 1 - y, ins[1])

        @pl.when(middle)
        def _():
            put(source, y, ins[2])
            put(source, 1 - y, ins[3])

        @pl.when(jnp.logical_not(middle))
        def _():
            put(source, y, ins[4])
            put(source, 1 - y, ins[5])

    return launch(
        body,
        idx,
        moved,
        [shaped((8 * rows, width), moved[0].dtype) for width in widths],
        name=name,
    )


def pack(idx, arrays, takes, shapes, name):
    flipped = [take for take in takes if take[-1]]

    def body(s, *refs):
        ins, outs = refs[: len(arrays)], refs[len(arrays) : len(arrays) + len(shapes)]
        *held, sems = refs[len(arrays) + len(shapes) :]
        copies, spare = [], list(held)
        for j, (k, row, col, rows, cols, out, place, flip) in enumerate(takes):
            at = pl.ds(0, rows) if row is None else rows_of(s[row], 0, rows)
            to = pl.ds(0, cols) if col is None else rows_of(s[col], 0, cols)
            if flip:
                target = spare.pop(0)
            else:
                target = outs[out].at[pl.ds(place[0], rows), pl.ds(place[1], cols)]
            copies.append(pltpu.make_async_copy(ins[k].at[at, to], target, sems.at[j]))
            copies[-1].start()
        spare = list(held)
        for copy, (k, row, col, rows, cols, out, place, flip) in zip(copies, takes):
            copy.wait()
            if flip:
                to = slice(place[1], place[1] + rows)
                outs[out][place[0] : place[0] + cols, to] = jnp.transpose(spare.pop(0)[...])

    return pl.pallas_call(
        body,
        in_specs=[pl.BlockSpec(memory_space=pltpu.SMEM)]
        + [pl.BlockSpec(memory_space=pl.ANY)] * len(arrays),
        out_specs=[pl.BlockSpec(memory_space=pltpu.VMEM)] * len(shapes),
        out_shape=[shaped(a, bf16) for a in shapes],
        scratch_shapes=[pltpu.VMEM((take[3], take[4]), bf16) for take in flipped]
        + [pltpu.SemaphoreType.DMA((len(takes),))],
        compiler_params=pltpu.CompilerParams(vmem_limit_bytes=8 << 20),
        cost_estimate=cost(0, arrays),
        name=name,
    )(idx, *[pltpu.with_memory_space_constraint(a, pltpu.HBM) for a in arrays])


def input_rows(idx, own, arrived, gx1s, tokens, gain, name):
    rows, features = tokens.shape
    count = len(gx1s)

    def body(s, *refs):
        own_refs, far_refs, gx_refs = refs[:count], refs[count : 2 * count], refs[2 * count : 3 * count]
        t_ref, g_ref, out_ref, gain_ref = refs[3 * count :]
        unit, inverse = unit_rows(t_ref[...].astype(f32))
        for b in range(count):

            @pl.when(s[2] // 2 == b)
            def _():
                at = rows_of(s[1])
                up = own_refs[b][at, :].astype(f32) + far_refs[b][...].astype(f32)
                base = gx_refs[b][rows_of(s[1]), :]
                out_ref[...] = base + unit_back(up, unit, inverse, g_ref[...])
                gain_ref[...] = jnp.sum(up * unit, axis=0, keepdims=True)

    return launch(
        body,
        idx,
        list(own) + list(arrived) + list(gx1s) + [tokens, gain],
        [shaped((rows, features), f32), shaped((1, features), f32)],
        name=name,
    )


def per_device(
    block_input,
    state_start,
    teacher,
    valid_mask,
    segment,
    image_offset,
    retain,
    to_query,
    to_key,
    to_value,
    to_output,
    to_hidden,
    to_model,
    state_query,
    state_key,
    state_value,
    state_write,
    first_gain,
    second_gain,
    state_gain,
):
    row_devices = lax.axis_size("row")
    col_devices = lax.axis_size("col")
    row_index = lax.axis_index("row")
    col_index = lax.axis_index("col")
    local_rows, features = block_input.shape[1:]
    length = local_rows * row_devices
    width = to_query.shape[1]
    heads = width // HEAD
    hidden = to_hidden.shape[1] // row_devices
    nblocks = length // BLOCK
    pairs = row_devices == 4 and 2 * local_rows == BLOCK
    lines = pairs and col_devices == 8
    core_pairs = [(k, k ^ 1) for k in range(row_devices)]
    chip_pairs = [(k, k ^ 2) for k in range(row_devices)] if pairs else None
    if pairs:
        idx = jnp.stack([row_index, row_index % 2, row_index, col_index // 2, col_index % 2])
    else:
        idx = jnp.stack([0, 1, row_index, 0, 0])
    idx = idx.astype(jnp.int32)

    def to_core(x):
        return lax.ppermute(x, "row", core_pairs)

    def to_chip(x):
        return lax.ppermute(x, "row", chip_pairs)

    def row_moves(x):
        if not pairs:
            stacked = lax.all_gather(x, "row", axis=0, tiled=False)
            return [stacked[k] for k in range(row_devices)]
        return [x, to_core(x), to_chip(x)]

    def row_pieces(moved, *ties):
        if not pairs:
            return moved
        x, near, far = moved
        return [x, near, far, to_core(after(far, *ties))]

    def along(v, steps):
        moves = [(2 * a + y, 2 * b + y) for a, b in steps for y in range(2)]
        return lax.ppermute(v, "col", moves)

    def across(v, levels):
        moves = [(2 * z + y, 2 * z + 1 - y) for z in levels for y in range(2)]
        return lax.ppermute(v, "col", moves)

    def col_order(x, widths, name):
        return col_arrange(col_last(col_moves(x)), widths, name)

    def col_arrange(moved, widths, name):
        if lines:
            return arrange_columns(idx, moved, widths, name)
        ends = [sum(widths[:k]) for k in range(len(widths) + 1)]
        return [lax.slice_in_dim(moved, a, b, axis=1) for a, b in zip(ends[:-1], ends[1:])]

    def col_moves(x):
        if not lines:
            return lax.all_gather(x, "col", axis=0, tiled=True)

        near_two = jnp.concatenate([x, along(x, [(0, 1), (1, 0), (2, 3), (3, 2)])])
        far_mid = along(near_two, [(1, 2), (2, 1)])
        far_end = along(far_mid, [(1, 0), (2, 3)])
        return [near_two, across(near_two, range(4)), far_mid, across(far_mid, (1, 2)), far_end]

    def col_last(moved):
        if not lines:
            return moved
        return moved + [across(moved[-1], (0, 3))]

    class RowSum:
        def __init__(self, partial, name, receiver=None):
            if pairs:
                self.chip, own = chip_sum(idx, partial, to_core(partial), 1, name)
                moves = [m for m in chip_pairs if receiver is None or m[1] // 2 == receiver]
                self.far = lax.ppermute(own, "row", moves)
            else:
                self.chip = lax.psum(partial, "row")

        def result(self, *ties):
            if pairs:
                return [self.chip, self.far, to_core(after(self.far, *ties))]
            none = jnp.zeros((HALF, features), bf16)
            return [self.chip, none, none]

    def all_sum(x):
        for axis, size in (("row", row_devices), ("col", col_devices)):
            step = 1
            while step < size:
                x = x + lax.ppermute(x, axis, [(k, k ^ step) for k in range(size)])
                step *= 2
        return x

    depth = to_query.shape[0]
    (near,) = pack(
        idx,
        [state_query, state_key, state_value, to_query, to_key, to_value],
        [(k, None, None, depth, width, 0, (0, k * width), False) for k in range(6)],
        [(depth, 6 * width)],
        "pack_near",
    )
    near = lax.all_gather(near, "col", axis=0, tiled=True)
    rows_in, mid, far_weights = pack(
        idx,
        [state_write, to_output, to_hidden, to_model, block_input[0], teacher[0]],
        [
            (4, None, None, local_rows, features, 0, (0, 0), False),
            (5, None, None, local_rows, features, 0, (local_rows, 0), False),
            (0, 2, None, width, depth, 1, (0, 0), True),
            (1, None, None, width, depth, 1, (0, width), True),
            (2, None, 2, depth, hidden, 2, (0, 0), False),
            (3, 2, None, hidden, depth, 2, (0, hidden), True),
        ],
        [(2 * local_rows, features), (depth, 2 * width), (depth, 2 * hidden)],
        "pack_rest",
    )
    rows_moved = row_moves(rows_in) if pairs else None
    (mid,) = col_order(mid, [2 * width], "mid")
    mid_moved = row_moves(mid)
    if pairs:
        tokens, teacher_all = arrange_rows(idx, row_pieces(rows_moved), 2, "tokens")
    else:
        tokens, teacher_all = [
            lax.all_gather(x[0], "row", axis=0, tiled=True) for x in (block_input, teacher)
        ]
    dense = lax.all_gather(after(far_weights, mid), "col", axis=0, tiled=True)

    valid_row = lax.dynamic_index_in_dim(valid_mask, col_index, 0, keepdims=False)
    segment_row = segment[0]
    numbers = jnp.arange(nblocks, dtype=jnp.int32)
    places = jnp.arange(length, dtype=jnp.int32)
    starts = numbers * BLOCK + image_offset[0]
    inside = (places[:, None] >= starts[None, :]) & (places[:, None] < starts[None, :] + PIECE)
    piece = jnp.sum(jnp.where(inside, numbers[None, :] + 1, 0), axis=1) - 1
    valid_count = jnp.sum(valid_mask.astype(f32))
    total_tokens = f32(length * col_devices)
    weight_of_row = total_tokens / valid_count * valid_row.astype(f32)
    document = segment_row.astype(f32)
    nothing = jnp.zeros_like(document)
    katt = jnp.stack(
        [jnp.where(valid_row > 0, document, -1.0), piece.astype(f32), weight_of_row, nothing],
        axis=1,
    )
    qatt = jnp.stack(
        [document, jnp.where(piece >= 0, piece, -2).astype(f32), nothing, nothing], axis=0
    )
    retain2 = retain[None]
    first_gain2, second_gain2, state_gain2 = first_gain[None], second_gain[None], state_gain[None]

    def token_segments(number, trio):
        found = []
        if number > 0:
            found.append(("prev", token_heads, number - 1, width, 2 * width, number - 1))
        found.append(("own", token_heads, number, width, 2 * width, number))
        found.append(("free", trio, 0, width, 2 * width, None))
        return found

    def state_segments(number, trio):
        return [
            ("valid", token_heads, number, width, 2 * width, number),
            ("free", trio, 0, width, 2 * width, None),
        ]

    current = state_start[0]
    state_low, trio = norm_project(idx, current, state_gain2, near, 0, 3 * width, "state_proj")
    first_low, token_heads = norm_project(
        idx, tokens, first_gain2, near, 3 * width, 3 * width, "token_proj"
    )
    states, lows, trios = [], [], []
    state_out, state_logs, token_out, token_logs = [], [], [], []
    x1s, second_lows, hiddens, slopes, dense_sums = [], [], [], [], []
    state_pieces, token_pieces = [], []

    def state_part(b):
        mixed, logs = attend(
            idx,
            (trios[b], 0, 0),
            state_segments(b, trios[b]),
            katt,
            None,
            heads,
            f"state_attend{b}",
        )
        state_out.append(mixed)
        state_logs.append(logs)
        state_pieces.append(row_moves(mixed) if b < nblocks - 1 else None)

    for b in range(nblocks):
        states.append(current)
        lows.append(state_low)
        trios.append(trio)
        last = b + 1 == nblocks
        if not last:
            state_part(b)
        if b == 0:
            mid_pieces = row_pieces(mid_moved)
        mixed, logs = attend(
            idx, (token_heads, b, 0), token_segments(b, trio), katt, qatt, heads, f"token_attend{b}"
        )
        token_out.append(mixed)
        token_logs.append(logs)
        token_pieces.append(row_moves(mixed))
        if not last:
            current, state_low, trio = state_update(
                idx,
                row_pieces(state_pieces[b], mixed),
                mid_pieces,
                current,
                retain2,
                state_gain2,
                near,
                3 * width,
                f"update{b}",
            )
            token_pieces[b] = row_pieces(token_pieces[b], trio)
    state_part(nblocks - 1)
    token_pieces[-1] = row_pieces(token_pieces[-1], state_out[-1])

    end = nblocks - 1
    gus = [None] * nblocks
    gms, gas, losses, gx1s, gps, gos, second_sums = [], [], [], [], [], [], []
    gys, second_back = [], []
    ready = after(tokens, state_out[-1], token_pieces[-1][2])
    for b in range(nblocks):
        x1, low, h, slope, partial = dense_forward(
            idx, b, token_pieces[b], mid_pieces, ready, second_gain2, dense, f"dense{b}"
        )
        x1s.append(x1)
        second_lows.append(low)
        hiddens.append(h)
        slopes.append(slope)
        dense_sums.append(RowSum(partial, f"dense_sum{b}"))
        ready = after(tokens, dense_sums[b].chip)

    def state_back_part(b, gos_state, own, free, dtype):
        return attend_back(
            idx,
            (trios[b], 0, 0),
            state_segments(b, trios[b]),
            katt,
            None,
            heads,
            state_logs[b],
            gos_state,
            [own, free],
            [dtype, dtype],
            f"state_back{b}",
        )

    def token_back_part(b, own, free, dtype, upstream):
        segments = token_segments(b, trios[b])
        added = ([[]] if b > 0 else []) + [own, free]
        dtypes = ([f32] if b > 0 else []) + [dtype, dtype]
        found = attend_back(
            idx,
            (token_heads, b, 0),
            segments,
            katt,
            qatt,
            heads,
            token_logs[b],
            upstream,
            added,
            dtypes,
            f"token_back{b}",
        )
        return found[0], found[-4:], (found[1], found[2]) if b > 0 else None

    late_mid = after(mid, dense_sums[end].chip)
    gus[end], gos_state = last_update_back(idx, retain2, late_mid, NS, "last_back")
    state_found = state_back_part(end, gos_state, [], [], f32)
    ready = teacher_all
    for b in range(nblocks):
        hides = [x1s[end]] if b == 0 else [gys[b - 1], state_found[0]]
        gy, gm, ga, loss, partial = dense_backward(
            idx, b, dense_sums[b].result(*hides), x1s[b], ready, katt, slopes[b], dense, f"back{b}"
        )
        gms.append(gm)
        gas.append(ga)
        losses.append(loss)
        gys.append(gy)
        second_back.append(RowSum(partial, f"back_sum{b}"))
        ready = after(teacher_all, second_back[b].chip)
    landed = [second_back[-1].chip] + ([second_back[0].far] if pairs else [])
    dense_grads = weight_grads(
        idx,
        [
            [(low, 0, ga) for low, ga in zip(second_lows, gas)],
            [(after(gm, *landed), 0, h) for gm, h in zip(gms, hiddens)],
        ],
        "dense_grads",
    )
    filled = [dense_grads]
    dense_grads = lax.psum_scatter(dense_grads, "col", scatter_dimension=0, tiled=True)

    token_found = [None] * nblocks
    for b in range(nblocks):
        gx1, gp, go, gain_sum = output_backward(
            idx,
            second_back[b].result(*(filled if b == end else [gys[end]])),
            gys[b],
            x1s[b],
            second_gain2,
            mid,
            f"out_back{b}",
        )
        gx1s.append(gx1)
        gps.append(gp)
        gos.append(go)
        second_sums.append(gain_sum)
        if b < end:
            token_found[b] = token_back_part(b, [], [], f32, go)
            filled.append(token_found[b][0])
    trio_grads = [None] * nblocks
    token_grads = [None] * nblocks
    first_sums = [None] * nblocks
    gain_sums = []
    grad_next = None
    gqs, gk, gv, gks, gvs = state_found
    gq, (gk, gv, gks, gvs), key_part = token_back_part(
        end, [(gk, gv)], [(gks, gvs)], bf16, gos[end]
    )
    state_pieces[-1] = row_moves(after(state_out[-1], gos[end]))
    gqs = after(gqs, state_pieces[-1][2])
    trio_grads[end] = (gqs, gks, gvs)
    token_grads[end] = (gq, gk, gv)
    for b in reversed(range(nblocks)):
        trio_sum = RowSum(project_back(idx, trio_grads[b], near, 0, f"trio_back{b}"), f"trio_sum{b}")
        if b == 0:
            late_grads = weight_grads(
                idx,
                [[(lows[b], 0, trio_grads[b][k]) for b in range(nblocks)] for k in range(3)]
                + [[(first_low, b, token_grads[b][k]) for b in range(nblocks)] for k in range(3)]
                + [
                    [(gp, 0, out) for gp, out in zip(gps, token_out)],
                    [(gu, 0, out) for gu, out in zip(gus, state_out)],
                ],
                "late_grads",
            )
            late_grads = lax.psum_scatter(late_grads, "col", scatter_dimension=0, tiled=True)
        hides = []
        if b == end:
            (final_state,) = state_update(
                idx,
                row_pieces(state_pieces[-1], gq),
                mid_pieces,
                current,
                retain2,
                None,
                None,
                0,
                "update_last",
            )
            hides.append(final_state)
        first_sums[b] = project_back(idx, token_grads[b], near, 3 * width, f"first_back{b}")
        hides.append(first_sums[b])
        first_sums[b] = RowSum(first_sums[b], f"first_sum{b}", b) if pairs else first_sums[b]
        if b > 0:
            grad_next, gain_sum, gus[b - 1], gos_state = state_back(
                idx,
                trio_sum.result(*hides),
                states[b],
                grad_next,
                retain2,
                state_gain2,
                mid,
                f"chain_back{b}",
            )
            gq, (gk, gv, gks, gvs), next_part = token_found[b - 1]
            gqs, gk, gv, gks, gvs = state_back_part(
                b - 1, gos_state, [(gk, gv), key_part], [(gks, gvs)], bf16
            )
            key_part = next_part
            trio_grads[b - 1] = (gqs, gks, gvs)
            token_grads[b - 1] = (gq, gk, gv)
        else:
            grad_next, gain_sum = state_back(
                idx,
                trio_sum.result(*hides),
                states[b],
                grad_next,
                retain2,
                state_gain2,
                None,
                "chain_back0",
            )
        gain_sums.append(gain_sum)

    if pairs:
        own_rows = [first.chip for first in first_sums]
        arrived = [first.far for first in first_sums]
        input_grad, first_sum = input_rows(
            idx, own_rows, arrived, gx1s, block_input[0], first_gain2, "input_rows"
        )
        first_sum = first_sum[0]
    else:
        both = jnp.concatenate(first_sums)
        grad_first = lax.psum_scatter(both, "row", scatter_dimension=0, tiled=True).astype(f32)
        own_gx1 = lax.dynamic_slice_in_dim(
            jnp.concatenate(gx1s), row_index * local_rows, local_rows
        )
        unit, inverse = unit_rows(block_input[0].astype(f32))
        input_grad = own_gx1 + unit_back(grad_first, unit, inverse, first_gain2)
        first_sum = jnp.sum(grad_first * unit, axis=0)

    share = 1.0 / row_devices
    summed = all_sum(
        jnp.stack(
            [
                sum(losses)[0] * share,
                first_sum,
                sum(second_sums)[0] * share,
                sum(gain_sums)[0] * share,
            ]
        )
    )
    total_loss = jnp.sum(summed[0]) / (2.0 * total_tokens)

    upper_grad, lower_grad = unpack_grads(
        dense_grads, [hidden, hidden], [False, True], "unpack_dense"
    )
    late = unpack_grads(late_grads, [width] * 8, [False] * 6 + [True] * 2, "unpack_late")

    return (
        total_loss,
        final_state[None],
        input_grad[None],
        grad_next[None],
        late[3],
        late[4],
        late[5],
        late[6],
        upper_grad,
        lower_grad,
        late[0],
        late[1],
        late[2],
        late[7],
        summed[1],
        summed[2],
        summed[3],
    )


def solution(mesh):
    in_specs = (
        P("col", "row", None),
        P("col", None, None),
        P("col", "row", None),
        P(),
        P("col", None),
        P("col", None),
        P(),
        P("col", "row"),
        P("col", "row"),
        P("col", "row"),
        P("row", "col"),
        P("col", None),
        P(None, "col"),
        P("col", "row"),
        P("col", "row"),
        P("col", "row"),
        P(None, "col"),
        P(),
        P(),
        P(),
    )
    out_specs = (
        P(),
        P("col", None, None),
        P("col", "row", None),
        P("col", None, None),
        P("col", "row"),
        P("col", "row"),
        P("col", "row"),
        P("row", "col"),
        P("col", "row"),
        P("row", "col"),
        P("col", "row"),
        P("col", "row"),
        P("col", "row"),
        P("row", "col"),
        P(),
        P(),
        P(),
    )
    return jax.shard_map(
        per_device, mesh=mesh, in_specs=in_specs, out_specs=out_specs, check_vma=False
    )
```

```python
import functools

import jax
import jax.numpy as jnp
from jax import lax
from jax.experimental import pallas as pl
from jax.experimental.pallas import tpu as pltpu
from jax.sharding import PartitionSpec as P

HEAD = 128
BLOCK = 512
HALF = 256
NS = 512
PIECE = 256
COST = 8
TILE = 256

epsilon = 1e-06
masked_value = -1e30
score_scale = HEAD ** (-0.5)
log2_scale = score_scale * 1.4426950408889634
f32 = jnp.float32
bf16 = jnp.bfloat16


def dot_nn(a, b):
    return lax.dot_general(a, b, (((1,), (0,)), ((), ())), preferred_element_type=f32)


def dot_nt(a, b):
    return lax.dot_general(a, b, (((1,), (1,)), ((), ())), preferred_element_type=f32)


def dot_tn(a, b):
    return lax.dot_general(a, b, (((0,), (0,)), ((), ())), preferred_element_type=f32)


def cost(flops, arrays):
    return pl.CostEstimate(flops=flops // COST, bytes_accessed=1024, transcendentals=0)


def after(x, *earlier):
    return lax.optimization_barrier((x,) + earlier)[0]


def shaped(shape, dtype):
    return jax.ShapeDtypeStruct(shape, dtype)


def launch(body, idx, inputs, outputs, scratch=(), flops=0, vmem=12, name=None):
    return pl.pallas_call(
        body,
        in_specs=[pl.BlockSpec(memory_space=pltpu.SMEM)]
        + [pl.BlockSpec(memory_space=pltpu.VMEM)] * len(inputs),
        out_specs=[pl.BlockSpec(memory_space=pltpu.VMEM)] * len(outputs),
        out_shape=list(outputs),
        scratch_shapes=list(scratch),
        compiler_params=pltpu.CompilerParams(vmem_limit_bytes=vmem << 20),
        cost_estimate=cost(flops, inputs),
        name=name,
    )(idx, *inputs)


def rows_of(i, base=0, size=HALF):
    return pl.ds(pl.multiple_of(base + i * size, size), size)


def tile_start(i, s):
    steps = HALF // TILE
    return lax.rem(i // steps + s[1], 2) * HALF + lax.rem(i, steps) * TILE


def span(start, base=0):
    return pl.ds(pl.multiple_of(base + start, TILE), TILE)


def unit_rows(x):
    inverse = lax.rsqrt(jnp.mean(x * x, axis=-1, keepdims=True) + epsilon)
    return x * inverse, inverse


def unit_back(up, unit, inverse, gain):
    scaled = up * gain
    inner = jnp.mean(scaled * unit, axis=-1, keepdims=True)
    return inverse * (scaled - unit * inner)


def norm_project(idx, values, gain, weights, column, width, name):
    rows, features = values.shape

    def body(s, x_ref, g_ref, w_ref, n_ref, p_ref):
        @pl.loop(0, rows // TILE)
        def _(i):
            at = span(i * TILE)
            unit, unused = unit_rows(x_ref[at, :].astype(f32))
            normed = (unit * g_ref[...]).astype(bf16)
            n_ref[at, :] = normed
            p_ref[at, :] = dot_nn(normed, w_ref[:, column : column + width]).astype(bf16)

    return launch(
        body,
        idx,
        [values, gain, weights],
        [shaped((rows, features), bf16), shaped((rows, width), bf16)],
        flops=2 * rows * features * width,
        name=name,
    )


def masked_scores(kind, keys, queries, katt, qatt):
    scores = dot_nt(keys, queries)
    if kind == "free":
        return scores
    if kind == "valid":
        return jnp.where(katt[:, 2:3] > 0.0, scores, masked_value)
    places = lax.broadcasted_iota(jnp.int32, scores.shape, 0)
    asking = lax.broadcasted_iota(jnp.int32, scores.shape, 1)
    same = katt[:, 0:1] == qatt[0:1, :]
    if kind == "prev":
        allowed = same & (places > asking)
    else:
        allowed = same & ((places <= asking) | (katt[:, 1:2] == qatt[1:2, :]))
    return jnp.where(allowed, scores, masked_value)


def attention_inputs(queries, segments, katt, qatt):
    arrays = []

    def place(array):
        for k, known in enumerate(arrays):
            if known is array:
                return k
        arrays.append(array)
        return len(arrays) - 1

    use_q = place(queries[0])
    use_k = [place(segment[1]) for segment in segments]
    use_att = place(katt)
    use_qatt = place(qatt) if qatt is not None else None
    return arrays, use_q, use_k, use_att, use_qatt


def read_attention(refs, uses, queries, segments, head):
    use_q, use_k, use_att, use_qatt = uses
    unused, q_row, q_col = queries

    def take(ref, row, col):
        lanes = pl.ds(pl.multiple_of(col + head * HEAD, HEAD), HEAD)
        return ref[row * BLOCK : (row + 1) * BLOCK, lanes]

    q = take(refs[use_q], q_row, q_col)
    parts = []
    for (kind, unused, row, k_col, v_col, att), k in zip(segments, use_k):
        rows = None if att is None else refs[use_att][att * BLOCK : (att + 1) * BLOCK, :]
        parts.append((kind, take(refs[k], row, k_col), take(refs[k], row, v_col), rows))
    qa = None if use_qatt is None else refs[use_qatt][:, q_row * BLOCK : (q_row + 1) * BLOCK]
    return q, parts, qa


def attend(idx, queries, segments, katt, qatt, heads, name):
    arrays, *uses = attention_inputs(queries, segments, katt, qatt)
    count = len(arrays)

    def body(s, *refs):
        o_ref, l_ref = refs[count:]

        @pl.loop(0, heads)
        def _(head):
            q, parts, qa = read_attention(refs, uses, queries, segments, head)
            scores = [masked_scores(kind, k, q, ka, qa) for kind, k, v, ka in parts]
            largest = functools.reduce(
                jnp.maximum, [jnp.max(x, axis=0, keepdims=True) for x in scores]
            )
            total = jnp.zeros_like(largest)
            mixed = jnp.zeros((HEAD, BLOCK), f32)
            for x, (kind, k, v, ka) in zip(scores, parts):
                raised = jnp.exp2((x - largest) * log2_scale)
                total = total + jnp.sum(raised, axis=0, keepdims=True)
                mixed = mixed + dot_tn(v, raised.astype(bf16))
            lanes = pl.ds(pl.multiple_of(head * HEAD, HEAD), HEAD)
            o_ref[:, lanes] = jnp.transpose(mixed * (1.0 / total)).astype(bf16)
            l_ref[head] = largest * log2_scale + jnp.log2(total)

    keys = BLOCK * len(segments)
    return launch(
        body,
        idx,
        arrays,
        [shaped((BLOCK, heads * HEAD), bf16), shaped((heads, 1, BLOCK), f32)],
        flops=4 * heads * BLOCK * keys * HEAD * 2,
        name=name,
    )


def attend_back(idx, queries, segments, katt, qatt, heads, logs, upstream, added, dtypes, name):
    arrays, *uses = attention_inputs(queries, segments, katt, qatt)
    count = len(arrays)
    inputs = arrays + [logs, upstream]
    for pairs in added:
        for pair in pairs:
            inputs.extend(pair)
    wide = (BLOCK, heads * HEAD)
    outputs = [shaped(wide, bf16)]
    for dtype in dtypes:
        outputs.extend([shaped(wide, dtype)] * 2)

    def body(s, *refs):
        rest = list(refs[count:])
        l_ref, go_ref = rest.pop(0), rest.pop(0)
        sums = []
        for pairs in added:
            sums.append([(rest.pop(0), rest.pop(0)) for unused in pairs])
        gq_ref = rest.pop(0)
        outs = list(zip(rest[0::2], rest[1::2]))

        @pl.loop(0, heads)
        def _(head):
            q, parts, qa = read_attention(refs, uses, queries, segments, head)
            lanes = pl.ds(pl.multiple_of(head * HEAD, HEAD), HEAD)
            log_total = l_ref[head]
            go = go_ref[:, lanes]
            chances, grads = [], []
            inner = jnp.zeros((1, BLOCK), f32)
            for kind, k, v, ka in parts:
                x = masked_scores(kind, k, q, ka, qa)
                chance = jnp.exp2(x * log2_scale - log_total)
                grad = dot_nt(v, go)
                inner = inner + jnp.sum(chance * grad, axis=0, keepdims=True)
                chances.append(chance)
                grads.append(grad)
            gq = jnp.zeros((HEAD, BLOCK), f32)
            for (kind, k, v, ka), chance, grad, pairs, out in zip(
                parts, chances, grads, sums, outs
            ):
                gl = (chance * (grad - inner)).astype(bf16)
                gk = dot_nn(gl, q) * score_scale
                gv = dot_nn(chance.astype(bf16), go)
                gq = gq + dot_tn(k, gl)
                for more_k, more_v in pairs:
                    gk = gk + more_k[:, lanes]
                    gv = gv + more_v[:, lanes]
                out[0][:, lanes] = gk.astype(out[0].dtype)
                out[1][:, lanes] = gv.astype(out[1].dtype)
            gq_ref[:, lanes] = jnp.transpose(gq * score_scale).astype(bf16)

    keys = BLOCK * len(segments)
    return launch(
        body,
        idx,
        inputs,
        outputs,
        flops=10 * heads * BLOCK * keys * HEAD * 2,
        vmem=20,
        name=name,
    )


def state_update(idx, pieces, write_pieces, state, retain, gain, weights, width, name):
    rows, features = state.shape
    count = len(pieces)
    project = weights is not None

    def body(s, *refs):
        refs = list(refs)
        piece_refs = [refs.pop(0) for unused in range(count)]
        w_refs = [refs.pop(0) for unused in range(count)]
        s_ref, r_ref = refs[:2]
        refs = refs[2:]
        if project:
            g_ref, p_ref, out_ref, n_ref, t_ref = refs
        else:
            (out_ref,) = refs

        @pl.loop(0, rows // TILE)
        def _(i):
            at = span(i * TILE)
            terms = [
                dot_nn(o_ref[at, :], w_ref[: o_ref.shape[1], :])
                for o_ref, w_ref in zip(piece_refs, w_refs)
            ]
            while len(terms) > 1:
                terms = [a + b for a, b in zip(terms[0::2], terms[1::2])]
            update = terms[0]
            keep = r_ref[...]
            following = keep * s_ref[at, :].astype(f32) + (1.0 - keep) * update
            out_ref[at, :] = following
            if project:
                normed = (unit_rows(following)[0] * g_ref[...]).astype(bf16)
                n_ref[at, :] = normed
                t_ref[at, :] = dot_nn(normed, p_ref[:, :width]).astype(bf16)

    inputs = list(pieces) + list(write_pieces) + [state, retain]
    outputs = [shaped((rows, features), f32)]
    if project:
        inputs += [gain, weights]
        outputs += [shaped((rows, features), bf16), shaped((rows, width), bf16)]
    return launch(
        body,
        idx,
        inputs,
        outputs,
        flops=2 * rows * features * (features + (width if project else 0)),
        name=name,
    )


def take_sum(i, s, refs, total):
    chip_ref, mine_ref, theirs_ref = refs
    steps = HALF // TILE
    at, inner = span(tile_start(i, s)), span(lax.rem(i, steps) * TILE)

    @pl.when(i < steps)
    def _():
        total[...] = chip_ref[at, :].astype(f32) + mine_ref[inner, :].astype(f32)

    @pl.when(i >= steps)
    def _():
        total[...] = chip_ref[at, :].astype(f32) + theirs_ref[inner, :].astype(f32)

    return total[...]


def chip_sum(idx, partial, other, name):
    rows, features = partial.shape
    tall = 32

    def body(s, a_ref, b_ref, sum_ref, own_ref):
        @pl.loop(0, rows // tall)
        def _(i):
            at = rows_of(i, 0, tall)
            sum_ref[at, :] = (a_ref[at, :].astype(f32) + b_ref[at, :].astype(f32)).astype(bf16)

        @pl.loop(0, HALF // tall)
        def _(i):
            own_ref[rows_of(i, 0, tall), :] = sum_ref[pl.ds(pl.multiple_of(s[1] * HALF + i * tall, tall), tall), :]

    return launch(
        body,
        idx,
        [partial, other],
        [shaped((rows, features), bf16), shaped((HALF, features), bf16)],
        name=name,
    )


def add_rows(i, ref, value):
    value = jnp.sum(value, axis=0, keepdims=True)

    @pl.when(i == 0)
    def _():
        ref[...] = value

    @pl.when(i != 0)
    def _():
        ref[...] = ref[...] + value


def project_back(idx, grads, weights, column, name):
    rows, width = grads[0].shape
    features = weights.shape[1]

    def body(s, *refs):
        *g_refs, w_ref, out_ref = refs

        @pl.loop(0, rows // TILE)
        def _(i):
            at = span(i * TILE)
            out = jnp.zeros((TILE, features), f32)
            for k, ref in enumerate(g_refs):
                first = column + k * width
                out = out + dot_nn(ref[at, :], w_ref[first : first + width, :])
            out_ref[at, :] = out.astype(bf16)

    return launch(
        body,
        idx,
        list(grads) + [weights],
        [shaped((rows, features), bf16)],
        flops=2 * rows * features * width * len(grads),
        name=name,
    )[0]


def state_back(idx, sums, state, following, retain, gain, write_own, name):
    rows, features = state.shape
    before = write_own is not None
    width = write_own.shape[1] // 2 if before else 10

    def body(s, *refs):
        refs = list(refs)
        total = refs.pop()
        sum_refs = [refs.pop(0) for unused in range(len(sums))]
        s_ref, r_ref, g_ref = refs[:3]
        refs = refs[3:]
        following_ref = refs.pop(0) if following is not None else None
        if before:
            w_ref, gs_ref, gain_ref, gu_ref, gos_ref = refs
        else:
            gs_ref, gain_ref = refs

        @pl.loop(0, rows // TILE)
        def _(i):
            at = span(tile_start(i, s))
            up = take_sum(i, s, sum_refs, total)
            unit, inverse = unit_rows(s_ref[at, :].astype(f32))
            out = unit_back(up, unit, inverse, g_ref[...])
            if following is not None:
                out = r_ref[...] * following_ref[at, :] + out
            gs_ref[at, :] = out
            add_rows(i, gain_ref, up * unit)
            if before:
                gu = ((1.0 - r_ref[...]) * out).astype(bf16)
                gu_ref[at, :] = gu
                gos_ref[at, :] = dot_nn(gu, w_ref[:, :width]).astype(bf16)

    inputs = list(sums) + [state, retain, gain]
    outputs = [shaped((rows, features), f32), shaped((1, features), f32)]
    if following is not None:
        inputs.append(following)
    if before:
        inputs.append(write_own)
        outputs += [shaped((rows, features), bf16), shaped((rows, width), bf16)]
    return launch(
        body,
        idx,
        inputs,
        outputs,
        scratch=[pltpu.VMEM((TILE, features), f32)],
        flops=2 * rows * features * width,
        name=name,
    )


def last_update_back(idx, retain, write_own, rows, name):
    features, width = write_own.shape[0], write_own.shape[1] // 2

    def body(s, r_ref, w_ref, gu_ref, gos_ref):
        gu = ((1.0 - r_ref[...]) * jnp.zeros((rows, features), f32)).astype(bf16)
        gu_ref[...] = gu
        gos_ref[...] = dot_nn(gu, w_ref[:, :width]).astype(bf16)

    return launch(
        body,
        idx,
        [retain, write_own],
        [shaped((rows, features), bf16), shaped((rows, width), bf16)],
        name=name,
    )


def gelu_both(a):
    root, cubic = 0.7978845608028654, 0.044715
    squared = a * a
    bent = jnp.tanh(root * (a + cubic * (squared * a)))
    rising = 0.5 * (1.0 + bent)
    slope = rising + (0.5 * root) * a * (1.0 - bent * bent) * (1.0 + (3.0 * cubic) * squared)
    return a * rising, slope


def output_forward(idx, number, pieces, out_pieces, tokens, gain, name):
    features = tokens.shape[1]
    count = len(pieces)

    def body(s, *refs):
        o_refs, w_refs = refs[:count], refs[count : 2 * count]
        t_ref, g_ref, x1_ref, xn_ref = refs[2 * count :]

        @pl.loop(0, BLOCK // TILE)
        def _(i):
            at = span(i * TILE)
            x1 = t_ref[span(i * TILE, number * BLOCK), :].astype(f32)
            for o_ref, w_ref in zip(o_refs, w_refs):
                x1 = x1 + dot_nn(o_ref[at, :], w_ref[o_ref.shape[1] :, :])
            x1_ref[at, :] = x1
            xn_ref[at, :] = (unit_rows(x1)[0] * g_ref[...]).astype(bf16)

    return launch(
        body,
        idx,
        list(pieces) + list(out_pieces) + [tokens, gain],
        [shaped((BLOCK, features), f32), shaped((BLOCK, features), bf16)],
        flops=2 * BLOCK * features * features,
        name=name,
    )


def dense_forward(idx, normed, dense, name):
    features = normed.shape[1]
    hidden = dense[1].shape[0]

    def body(s, n_ref, up_ref, down_ref, h_ref, slope_ref, part_ref):
        @pl.loop(0, BLOCK // TILE)
        def _(i):
            at = span(i * TILE)
            h, slope = gelu_both(dot_nn(n_ref[at, :], up_ref[:, :hidden]))
            h = h.astype(bf16)
            h_ref[at, :] = h
            slope_ref[at, :] = slope.astype(bf16)
            part_ref[at, :] = dot_nn(h, down_ref[...]).astype(bf16)

    return launch(
        body,
        idx,
        [normed, *dense],
        [
            shaped((BLOCK, hidden), bf16),
            shaped((BLOCK, hidden), bf16),
            shaped((BLOCK, features), bf16),
        ],
        flops=4 * BLOCK * features * hidden,
        name=name,
    )


def dense_backward(idx, number, sums, x1, teacher, katt, slope, dense, name):
    features = x1.shape[1]
    up_t, both = dense
    hidden = up_t.shape[0]

    def body(s, *refs):
        refs = list(refs)
        total = refs.pop()
        sum_refs = [refs.pop(0) for unused in range(len(sums))]
        x_ref, t_ref, v_ref, slope_ref, up_ref, d_ref = refs[:6]
        gy_ref, gm_ref, ga_ref, loss_ref, part_ref = refs[6:]

        @pl.loop(0, BLOCK // TILE)
        def _(i):
            start = tile_start(i, s)
            at, far = span(start), span(start, number * BLOCK)
            errors = x_ref[at, :] + take_sum(i, s, sum_refs, total) - t_ref[far, :].astype(f32)
            gy = v_ref[far, 2:3] * errors
            gy_ref[at, :] = gy
            add_rows(i, loss_ref, gy * errors)
            gm = gy.astype(bf16)
            gm_ref[at, :] = gm
            ga = (dot_nn(gm, d_ref[:, hidden:]) * slope_ref[at, :].astype(f32)).astype(bf16)
            ga_ref[at, :] = ga
            part_ref[at, :] = dot_nn(ga, up_ref[...]).astype(bf16)

    return launch(
        body,
        idx,
        list(sums) + [x1, teacher, katt, slope, up_t, both],
        [
            shaped((BLOCK, features), f32),
            shaped((BLOCK, features), bf16),
            shaped((BLOCK, hidden), bf16),
            shaped((1, features), f32),
            shaped((BLOCK, features), bf16),
        ],
        scratch=[pltpu.VMEM((TILE, features), f32)],
        flops=4 * BLOCK * features * hidden,
        name=name,
    )


def output_backward(idx, sums, gy, x1, gain, out_own, name):
    features = x1.shape[1]
    width = out_own.shape[1] // 2

    def body(s, *refs):
        refs = list(refs)
        total = refs.pop()
        sum_refs = [refs.pop(0) for unused in range(len(sums))]
        gy_ref, x_ref, g_ref, w_ref, gx_ref, gp_ref, go_ref, gain_ref = refs

        @pl.loop(0, BLOCK // TILE)
        def _(i):
            at = span(tile_start(i, s))
            up = take_sum(i, s, sum_refs, total)
            unit, inverse = unit_rows(x_ref[at, :])
            gx = gy_ref[at, :] + unit_back(up, unit, inverse, g_ref[...])
            gx_ref[at, :] = gx
            gp = gx.astype(bf16)
            gp_ref[at, :] = gp
            go_ref[at, :] = dot_nn(gp, w_ref[:, width:]).astype(bf16)
            add_rows(i, gain_ref, up * unit)

    return launch(
        body,
        idx,
        list(sums) + [gy, x1, gain, out_own],
        [
            shaped((BLOCK, features), f32),
            shaped((BLOCK, features), bf16),
            shaped((BLOCK, width), bf16),
            shaped((1, features), f32),
        ],
        scratch=[pltpu.VMEM((TILE, features), f32)],
        flops=2 * BLOCK * features * width,
        name=name,
    )


def weight_grads(idx, groups, name):
    features = groups[0][0][0].shape[1]
    inputs, specs, total, flops = [], [], 0, 0
    for parts in groups:
        for left, block, right in parts:
            rows = right.shape[0]
            inputs += [left, right]
            specs.append(pl.BlockSpec((rows, HALF), lambda i, block=block: (block, i)))
            specs.append(
                pl.BlockSpec(right.shape, lambda i: (0, 0), pipeline_mode=pl.Buffered(1))
            )
            flops += 2 * rows * features * right.shape[1]
        total += parts[0][2].shape[1]

    def body(s, *refs):
        refs = list(refs)
        out_ref = refs.pop()
        at = 0
        for parts in groups:
            size = parts[0][2].shape[1]
            out = jnp.zeros((HALF, size), f32)
            for unused in parts:
                left, right = refs.pop(0), refs.pop(0)
                out = out + dot_tn(left[...], right[...])
            out_ref[:, at : at + size] = out.astype(bf16)
            at += size

    return pl.pallas_call(
        body,
        grid=(features // HALF,),
        in_specs=[pl.BlockSpec(memory_space=pltpu.SMEM)] + specs,
        out_specs=pl.BlockSpec((HALF, total), lambda i: (i, 0)),
        out_shape=pltpu.HBM((features, total), bf16),
        compiler_params=pltpu.CompilerParams(
            dimension_semantics=("arbitrary",), vmem_limit_bytes=20 << 20
        ),
        cost_estimate=cost(flops, inputs),
        name=name,
    )(idx, *inputs)


def unpack_grads(packed, widths, flipped, name):
    rows = packed.shape[0]

    def body(p_ref, *out_refs):
        at = 0
        for size, flip, out_ref in zip(widths, flipped, out_refs):
            values = p_ref[:, at : at + size].astype(f32)
            out_ref[...] = jnp.transpose(values) if flip else values
            at += size

    return pl.pallas_call(
        body,
        in_specs=[pl.BlockSpec(memory_space=pltpu.VMEM)],
        out_specs=[pl.BlockSpec(memory_space=pltpu.VMEM)] * len(widths),
        out_shape=[
            shaped((size, rows) if flip else (rows, size), f32)
            for size, flip in zip(widths, flipped)
        ],
        compiler_params=pltpu.CompilerParams(vmem_limit_bytes=8 << 20),
        cost_estimate=cost(0, [packed]),
        name=name,
    )(packed)


def arrange_rows(idx, pieces, count, name):
    rows, features = pieces[0].shape
    rows = rows // count

    def body(s, *refs):
        ins, outs = refs[: len(pieces)], refs[len(pieces) :]
        for k, ref in enumerate(ins):
            for j, out_ref in enumerate(outs):
                out_ref[rows_of(s[0] ^ k, 0, rows), :] = ref[j * rows : (j + 1) * rows, :]

    return launch(
        body,
        idx,
        pieces,
        [shaped((rows * len(pieces), features), pieces[0].dtype)] * count,
        name=name,
    )


def turn(idx, values, first, count, name):
    rows = values.shape[0]
    wide = 256

    def body(s, v_ref, out_ref):
        @pl.loop(0, count // wide)
        def _(i):
            lanes = pl.ds(pl.multiple_of(first + i * wide, HEAD), wide)
            out_ref[rows_of(i, 0, wide), :] = jnp.transpose(v_ref[:, lanes])

    return launch(body, idx, [values], [shaped((count, rows), values.dtype)], name=name)[0]


def arrange_columns(idx, blocks, across, name):
    rows, width = blocks[0].shape
    depth = len(blocks)

    def body(s, *refs):
        out_ref = refs[-1]
        for k in range(depth):
            level = lax.rem(s[3] + depth - k, depth)
            out_ref[rows_of(2 * level + s[4], 0, rows), :] = refs[k][...]
            out_ref[rows_of(2 * level + 1 - s[4], 0, rows), :] = refs[depth + k][...]

    return launch(
        body,
        idx,
        list(blocks) + list(across),
        [shaped((2 * depth * rows, width), blocks[0].dtype)],
        name=name,
    )[0]


def split_grads(idx, groups, depth, name):
    features = groups[0][0][0].shape[1]
    rows = features // (2 * depth)
    total = sum(parts[0][2].shape[1] for parts in groups)
    inputs = []

    def place(array):
        for k, known in enumerate(inputs):
            if known is array:
                return k
        inputs.append(array)
        return len(inputs) - 1

    uses = [[(place(a), block, place(c)) for a, block, c in parts] for parts in groups]

    def body(s, *refs):
        *ins, theirs_ref, mine_ref, held = refs

        @pl.loop(0, depth)
        def _(i):
            lanes = pl.ds(pl.multiple_of(i * 2 * rows, 2 * rows), 2 * rows)
            at = 0
            for parts in uses:
                size = ins[parts[0][2]].shape[1]
                out = jnp.zeros((2 * rows, size), f32)
                for left, block, right in parts:
                    count = ins[right].shape[0]
                    tall = slice(block * count, (block + 1) * count)
                    out = out + dot_tn(ins[left][tall, lanes], ins[right][...])
                held[:, at : at + size] = out.astype(bf16)
                at += size
            mine_ref[rows_of(i, 0, rows), :] = held[rows_of(s[4], 0, rows), :]
            theirs_ref[rows_of(i, 0, rows), :] = held[rows_of(1 - s[4], 0, rows), :]

    return launch(
        body,
        idx,
        inputs,
        [shaped((depth * rows, total), bf16)] * 2,
        scratch=[pltpu.VMEM((2 * rows, total), bf16)],
        name=name,
    )


def pair_blocks(idx, mine, got, depth, name):
    rows, width = mine.shape[0] // depth, mine.shape[1]

    def body(s, mine_ref, got_ref, *out_refs):
        for k, ref in enumerate(out_refs):
            at = rows_of(lax.rem(s[3] + k, depth), 0, rows)
            ref[...] = (mine_ref[at, :].astype(f32) + got_ref[at, :].astype(f32)).astype(ref.dtype)

    return launch(
        body,
        idx,
        [mine, got],
        [shaped((rows, width), f32)] + [shaped((rows, width), bf16)] * (depth - 1),
        name=name,
    )


def line_sum(idx, own, others, widths, flipped, name):
    rows = own.shape[0]

    def body(s, own_ref, *refs):
        ins, outs = refs[: len(others)], refs[len(others) :]
        total = own_ref[...]
        for ref in ins:
            total = total + ref[...].astype(f32)
        at = 0
        for size, flip, out_ref in zip(widths, flipped, outs):
            values = total[:, at : at + size]
            out_ref[...] = jnp.transpose(values) if flip else values
            at += size

    return launch(
        body,
        idx,
        [own] + list(others),
        [
            shaped((size, rows) if flip else (rows, size), f32)
            for size, flip in zip(widths, flipped)
        ],
        name=name,
    )


def pack(idx, arrays, takes, shapes, name):
    flipped = [take for take in takes if take[-1]]

    def body(s, *refs):
        ins, outs = refs[: len(arrays)], refs[len(arrays) : len(arrays) + len(shapes)]
        *held, sems = refs[len(arrays) + len(shapes) :]
        copies, spare = [], list(held)
        for j, (k, row, col, rows, cols, out, place, flip) in enumerate(takes):
            at = pl.ds(0, rows) if row is None else rows_of(s[row], 0, rows)
            to = pl.ds(0, cols) if col is None else rows_of(s[col], 0, cols)
            if flip:
                target = spare.pop(0)
            else:
                target = outs[out].at[pl.ds(place[0], rows), pl.ds(place[1], cols)]
            copies.append(pltpu.make_async_copy(ins[k].at[at, to], target, sems.at[j]))
            copies[-1].start()
        spare = list(held)
        for copy, (k, row, col, rows, cols, out, place, flip) in zip(copies, takes):
            copy.wait()
            if flip:
                to = slice(place[1], place[1] + rows)
                outs[out][place[0] : place[0] + cols, to] = jnp.transpose(spare.pop(0)[...])

    return pl.pallas_call(
        body,
        in_specs=[pl.BlockSpec(memory_space=pltpu.SMEM)]
        + [pl.BlockSpec(memory_space=pl.ANY)] * len(arrays),
        out_specs=[pl.BlockSpec(memory_space=pltpu.VMEM)] * len(shapes),
        out_shape=[shaped(a, bf16) for a in shapes],
        scratch_shapes=[pltpu.VMEM((take[3], take[4]), bf16) for take in flipped]
        + [pltpu.SemaphoreType.DMA((len(takes),))],
        compiler_params=pltpu.CompilerParams(vmem_limit_bytes=8 << 20),
        cost_estimate=cost(0, arrays),
        name=name,
    )(idx, *[pltpu.with_memory_space_constraint(a, pltpu.HBM) for a in arrays])


def input_rows(idx, own, arrived, gx1s, tokens, gain, name):
    rows, features = tokens.shape
    count = len(gx1s)

    def body(s, *refs):
        own_refs, far_refs, gx_refs = refs[:count], refs[count : 2 * count], refs[2 * count : 3 * count]
        t_ref, g_ref, out_ref, gain_ref = refs[3 * count :]
        unit, inverse = unit_rows(t_ref[...].astype(f32))
        for b in range(count):

            @pl.when(s[2] // 2 == b)
            def _():
                at = rows_of(s[1])
                up = own_refs[b][at, :].astype(f32) + far_refs[b][...].astype(f32)
                base = gx_refs[b][rows_of(s[1]), :]
                out_ref[...] = base + unit_back(up, unit, inverse, g_ref[...])
                gain_ref[...] = jnp.sum(up * unit, axis=0, keepdims=True)

    return launch(
        body,
        idx,
        list(own) + list(arrived) + list(gx1s) + [tokens, gain],
        [shaped((rows, features), f32), shaped((1, features), f32)],
        name=name,
    )


def per_device(
    block_input,
    state_start,
    teacher,
    valid_mask,
    segment,
    image_offset,
    retain,
    to_query,
    to_key,
    to_value,
    to_output,
    to_hidden,
    to_model,
    state_query,
    state_key,
    state_value,
    state_write,
    first_gain,
    second_gain,
    state_gain,
):
    row_devices = lax.axis_size("row")
    col_devices = lax.axis_size("col")
    row_index = lax.axis_index("row")
    col_index = lax.axis_index("col")
    local_rows, features = block_input.shape[1:]
    length = local_rows * row_devices
    width = to_query.shape[1]
    heads = width // HEAD
    hidden = to_hidden.shape[1] // row_devices
    nblocks = length // BLOCK
    pairs = row_devices == 4 and 2 * local_rows == BLOCK
    lines = pairs and col_devices == 8
    core_pairs = [(k, k ^ 1) for k in range(row_devices)]
    chip_pairs = [(k, k ^ 2) for k in range(row_devices)] if pairs else None
    if pairs:
        idx = jnp.stack([row_index, row_index % 2, row_index, col_index // 2, col_index % 2])
    else:
        idx = jnp.stack([0, 1, row_index, 0, 0])
    idx = idx.astype(jnp.int32)

    def to_core(x):
        return lax.ppermute(x, "row", core_pairs)

    def to_chip(x):
        return lax.ppermute(x, "row", chip_pairs)

    def row_moves(x):
        if not pairs:
            stacked = lax.all_gather(x, "row", axis=0, tiled=False)
            return [stacked[k] for k in range(row_devices)]
        return [x, to_core(x), to_chip(x)]

    def row_pieces(moved, *ties):
        if not pairs:
            return moved
        x, near, far = moved
        return [x, near, far, to_core(after(far, *ties))]

    depth_z = col_devices // 2

    def along(v, step):
        levels = range(depth_z)
        moves = [(2 * z + y, 2 * ((z + step) % depth_z) + y) for z in levels for y in range(2)]
        return lax.ppermute(v, "col", moves)

    def across(v):
        return lax.ppermute(v, "col", [(k, k ^ 1) for k in range(col_devices)])

    class Columns:
        def __init__(self, x, name):
            self.name = name
            if lines:
                self.blocks = [x] + [along(x, k) for k in range(1, depth_z)]
                self.crossed = [across(x)]
            else:
                self.whole = lax.all_gather(x, "col", axis=0, tiled=True)

        def cross(self, k, *ties):
            if lines:
                self.crossed.append(across(after(self.blocks[k], *ties)))

        def landed(self, k):
            return [self.blocks[k], self.crossed[k - 1]] if lines else []

        def result(self, *ties):
            if lines:
                order = after(idx, *ties)
                return arrange_columns(order, self.blocks, self.crossed, self.name)
            return self.whole

    class Scattered:
        def __init__(self, groups, name, *ties):
            self.name, self.widths = name, [parts[0][2].shape[1] for parts in groups]
            if lines:
                order = after(idx, *ties) if ties else idx
                theirs, self.mine = split_grads(order, groups, depth_z, name)
                self.got = across(theirs)
            else:
                packed = weight_grads(idx, groups, name)
                self.whole = lax.psum_scatter(packed, "col", scatter_dimension=0, tiled=True)

        def send(self, *ties):
            if lines:
                mine = after(self.mine, *ties) if ties else self.mine
                self.own, *blocks = pair_blocks(idx, mine, self.got, depth_z, f"{self.name}_y")
                self.far = [along(block, k + 1) for k, block in enumerate(blocks)]

        def result(self, flipped):
            if lines:
                return line_sum(idx, self.own, self.far, self.widths, flipped, f"{self.name}_z")
            return unpack_grads(self.whole, self.widths, flipped, f"{self.name}_z")

    class RowSum:
        def __init__(self, partial, name, receiver=None, ties=()):
            if pairs:
                order = after(idx, *ties) if ties else idx
                self.chip, own = chip_sum(order, partial, to_core(partial), name)
                moves = [m for m in chip_pairs if receiver is None or m[1] // 2 == receiver]
                self.far = lax.ppermute(own, "row", moves)
            else:
                self.chip = lax.psum(partial, "row")

        def result(self, *ties):
            if pairs:
                return [self.chip, self.far, to_core(after(self.far, *ties))]
            none = jnp.zeros((HALF, features), bf16)
            return [self.chip, none, none]

    def all_sum(x):
        for axis, size in (("row", row_devices), ("col", col_devices)):
            step = 1
            while step < size:
                x = x + lax.ppermute(x, axis, [(k, k ^ step) for k in range(size)])
                step *= 2
        return x

    depth = to_query.shape[0]
    (near,) = pack(
        idx,
        [state_query, state_key, state_value, to_query, to_key, to_value],
        [(k, None, None, depth, width, 0, (0, k * width), False) for k in range(6)],
        [(depth, 6 * width)],
        "pack_near",
    )
    near = lax.all_gather(near, "col", axis=0, tiled=True)
    rows_in, mid, far_weights = pack(
        idx,
        [state_write, to_output, to_hidden, to_model, block_input[0], teacher[0]],
        [
            (4, None, None, local_rows, features, 0, (0, 0), False),
            (5, None, None, local_rows, features, 0, (local_rows, 0), False),
            (0, 2, None, width, depth, 1, (0, 0), True),
            (1, None, None, width, depth, 1, (0, width), True),
            (2, None, 2, depth, hidden, 2, (0, 0), False),
            (3, 2, None, hidden, depth, 2, (0, hidden), True),
        ],
        [(2 * local_rows, features), (depth, 2 * width), (depth, 2 * hidden)],
        "pack_rest",
    )
    rows_moved = row_moves(rows_in) if pairs else None
    mid = Columns(mid, "mid")
    for k in range(1, depth_z):
        mid.cross(k)
    mid = mid.result()
    mid_n = turn(idx, mid, 0, 2 * width, "mid_turn")
    held = [mid_n] + (rows_moved[2:] if pairs else [])
    dense = lax.all_gather(after(far_weights, *held), "col", axis=0, tiled=True)
    mid_moved = row_moves(mid_n)
    if pairs:
        tokens, teacher_all = arrange_rows(idx, row_pieces(rows_moved), 2, "tokens")
    else:
        tokens, teacher_all = [
            lax.all_gather(x[0], "row", axis=0, tiled=True) for x in (block_input, teacher)
        ]

    valid_row = lax.dynamic_index_in_dim(valid_mask, col_index, 0, keepdims=False)
    segment_row = segment[0]
    numbers = jnp.arange(nblocks, dtype=jnp.int32)
    places = jnp.arange(length, dtype=jnp.int32)
    starts = numbers * BLOCK + image_offset[0]
    inside = (places[:, None] >= starts[None, :]) & (places[:, None] < starts[None, :] + PIECE)
    piece = jnp.sum(jnp.where(inside, numbers[None, :] + 1, 0), axis=1) - 1
    valid_count = jnp.sum(valid_mask.astype(f32))
    total_tokens = f32(length * col_devices)
    weight_of_row = total_tokens / valid_count * valid_row.astype(f32)
    document = segment_row.astype(f32)
    nothing = jnp.zeros_like(document)
    katt = jnp.stack(
        [jnp.where(valid_row > 0, document, -1.0), piece.astype(f32), weight_of_row, nothing],
        axis=1,
    )
    qatt = jnp.stack(
        [document, jnp.where(piece >= 0, piece, -2).astype(f32), nothing, nothing], axis=0
    )
    retain2 = retain[None]
    first_gain2, second_gain2, state_gain2 = first_gain[None], second_gain[None], state_gain[None]

    def token_segments(number, trio):
        found = []
        if number > 0:
            found.append(("prev", token_heads, number - 1, width, 2 * width, number - 1))
        found.append(("own", token_heads, number, width, 2 * width, number))
        found.append(("free", trio, 0, width, 2 * width, None))
        return found

    def state_segments(number, trio):
        return [
            ("valid", token_heads, number, width, 2 * width, number),
            ("free", trio, 0, width, 2 * width, None),
        ]

    current = state_start[0]
    near_t = turn(idx, near, 0, 6 * width, "near_turn")
    state_low, trio = norm_project(after(idx, near_t), current, state_gain2, near, 0, 3 * width, "state_proj")
    first_low, token_heads = norm_project(
        idx, tokens, first_gain2, near, 3 * width, 3 * width, "token_proj"
    )
    states, lows, trios = [], [], []
    state_out, state_logs, token_out, token_logs = [], [], [], []
    x1s, second_lows, hiddens, slopes, dense_sums = [], [], [], [], []
    state_pieces, token_pieces = [], []
    end = nblocks - 1

    def state_part(b):
        mixed, logs = attend(
            idx,
            (trios[b], 0, 0),
            state_segments(b, trios[b]),
            katt,
            None,
            heads,
            f"state_attend{b}",
        )
        state_out.append(mixed)
        state_logs.append(logs)
        state_pieces.append(row_moves(mixed) if b < nblocks - 1 else None)

    for b in range(nblocks):
        states.append(current)
        lows.append(state_low)
        trios.append(trio)
        last = b + 1 == nblocks
        if not last:
            state_part(b)
        mixed, logs = attend(
            idx, (token_heads, b, 0), token_segments(b, trio), katt, qatt, heads, f"token_attend{b}"
        )
        if b == 0:
            mid_pieces = row_pieces(mid_moved, mixed)
        token_out.append(mixed)
        token_logs.append(logs)
        token_pieces.append(row_moves(mixed))
        if not last:
            current, state_low, trio = state_update(
                idx,
                row_pieces(state_pieces[b], mixed),
                mid_pieces,
                current,
                retain2,
                state_gain2,
                near,
                3 * width,
                f"update{b}",
            )
            token_pieces[b] = row_pieces(token_pieces[b], trio)
    state_part(nblocks - 1)
    token_pieces[-1] = row_pieces(token_pieces[-1], state_out[-1])

    gus = [None] * nblocks
    gms, gas, losses, gx1s, gps, gos, second_sums = [], [], [], [], [], [], []
    gys, second_back = [], []
    for b in range(nblocks):
        x1, low = output_forward(
            idx, b, token_pieces[b], mid_pieces, tokens, second_gain2, f"out{b}"
        )
        x1s.append(x1)
        second_lows.append(low)
    down = turn(after(idx, state_out[-1], *second_lows), dense, hidden, hidden, "down_turn")
    order = idx
    for b in range(nblocks):
        h, slope, partial = dense_forward(order, second_lows[b], (dense, down), f"dense{b}")
        hiddens.append(h)
        slopes.append(slope)
        ties = []
        if b == end:
            up_t = turn(after(idx, h), dense, 0, hidden, "up_turn")
            ties.append(up_t)
        dense_sums.append(RowSum(partial, f"dense_sum{b}", ties=ties))
        order = after(idx, dense_sums[b].chip)

    def state_back_part(b, gos_state, own, free, dtype):
        return attend_back(
            idx,
            (trios[b], 0, 0),
            state_segments(b, trios[b]),
            katt,
            None,
            heads,
            state_logs[b],
            gos_state,
            [own, free],
            [dtype, dtype],
            f"state_back{b}",
        )

    def token_back_part(b, own, free, dtype, upstream):
        segments = token_segments(b, trios[b])
        added = ([[]] if b > 0 else []) + [own, free]
        dtypes = ([f32] if b > 0 else []) + [dtype, dtype]
        found = attend_back(
            idx,
            (token_heads, b, 0),
            segments,
            katt,
            qatt,
            heads,
            token_logs[b],
            upstream,
            added,
            dtypes,
            f"token_back{b}",
        )
        return found[0], found[-4:], (found[1], found[2]) if b > 0 else None

    late_mid = after(mid, dense_sums[end].chip)
    gus[end], gos_state = last_update_back(idx, retain2, late_mid, NS, "last_back")
    state_found = state_back_part(end, gos_state, [], [], f32)
    ready = teacher_all
    for b in range(nblocks):
        hides = [hiddens[end]] if b == 0 else [gys[b - 1], state_found[0]]
        gy, gm, ga, loss, partial = dense_backward(
            idx, b, dense_sums[b].result(*hides), x1s[b], ready, katt, slopes[b], (up_t, dense), f"back{b}"
        )
        gms.append(gm)
        gas.append(ga)
        losses.append(loss)
        gys.append(gy)
        if b < end:
            second_back.append(RowSum(partial, f"back_sum{b}"))
            ready = after(teacher_all, second_back[b].chip)
    dense_grads = weight_grads(
        idx,
        [
            [(low, 0, ga) for low, ga in zip(second_lows, gas)],
            [(gm, 0, h) for gm, h in zip(gms, hiddens)],
        ],
        "dense_grads",
    )
    filled = [dense_grads]
    ties = [dense_grads] + [back.far for back in second_back] if pairs else []
    second_back.append(RowSum(partial, f"back_sum{end}", ties=ties))
    dense_grads = lax.psum_scatter(dense_grads, "col", scatter_dimension=0, tiled=True)

    token_found = [None] * nblocks
    for b in range(nblocks):
        gx1, gp, go, gain_sum = output_backward(
            idx,
            second_back[b].result(*(filled if b == end else [gys[end]])),
            gys[b],
            x1s[b],
            second_gain2,
            mid,
            f"out_back{b}",
        )
        gx1s.append(gx1)
        gps.append(gp)
        gos.append(go)
        second_sums.append(gain_sum)
        if b < end:
            token_found[b] = token_back_part(b, [], [], f32, go)
            filled.append(token_found[b][0])
    trio_grads = [None] * nblocks
    token_grads = [None] * nblocks
    first_sums = [None] * nblocks
    gain_sums = []
    grad_next = None
    gqs, gk, gv, gks, gvs = state_found
    gq, (gk, gv, gks, gvs), key_part = token_back_part(
        end, [(gk, gv)], [(gks, gvs)], bf16, gos[end]
    )
    state_pieces[-1] = row_moves(after(state_out[-1], gos[end]))
    gqs = after(gqs, state_pieces[-1][2])
    trio_grads[end] = (gqs, gks, gvs)
    token_grads[end] = (gq, gk, gv)
    for b in reversed(range(nblocks)):
        order = idx
        if b == 0:

            def state_group(k):
                return [(lows[c], 0, trio_grads[c][k]) for c in range(nblocks)]

            def token_group(k):
                return [(first_low, c, token_grads[c][k]) for c in range(nblocks)]

            write_group = [(gu, 0, out) for gu, out in zip(gus, state_out)]
            late_grads = weight_grads(
                idx,
                [state_group(k) for k in range(3)]
                + [token_group(k) for k in range(3)]
                + [[(gp, 0, out) for gp, out in zip(gps, token_out)], write_group],
                "late_grads",
            )
            order = after(idx, late_grads)
            late_grads = lax.psum_scatter(late_grads, "col", scatter_dimension=0, tiled=True)
        trio_sum = RowSum(
            project_back(order, trio_grads[b], near_t, 0, f"trio_back{b}"),
            f"trio_sum{b}",
        )
        hides = []
        if b == end:
            (final_state,) = state_update(
                idx,
                row_pieces(state_pieces[-1], gq),
                mid_pieces,
                current,
                retain2,
                None,
                None,
                0,
                "update_last",
            )
            hides.append(final_state)
        first_sums[b] = project_back(idx, token_grads[b], near_t, 3 * width, f"first_back{b}")
        hides.append(first_sums[b])
        first_sums[b] = RowSum(first_sums[b], f"first_sum{b}", b) if pairs else first_sums[b]
        if b > 0:
            grad_next, gain_sum, gus[b - 1], gos_state = state_back(
                idx,
                trio_sum.result(*hides),
                states[b],
                grad_next,
                retain2,
                state_gain2,
                mid,
                f"chain_back{b}",
            )
            gq, (gk, gv, gks, gvs), next_part = token_found[b - 1]
            gqs, gk, gv, gks, gvs = state_back_part(
                b - 1, gos_state, [(gk, gv), key_part], [(gks, gvs)], bf16
            )
            key_part = next_part
            trio_grads[b - 1] = (gqs, gks, gvs)
            token_grads[b - 1] = (gq, gk, gv)
        else:
            grad_next, gain_sum = state_back(
                idx,
                trio_sum.result(*hides),
                states[b],
                grad_next,
                retain2,
                state_gain2,
                None,
                "chain_back0",
            )
        gain_sums.append(gain_sum)

    if pairs:
        own_rows = [first.chip for first in first_sums]
        arrived = [first.far for first in first_sums]
        input_grad, first_sum = input_rows(
            idx, own_rows, arrived, gx1s, block_input[0], first_gain2, "input_rows"
        )
        first_sum = first_sum[0]
    else:
        both = jnp.concatenate(first_sums)
        grad_first = lax.psum_scatter(both, "row", scatter_dimension=0, tiled=True).astype(f32)
        own_gx1 = lax.dynamic_slice_in_dim(
            jnp.concatenate(gx1s), row_index * local_rows, local_rows
        )
        unit, inverse = unit_rows(block_input[0].astype(f32))
        input_grad = own_gx1 + unit_back(grad_first, unit, inverse, first_gain2)
        first_sum = jnp.sum(grad_first * unit, axis=0)

    share = 1.0 / row_devices
    summed = all_sum(
        jnp.stack(
            [
                sum(losses)[0] * share,
                first_sum,
                sum(second_sums)[0] * share,
                sum(gain_sums)[0] * share,
            ]
        )
    )
    total_loss = jnp.sum(summed[0]) / (2.0 * total_tokens)

    upper_grad, lower_grad = unpack_grads(
        dense_grads, [hidden, hidden], [False, True], "unpack_dense"
    )
    late = unpack_grads(late_grads, [width] * 8, [False] * 6 + [True] * 2, "unpack_late")

    return (
        total_loss,
        final_state[None],
        input_grad[None],
        grad_next[None],
        late[3],
        late[4],
        late[5],
        late[6],
        upper_grad,
        lower_grad,
        late[0],
        late[1],
        late[2],
        late[7],
        summed[1],
        summed[2],
        summed[3],
    )


def solution(mesh):
    in_specs = (
        P("col", "row", None),
        P("col", None, None),
        P("col", "row", None),
        P(),
        P("col", None),
        P("col", None),
        P(),
        P("col", "row"),
        P("col", "row"),
        P("col", "row"),
        P("row", "col"),
        P("col", None),
        P(None, "col"),
        P("col", "row"),
        P("col", "row"),
        P("col", "row"),
        P(None, "col"),
        P(),
        P(),
        P(),
    )
    out_specs = (
        P(),
        P("col", None, None),
        P("col", "row", None),
        P("col", None, None),
        P("col", "row"),
        P("col", "row"),
        P("col", "row"),
        P("row", "col"),
        P("col", "row"),
        P("row", "col"),
        P("col", "row"),
        P("col", "row"),
        P("col", "row"),
        P("row", "col"),
        P(),
        P(),
        P(),
    )
    return jax.shard_map(
        per_device, mesh=mesh, in_specs=in_specs, out_specs=out_specs, check_vma=False
    )
```

```python
import functools

import jax
import jax.numpy as jnp
from jax import lax
from jax.experimental import pallas as pl
from jax.experimental.pallas import tpu as pltpu
from jax.sharding import PartitionSpec as P

HEAD = 128
BLOCK = 512
HALF = 256
NS = 512
PIECE = 256
COST = 8
TILE = 256

epsilon = 1e-06
masked_value = -1e30
score_scale = HEAD ** (-0.5)
log2_scale = score_scale * 1.4426950408889634
f32 = jnp.float32
bf16 = jnp.bfloat16


def dot_nn(a, b):
    return lax.dot_general(a, b, (((1,), (0,)), ((), ())), preferred_element_type=f32)


def dot_nt(a, b):
    return lax.dot_general(a, b, (((1,), (1,)), ((), ())), preferred_element_type=f32)


def dot_tn(a, b):
    return lax.dot_general(a, b, (((0,), (0,)), ((), ())), preferred_element_type=f32)


def cost(flops, arrays):
    return pl.CostEstimate(flops=flops // COST, bytes_accessed=1024, transcendentals=0)


def after(x, *earlier):
    return lax.optimization_barrier((x,) + earlier)[0]


def shaped(shape, dtype):
    return jax.ShapeDtypeStruct(shape, dtype)


def launch(body, idx, inputs, outputs, scratch=(), flops=0, vmem=12, name=None):
    return pl.pallas_call(
        body,
        in_specs=[pl.BlockSpec(memory_space=pltpu.SMEM)]
        + [pl.BlockSpec(memory_space=pltpu.VMEM)] * len(inputs),
        out_specs=[pl.BlockSpec(memory_space=pltpu.VMEM)] * len(outputs),
        out_shape=list(outputs),
        scratch_shapes=list(scratch),
        compiler_params=pltpu.CompilerParams(vmem_limit_bytes=vmem << 20),
        cost_estimate=cost(flops, inputs),
        name=name,
    )(idx, *inputs)


def rows_of(i, base=0, size=HALF):
    return pl.ds(pl.multiple_of(base + i * size, size), size)


def tile_start(i, s):
    steps = HALF // TILE
    return lax.rem(i // steps + s[1], 2) * HALF + lax.rem(i, steps) * TILE


def span(start, base=0):
    return pl.ds(pl.multiple_of(base + start, TILE), TILE)


def unit_rows(x):
    inverse = lax.rsqrt(jnp.mean(x * x, axis=-1, keepdims=True) + epsilon)
    return x * inverse, inverse


def unit_back(up, unit, inverse, gain):
    scaled = up * gain
    inner = jnp.mean(scaled * unit, axis=-1, keepdims=True)
    return inverse * (scaled - unit * inner)


def norm_project(idx, values, gain, weights, column, width, name):
    rows, features = values.shape

    def body(s, x_ref, g_ref, w_ref, n_ref, p_ref):
        @pl.loop(0, rows // TILE)
        def _(i):
            at = span(i * TILE)
            unit, unused = unit_rows(x_ref[at, :].astype(f32))
            normed = (unit * g_ref[...]).astype(bf16)
            n_ref[at, :] = normed
            p_ref[at, :] = dot_nn(normed, w_ref[:, column : column + width]).astype(bf16)

    return launch(
        body,
        idx,
        [values, gain, weights],
        [shaped((rows, features), bf16), shaped((rows, width), bf16)],
        flops=2 * rows * features * width,
        name=name,
    )


def masked_scores(kind, keys, queries, katt, qatt):
    scores = dot_nt(keys, queries)
    if kind == "free":
        return scores
    if kind == "valid":
        return jnp.where(katt[:, 2:3] > 0.0, scores, masked_value)
    places = lax.broadcasted_iota(jnp.int32, scores.shape, 0)
    asking = lax.broadcasted_iota(jnp.int32, scores.shape, 1)
    same = katt[:, 0:1] == qatt[0:1, :]
    if kind == "prev":
        allowed = same & (places > asking)
    else:
        allowed = same & ((places <= asking) | (katt[:, 1:2] == qatt[1:2, :]))
    return jnp.where(allowed, scores, masked_value)


def attention_inputs(queries, segments, katt, qatt):
    arrays = []

    def place(array):
        for k, known in enumerate(arrays):
            if known is array:
                return k
        arrays.append(array)
        return len(arrays) - 1

    use_q = place(queries[0])
    use_k = [place(segment[1]) for segment in segments]
    use_att = place(katt)
    use_qatt = place(qatt) if qatt is not None else None
    return arrays, use_q, use_k, use_att, use_qatt


def read_attention(refs, uses, queries, segments, head):
    use_q, use_k, use_att, use_qatt = uses
    unused, q_row, q_col = queries

    def take(ref, row, col):
        lanes = pl.ds(pl.multiple_of(col + head * HEAD, HEAD), HEAD)
        return ref[row * BLOCK : (row + 1) * BLOCK, lanes]

    q = take(refs[use_q], q_row, q_col)
    parts = []
    for (kind, unused, row, k_col, v_col, att), k in zip(segments, use_k):
        rows = None if att is None else refs[use_att][att * BLOCK : (att + 1) * BLOCK, :]
        parts.append((kind, take(refs[k], row, k_col), take(refs[k], row, v_col), rows))
    qa = None if use_qatt is None else refs[use_qatt][:, q_row * BLOCK : (q_row + 1) * BLOCK]
    return q, parts, qa


def attend(idx, queries, segments, katt, qatt, heads, name):
    arrays, *uses = attention_inputs(queries, segments, katt, qatt)
    count = len(arrays)

    def body(s, *refs):
        o_ref, l_ref = refs[count:]

        @pl.loop(0, heads)
        def _(head):
            q, parts, qa = read_attention(refs, uses, queries, segments, head)
            scores = [masked_scores(kind, k, q, ka, qa) for kind, k, v, ka in parts]
            largest = functools.reduce(
                jnp.maximum, [jnp.max(x, axis=0, keepdims=True) for x in scores]
            )
            total = jnp.zeros_like(largest)
            mixed = jnp.zeros((HEAD, BLOCK), f32)
            for x, (kind, k, v, ka) in zip(scores, parts):
                raised = jnp.exp2((x - largest) * log2_scale)
                total = total + jnp.sum(raised, axis=0, keepdims=True)
                mixed = mixed + dot_tn(v, raised.astype(bf16))
            lanes = pl.ds(pl.multiple_of(head * HEAD, HEAD), HEAD)
            o_ref[:, lanes] = jnp.transpose(mixed * (1.0 / total)).astype(bf16)
            l_ref[head] = largest * log2_scale + jnp.log2(total)

    keys = BLOCK * len(segments)
    return launch(
        body,
        idx,
        arrays,
        [shaped((BLOCK, heads * HEAD), bf16), shaped((heads, 1, BLOCK), f32)],
        flops=4 * heads * BLOCK * keys * HEAD * 2,
        name=name,
    )


def attend_back(idx, queries, segments, katt, qatt, heads, logs, upstream, added, dtypes, name):
    arrays, *uses = attention_inputs(queries, segments, katt, qatt)
    count = len(arrays)
    inputs = arrays + [logs, upstream]
    for pairs in added:
        for pair in pairs:
            inputs.extend(pair)
    wide = (BLOCK, heads * HEAD)
    outputs = [shaped(wide, bf16)]
    for dtype in dtypes:
        outputs.extend([shaped(wide, dtype)] * 2)

    def body(s, *refs):
        rest = list(refs[count:])
        l_ref, go_ref = rest.pop(0), rest.pop(0)
        sums = []
        for pairs in added:
            sums.append([(rest.pop(0), rest.pop(0)) for unused in pairs])
        gq_ref = rest.pop(0)
        outs = list(zip(rest[0::2], rest[1::2]))

        @pl.loop(0, heads)
        def _(head):
            q, parts, qa = read_attention(refs, uses, queries, segments, head)
            lanes = pl.ds(pl.multiple_of(head * HEAD, HEAD), HEAD)
            log_total = l_ref[head]
            go = go_ref[:, lanes]
            chances, grads = [], []
            inner = jnp.zeros((1, BLOCK), f32)
            for kind, k, v, ka in parts:
                x = masked_scores(kind, k, q, ka, qa)
                chance = jnp.exp2(x * log2_scale - log_total)
                grad = dot_nt(v, go)
                inner = inner + jnp.sum(chance * grad, axis=0, keepdims=True)
                chances.append(chance)
                grads.append(grad)
            gq = jnp.zeros((HEAD, BLOCK), f32)
            for (kind, k, v, ka), chance, grad, pairs, out in zip(
                parts, chances, grads, sums, outs
            ):
                gl = (chance * (grad - inner)).astype(bf16)
                gk = dot_nn(gl, q) * score_scale
                gv = dot_nn(chance.astype(bf16), go)
                gq = gq + dot_tn(k, gl)
                for more_k, more_v in pairs:
                    gk = gk + more_k[:, lanes]
                    gv = gv + more_v[:, lanes]
                out[0][:, lanes] = gk.astype(out[0].dtype)
                out[1][:, lanes] = gv.astype(out[1].dtype)
            gq_ref[:, lanes] = jnp.transpose(gq * score_scale).astype(bf16)

    keys = BLOCK * len(segments)
    return launch(
        body,
        idx,
        inputs,
        outputs,
        flops=10 * heads * BLOCK * keys * HEAD * 2,
        vmem=20,
        name=name,
    )


def state_update(idx, pieces, write_pieces, state, retain, gain, weights, width, name):
    rows, features = state.shape
    count = len(pieces)
    project = weights is not None

    def body(s, *refs):
        refs = list(refs)
        piece_refs = [refs.pop(0) for unused in range(count)]
        w_refs = [refs.pop(0) for unused in range(count)]
        s_ref, r_ref = refs[:2]
        refs = refs[2:]
        if project:
            g_ref, p_ref, out_ref, n_ref, t_ref = refs
        else:
            (out_ref,) = refs

        @pl.loop(0, rows // TILE)
        def _(i):
            at = span(i * TILE)
            terms = [
                dot_nn(o_ref[at, :], w_ref[: o_ref.shape[1], :])
                for o_ref, w_ref in zip(piece_refs, w_refs)
            ]
            while len(terms) > 1:
                terms = [a + b for a, b in zip(terms[0::2], terms[1::2])]
            update = terms[0]
            keep = r_ref[...]
            following = keep * s_ref[at, :].astype(f32) + (1.0 - keep) * update
            out_ref[at, :] = following
            if project:
                normed = (unit_rows(following)[0] * g_ref[...]).astype(bf16)
                n_ref[at, :] = normed
                t_ref[at, :] = dot_nn(normed, p_ref[:, :width]).astype(bf16)

    inputs = list(pieces) + list(write_pieces) + [state, retain]
    outputs = [shaped((rows, features), f32)]
    if project:
        inputs += [gain, weights]
        outputs += [shaped((rows, features), bf16), shaped((rows, width), bf16)]
    return launch(
        body,
        idx,
        inputs,
        outputs,
        flops=2 * rows * features * (features + (width if project else 0)),
        name=name,
    )


def take_sum(i, s, refs, total):
    chip_ref, mine_ref, theirs_ref = refs
    steps = HALF // TILE
    at, inner = span(tile_start(i, s)), span(lax.rem(i, steps) * TILE)

    @pl.when(i < steps)
    def _():
        total[...] = chip_ref[at, :].astype(f32) + mine_ref[inner, :].astype(f32)

    @pl.when(i >= steps)
    def _():
        total[...] = chip_ref[at, :].astype(f32) + theirs_ref[inner, :].astype(f32)

    return total[...]


def chip_sum(idx, partial, other, name):
    rows, features = partial.shape
    tall = 32

    def body(s, a_ref, b_ref, sum_ref, own_ref):
        @pl.loop(0, rows // tall)
        def _(i):
            at = rows_of(i, 0, tall)
            sum_ref[at, :] = (a_ref[at, :].astype(f32) + b_ref[at, :].astype(f32)).astype(bf16)

        @pl.loop(0, HALF // tall)
        def _(i):
            own_ref[rows_of(i, 0, tall), :] = sum_ref[pl.ds(pl.multiple_of(s[1] * HALF + i * tall, tall), tall), :]

    return launch(
        body,
        idx,
        [partial, other],
        [shaped((rows, features), bf16), shaped((HALF, features), bf16)],
        name=name,
    )


def add_rows(i, ref, value):
    value = jnp.sum(value, axis=0, keepdims=True)

    @pl.when(i == 0)
    def _():
        ref[...] = value

    @pl.when(i != 0)
    def _():
        ref[...] = ref[...] + value


def project_back(idx, grads, weights, column, name):
    rows, width = grads[0].shape
    features = weights.shape[1]

    def body(s, *refs):
        *g_refs, w_ref, out_ref = refs

        @pl.loop(0, rows // TILE)
        def _(i):
            at = span(i * TILE)
            out = jnp.zeros((TILE, features), f32)
            for k, ref in enumerate(g_refs):
                first = column + k * width
                out = out + dot_nn(ref[at, :], w_ref[first : first + width, :])
            out_ref[at, :] = out.astype(bf16)

    return launch(
        body,
        idx,
        list(grads) + [weights],
        [shaped((rows, features), bf16)],
        flops=2 * rows * features * width * len(grads),
        name=name,
    )[0]


def state_back(idx, sums, state, following, retain, gain, write_own, name):
    rows, features = state.shape
    before = write_own is not None
    width = write_own.shape[1] // 2 if before else 10

    def body(s, *refs):
        refs = list(refs)
        total = refs.pop()
        sum_refs = [refs.pop(0) for unused in range(len(sums))]
        s_ref, r_ref, g_ref = refs[:3]
        refs = refs[3:]
        following_ref = refs.pop(0) if following is not None else None
        if before:
            w_ref, gs_ref, gain_ref, gu_ref, gos_ref = refs
        else:
            gs_ref, gain_ref = refs

        @pl.loop(0, rows // TILE)
        def _(i):
            at = span(tile_start(i, s))
            up = take_sum(i, s, sum_refs, total)
            unit, inverse = unit_rows(s_ref[at, :].astype(f32))
            out = unit_back(up, unit, inverse, g_ref[...])
            if following is not None:
                out = r_ref[...] * following_ref[at, :] + out
            gs_ref[at, :] = out
            add_rows(i, gain_ref, up * unit)
            if before:
                gu = ((1.0 - r_ref[...]) * out).astype(bf16)
                gu_ref[at, :] = gu
                gos_ref[at, :] = dot_nn(gu, w_ref[:, :width]).astype(bf16)

    inputs = list(sums) + [state, retain, gain]
    outputs = [shaped((rows, features), f32), shaped((1, features), f32)]
    if following is not None:
        inputs.append(following)
    if before:
        inputs.append(write_own)
        outputs += [shaped((rows, features), bf16), shaped((rows, width), bf16)]
    return launch(
        body,
        idx,
        inputs,
        outputs,
        scratch=[pltpu.VMEM((TILE, features), f32)],
        flops=2 * rows * features * width,
        name=name,
    )


def last_update_back(idx, retain, write_own, rows, name):
    features, width = write_own.shape[0], write_own.shape[1] // 2

    def body(s, r_ref, w_ref, gu_ref, gos_ref):
        gu = ((1.0 - r_ref[...]) * jnp.zeros((rows, features), f32)).astype(bf16)
        gu_ref[...] = gu
        gos_ref[...] = dot_nn(gu, w_ref[:, :width]).astype(bf16)

    return launch(
        body,
        idx,
        [retain, write_own],
        [shaped((rows, features), bf16), shaped((rows, width), bf16)],
        name=name,
    )


def gelu_both(a):
    root, cubic = 0.7978845608028654, 0.044715
    squared = a * a
    bent = jnp.tanh(root * (a + cubic * (squared * a)))
    rising = 0.5 * (1.0 + bent)
    slope = rising + (0.5 * root) * a * (1.0 - bent * bent) * (1.0 + (3.0 * cubic) * squared)
    return a * rising, slope


def output_forward(idx, number, pieces, out_pieces, tokens, gain, name):
    features = tokens.shape[1]
    count = len(pieces)

    def body(s, *refs):
        o_refs, w_refs = refs[:count], refs[count : 2 * count]
        t_ref, g_ref, x1_ref, xn_ref = refs[2 * count :]

        @pl.loop(0, BLOCK // TILE)
        def _(i):
            at = span(i * TILE)
            x1 = t_ref[span(i * TILE, number * BLOCK), :].astype(f32)
            for o_ref, w_ref in zip(o_refs, w_refs):
                x1 = x1 + dot_nn(o_ref[at, :], w_ref[o_ref.shape[1] :, :])
            x1_ref[at, :] = x1
            xn_ref[at, :] = (unit_rows(x1)[0] * g_ref[...]).astype(bf16)

    return launch(
        body,
        idx,
        list(pieces) + list(out_pieces) + [tokens, gain],
        [shaped((BLOCK, features), f32), shaped((BLOCK, features), bf16)],
        flops=2 * BLOCK * features * features,
        name=name,
    )


def dense_forward(idx, normed, dense, name):
    features = normed.shape[1]
    hidden = dense[1].shape[0]

    def body(s, n_ref, up_ref, down_ref, h_ref, slope_ref, part_ref):
        @pl.loop(0, BLOCK // TILE)
        def _(i):
            at = span(i * TILE)
            h, slope = gelu_both(dot_nn(n_ref[at, :], up_ref[:, :hidden]))
            h = h.astype(bf16)
            h_ref[at, :] = h
            slope_ref[at, :] = slope.astype(bf16)
            part_ref[at, :] = dot_nn(h, down_ref[...]).astype(bf16)

    return launch(
        body,
        idx,
        [normed, *dense],
        [
            shaped((BLOCK, hidden), bf16),
            shaped((BLOCK, hidden), bf16),
            shaped((BLOCK, features), bf16),
        ],
        flops=4 * BLOCK * features * hidden,
        name=name,
    )


def dense_backward(idx, number, sums, x1, teacher, katt, slope, dense, name):
    features = x1.shape[1]
    up_t, both = dense
    hidden = up_t.shape[0]

    def body(s, *refs):
        refs = list(refs)
        total = refs.pop()
        sum_refs = [refs.pop(0) for unused in range(len(sums))]
        x_ref, t_ref, v_ref, slope_ref, up_ref, d_ref = refs[:6]
        gm_ref, ga_ref, loss_ref, part_ref = refs[6:]

        @pl.loop(0, BLOCK // TILE)
        def _(i):
            start = tile_start(i, s)
            at, far = span(start), span(start, number * BLOCK)
            errors = x_ref[at, :] + take_sum(i, s, sum_refs, total) - t_ref[far, :].astype(f32)
            gy = v_ref[far, 2:3] * errors
            add_rows(i, loss_ref, gy * errors)
            gm = gy.astype(bf16)
            gm_ref[at, :] = gm
            ga = (dot_nn(gm, d_ref[:, hidden:]) * slope_ref[at, :].astype(f32)).astype(bf16)
            ga_ref[at, :] = ga
            part_ref[at, :] = dot_nn(ga, up_ref[...]).astype(bf16)

    return launch(
        body,
        idx,
        list(sums) + [x1, teacher, katt, slope, up_t, both],
        [
            shaped((BLOCK, features), bf16),
            shaped((BLOCK, hidden), bf16),
            shaped((1, features), f32),
            shaped((BLOCK, features), bf16),
        ],
        scratch=[pltpu.VMEM((TILE, features), f32)],
        flops=4 * BLOCK * features * hidden,
        name=name,
    )


def output_backward(idx, sums, gy, x1, gain, out_own, name):
    features = x1.shape[1]
    width = out_own.shape[1] // 2

    def body(s, *refs):
        refs = list(refs)
        total = refs.pop()
        sum_refs = [refs.pop(0) for unused in range(len(sums))]
        gy_ref, x_ref, g_ref, w_ref, gp_ref, go_ref, gain_ref = refs

        @pl.loop(0, BLOCK // TILE)
        def _(i):
            at = span(tile_start(i, s))
            up = take_sum(i, s, sum_refs, total)
            unit, inverse = unit_rows(x_ref[at, :])
            gx = gy_ref[at, :].astype(f32) + unit_back(up, unit, inverse, g_ref[...])
            gp = gx.astype(bf16)
            gp_ref[at, :] = gp
            go_ref[at, :] = dot_nn(gp, w_ref[:, width:]).astype(bf16)
            add_rows(i, gain_ref, up * unit)

    return launch(
        body,
        idx,
        list(sums) + [gy, x1, gain, out_own],
        [
            shaped((BLOCK, features), bf16),
            shaped((BLOCK, width), bf16),
            shaped((1, features), f32),
        ],
        scratch=[pltpu.VMEM((TILE, features), f32)],
        flops=2 * BLOCK * features * width,
        name=name,
    )


def weight_grads(idx, groups, name):
    features = groups[0][0][0].shape[1]
    inputs, specs, total, flops = [], [], 0, 0
    for parts in groups:
        for left, block, right in parts:
            rows = right.shape[0]
            inputs += [left, right]
            specs.append(pl.BlockSpec((rows, HALF), lambda i, block=block: (block, i)))
            specs.append(
                pl.BlockSpec(right.shape, lambda i: (0, 0), pipeline_mode=pl.Buffered(1))
            )
            flops += 2 * rows * features * right.shape[1]
        total += parts[0][2].shape[1]

    def body(s, *refs):
        refs = list(refs)
        out_ref = refs.pop()
        at = 0
        for parts in groups:
            size = parts[0][2].shape[1]
            out = jnp.zeros((HALF, size), f32)
            for unused in parts:
                left, right = refs.pop(0), refs.pop(0)
                out = out + dot_tn(left[...], right[...])
            out_ref[:, at : at + size] = out.astype(bf16)
            at += size

    return pl.pallas_call(
        body,
        grid=(features // HALF,),
        in_specs=[pl.BlockSpec(memory_space=pltpu.SMEM)] + specs,
        out_specs=pl.BlockSpec((HALF, total), lambda i: (i, 0)),
        out_shape=pltpu.HBM((features, total), bf16),
        compiler_params=pltpu.CompilerParams(
            dimension_semantics=("arbitrary",), vmem_limit_bytes=20 << 20
        ),
        cost_estimate=cost(flops, inputs),
        name=name,
    )(idx, *inputs)


def unpack_grads(packed, widths, flipped, name):
    rows = packed.shape[0]

    def body(p_ref, *out_refs):
        at = 0
        for size, flip, out_ref in zip(widths, flipped, out_refs):
            values = p_ref[:, at : at + size].astype(f32)
            out_ref[...] = jnp.transpose(values) if flip else values
            at += size

    return pl.pallas_call(
        body,
        in_specs=[pl.BlockSpec(memory_space=pltpu.VMEM)],
        out_specs=[pl.BlockSpec(memory_space=pltpu.VMEM)] * len(widths),
        out_shape=[
            shaped((size, rows) if flip else (rows, size), f32)
            for size, flip in zip(widths, flipped)
        ],
        compiler_params=pltpu.CompilerParams(vmem_limit_bytes=8 << 20),
        cost_estimate=cost(0, [packed]),
        name=name,
    )(packed)


def arrange_rows(idx, pieces, count, name):
    rows, features = pieces[0].shape
    rows = rows // count

    def body(s, *refs):
        ins, outs = refs[: len(pieces)], refs[len(pieces) :]
        for k, ref in enumerate(ins):
            for j, out_ref in enumerate(outs):
                out_ref[rows_of(s[0] ^ k, 0, rows), :] = ref[j * rows : (j + 1) * rows, :]

    return launch(
        body,
        idx,
        pieces,
        [shaped((rows * len(pieces), features), pieces[0].dtype)] * count,
        name=name,
    )


def turn(idx, values, first, count, name):
    rows = values.shape[0]
    wide = 256

    def body(s, v_ref, out_ref):
        @pl.loop(0, count // wide)
        def _(i):
            lanes = pl.ds(pl.multiple_of(first + i * wide, HEAD), wide)
            out_ref[rows_of(i, 0, wide), :] = jnp.transpose(v_ref[:, lanes])

    return launch(body, idx, [values], [shaped((count, rows), values.dtype)], name=name)[0]


def arrange_columns(idx, blocks, across, name):
    rows, width = blocks[0].shape
    depth = len(blocks)

    def body(s, *refs):
        out_ref = refs[-1]
        for k in range(depth):
            level = lax.rem(s[3] + depth - k, depth)
            out_ref[rows_of(2 * level + s[4], 0, rows), :] = refs[k][...]
            out_ref[rows_of(2 * level + 1 - s[4], 0, rows), :] = refs[depth + k][...]

    return launch(
        body,
        idx,
        list(blocks) + list(across),
        [shaped((2 * depth * rows, width), blocks[0].dtype)],
        name=name,
    )[0]


def split_grads(idx, groups, depth, name):
    features = groups[0][0][0].shape[1]
    rows = features // (2 * depth)
    total = sum(parts[0][2].shape[1] for parts in groups)
    inputs = []

    def place(array):
        for k, known in enumerate(inputs):
            if known is array:
                return k
        inputs.append(array)
        return len(inputs) - 1

    uses = [[(place(a), block, place(c)) for a, block, c in parts] for parts in groups]

    def body(s, *refs):
        *ins, theirs_ref, mine_ref, held = refs

        @pl.loop(0, depth)
        def _(i):
            lanes = pl.ds(pl.multiple_of(i * 2 * rows, 2 * rows), 2 * rows)
            at = 0
            for parts in uses:
                size = ins[parts[0][2]].shape[1]
                out = jnp.zeros((2 * rows, size), f32)
                for left, block, right in parts:
                    count = ins[right].shape[0]
                    tall = slice(block * count, (block + 1) * count)
                    out = out + dot_tn(ins[left][tall, lanes], ins[right][...])
                held[:, at : at + size] = out.astype(bf16)
                at += size
            mine_ref[rows_of(i, 0, rows), :] = held[rows_of(s[4], 0, rows), :]
            theirs_ref[rows_of(i, 0, rows), :] = held[rows_of(1 - s[4], 0, rows), :]

    return launch(
        body,
        idx,
        inputs,
        [shaped((depth * rows, total), bf16)] * 2,
        scratch=[pltpu.VMEM((2 * rows, total), bf16)],
        name=name,
    )


def pair_blocks(idx, mine, got, depth, name):
    rows, width = mine.shape[0] // depth, mine.shape[1]

    def body(s, mine_ref, got_ref, *out_refs):
        for k, ref in enumerate(out_refs):
            at = rows_of(lax.rem(s[3] + k, depth), 0, rows)
            ref[...] = (mine_ref[at, :].astype(f32) + got_ref[at, :].astype(f32)).astype(ref.dtype)

    return launch(
        body,
        idx,
        [mine, got],
        [shaped((rows, width), f32)] + [shaped((rows, width), bf16)] * (depth - 1),
        name=name,
    )


def line_sum(idx, own, others, widths, flipped, name):
    rows = own.shape[0]

    def body(s, own_ref, *refs):
        ins, outs = refs[: len(others)], refs[len(others) :]
        total = own_ref[...]
        for ref in ins:
            total = total + ref[...].astype(f32)
        at = 0
        for size, flip, out_ref in zip(widths, flipped, outs):
            values = total[:, at : at + size]
            out_ref[...] = jnp.transpose(values) if flip else values
            at += size

    return launch(
        body,
        idx,
        [own] + list(others),
        [
            shaped((size, rows) if flip else (rows, size), f32)
            for size, flip in zip(widths, flipped)
        ],
        name=name,
    )


def pack(idx, arrays, takes, shapes, name):
    flipped = [take for take in takes if take[-1]]

    def body(s, *refs):
        ins, outs = refs[: len(arrays)], refs[len(arrays) : len(arrays) + len(shapes)]
        *held, sems = refs[len(arrays) + len(shapes) :]
        copies, spare = [], list(held)
        for j, (k, row, col, rows, cols, out, place, flip) in enumerate(takes):
            at = pl.ds(0, rows) if row is None else rows_of(s[row], 0, rows)
            to = pl.ds(0, cols) if col is None else rows_of(s[col], 0, cols)
            if flip:
                target = spare.pop(0)
            else:
                target = outs[out].at[pl.ds(place[0], rows), pl.ds(place[1], cols)]
            copies.append(pltpu.make_async_copy(ins[k].at[at, to], target, sems.at[j]))
            copies[-1].start()
        spare = list(held)
        for copy, (k, row, col, rows, cols, out, place, flip) in zip(copies, takes):
            copy.wait()
            if flip:
                to = slice(place[1], place[1] + rows)
                outs[out][place[0] : place[0] + cols, to] = jnp.transpose(spare.pop(0)[...])

    return pl.pallas_call(
        body,
        in_specs=[pl.BlockSpec(memory_space=pltpu.SMEM)]
        + [pl.BlockSpec(memory_space=pl.ANY)] * len(arrays),
        out_specs=[pl.BlockSpec(memory_space=pltpu.VMEM)] * len(shapes),
        out_shape=[shaped(a, bf16) for a in shapes],
        scratch_shapes=[pltpu.VMEM((take[3], take[4]), bf16) for take in flipped]
        + [pltpu.SemaphoreType.DMA((len(takes),))],
        compiler_params=pltpu.CompilerParams(vmem_limit_bytes=8 << 20),
        cost_estimate=cost(0, arrays),
        name=name,
    )(idx, *[pltpu.with_memory_space_constraint(a, pltpu.HBM) for a in arrays])


def input_rows(idx, own, arrived, gps, tokens, gain, name):
    rows, features = tokens.shape
    count = len(gps)

    def body(s, *refs):
        own_refs, far_refs, gp_refs = refs[:count], refs[count : 2 * count], refs[2 * count : 3 * count]
        t_ref, g_ref, out_ref, gain_ref = refs[3 * count :]
        unit, inverse = unit_rows(t_ref[...].astype(f32))
        for b in range(count):

            @pl.when(s[2] // 2 == b)
            def _():
                at = rows_of(s[1])
                up = own_refs[b][at, :].astype(f32) + far_refs[b][...].astype(f32)
                base = gp_refs[b][rows_of(s[1]), :].astype(f32)
                out_ref[...] = base + unit_back(up, unit, inverse, g_ref[...])
                gain_ref[...] = jnp.sum(up * unit, axis=0, keepdims=True)

    return launch(
        body,
        idx,
        list(own) + list(arrived) + list(gps) + [tokens, gain],
        [shaped((rows, features), f32), shaped((1, features), f32)],
        name=name,
    )


def per_device(
    block_input,
    state_start,
    teacher,
    valid_mask,
    segment,
    image_offset,
    retain,
    to_query,
    to_key,
    to_value,
    to_output,
    to_hidden,
    to_model,
    state_query,
    state_key,
    state_value,
    state_write,
    first_gain,
    second_gain,
    state_gain,
):
    row_devices = lax.axis_size("row")
    col_devices = lax.axis_size("col")
    row_index = lax.axis_index("row")
    col_index = lax.axis_index("col")
    local_rows, features = block_input.shape[1:]
    length = local_rows * row_devices
    width = to_query.shape[1]
    heads = width // HEAD
    hidden = to_hidden.shape[1] // row_devices
    nblocks = length // BLOCK
    pairs = row_devices == 4 and 2 * local_rows == BLOCK
    lines = pairs and col_devices == 8
    core_pairs = [(k, k ^ 1) for k in range(row_devices)]
    chip_pairs = [(k, k ^ 2) for k in range(row_devices)] if pairs else None
    if pairs:
        idx = jnp.stack([row_index, row_index % 2, row_index, col_index // 2, col_index % 2])
    else:
        idx = jnp.stack([0, 1, row_index, 0, 0])
    idx = idx.astype(jnp.int32)

    def to_core(x):
        return lax.ppermute(x, "row", core_pairs)

    def to_chip(x):
        return lax.ppermute(x, "row", chip_pairs)

    def row_moves(x):
        if not pairs:
            stacked = lax.all_gather(x, "row", axis=0, tiled=False)
            return [stacked[k] for k in range(row_devices)]
        return [x, to_core(x), to_chip(x)]

    def row_pieces(moved, *ties):
        if not pairs:
            return moved
        x, near, far = moved
        return [x, near, far, to_core(after(far, *ties))]

    depth_z = col_devices // 2

    def along(v, step):
        levels = range(depth_z)
        moves = [(2 * z + y, 2 * ((z + step) % depth_z) + y) for z in levels for y in range(2)]
        return lax.ppermute(v, "col", moves)

    def across(v):
        return lax.ppermute(v, "col", [(k, k ^ 1) for k in range(col_devices)])

    class Columns:
        def __init__(self, x, name):
            self.name = name
            if lines:
                self.blocks = [x] + [along(x, k) for k in range(1, depth_z)]
                self.crossed = [across(x)]
            else:
                self.whole = lax.all_gather(x, "col", axis=0, tiled=True)

        def cross(self, k, *ties):
            if lines:
                self.crossed.append(across(after(self.blocks[k], *ties)))

        def landed(self, k):
            return [self.blocks[k], self.crossed[k - 1]] if lines else []

        def result(self, *ties):
            if lines:
                order = after(idx, *ties)
                return arrange_columns(order, self.blocks, self.crossed, self.name)
            return self.whole

    class Scattered:
        def __init__(self, groups, name, *ties):
            self.name, self.widths = name, [parts[0][2].shape[1] for parts in groups]
            if lines:
                order = after(idx, *ties) if ties else idx
                theirs, self.mine = split_grads(order, groups, depth_z, name)
                self.got = across(theirs)
            else:
                packed = weight_grads(idx, groups, name)
                self.whole = lax.psum_scatter(packed, "col", scatter_dimension=0, tiled=True)

        def send(self, *ties):
            if lines:
                mine = after(self.mine, *ties) if ties else self.mine
                self.own, *blocks = pair_blocks(idx, mine, self.got, depth_z, f"{self.name}_y")
                self.far = [along(block, k + 1) for k, block in enumerate(blocks)]

        def result(self, flipped):
            if lines:
                return line_sum(idx, self.own, self.far, self.widths, flipped, f"{self.name}_z")
            return unpack_grads(self.whole, self.widths, flipped, f"{self.name}_z")

    class RowSum:
        def __init__(self, partial, name, receiver=None, ties=()):
            if pairs:
                order = after(idx, *ties) if ties else idx
                self.chip, own = chip_sum(order, partial, to_core(partial), name)
                moves = [m for m in chip_pairs if receiver is None or m[1] // 2 == receiver]
                self.far = lax.ppermute(own, "row", moves)
            else:
                self.chip = lax.psum(partial, "row")

        def result(self, *ties):
            if pairs:
                return [self.chip, self.far, to_core(after(self.far, *ties))]
            none = jnp.zeros((HALF, features), bf16)
            return [self.chip, none, none]

    def all_sum(x):
        for axis, size in (("row", row_devices), ("col", col_devices)):
            step = 1
            while step < size:
                x = x + lax.ppermute(x, axis, [(k, k ^ step) for k in range(size)])
                step *= 2
        return x

    depth = to_query.shape[0]
    (near,) = pack(
        idx,
        [state_query, state_key, state_value, to_query, to_key, to_value],
        [(k, None, None, depth, width, 0, (0, k * width), False) for k in range(6)],
        [(depth, 6 * width)],
        "pack_near",
    )
    near = lax.all_gather(near, "col", axis=0, tiled=True)
    rows_in, mid, far_weights = pack(
        idx,
        [state_write, to_output, to_hidden, to_model, block_input[0], teacher[0]],
        [
            (4, None, None, local_rows, features, 0, (0, 0), False),
            (5, None, None, local_rows, features, 0, (local_rows, 0), False),
            (0, 2, None, width, depth, 1, (0, 0), True),
            (1, None, None, width, depth, 1, (0, width), True),
            (2, None, 2, depth, hidden, 2, (0, 0), False),
            (3, 2, None, hidden, depth, 2, (0, hidden), True),
        ],
        [(2 * local_rows, features), (depth, 2 * width), (depth, 2 * hidden)],
        "pack_rest",
    )
    rows_moved = row_moves(rows_in) if pairs else None
    mid = Columns(mid, "mid")
    for k in range(1, depth_z):
        mid.cross(k)
    mid = mid.result()
    mid_n = turn(idx, mid, 0, 2 * width, "mid_turn")
    held = [mid_n] + (rows_moved[2:] if pairs else [])
    dense = lax.all_gather(after(far_weights, *held), "col", axis=0, tiled=True)
    mid_moved = row_moves(mid_n)
    if pairs:
        tokens, teacher_all = arrange_rows(idx, row_pieces(rows_moved), 2, "tokens")
    else:
        tokens, teacher_all = [
            lax.all_gather(x[0], "row", axis=0, tiled=True) for x in (block_input, teacher)
        ]

    valid_row = lax.dynamic_index_in_dim(valid_mask, col_index, 0, keepdims=False)
    segment_row = segment[0]
    numbers = jnp.arange(nblocks, dtype=jnp.int32)
    places = jnp.arange(length, dtype=jnp.int32)
    starts = numbers * BLOCK + image_offset[0]
    inside = (places[:, None] >= starts[None, :]) & (places[:, None] < starts[None, :] + PIECE)
    piece = jnp.sum(jnp.where(inside, numbers[None, :] + 1, 0), axis=1) - 1
    valid_count = jnp.sum(valid_mask.astype(f32))
    total_tokens = f32(length * col_devices)
    weight_of_row = total_tokens / valid_count * valid_row.astype(f32)
    document = segment_row.astype(f32)
    nothing = jnp.zeros_like(document)
    katt = jnp.stack(
        [jnp.where(valid_row > 0, document, -1.0), piece.astype(f32), weight_of_row, nothing],
        axis=1,
    )
    qatt = jnp.stack(
        [document, jnp.where(piece >= 0, piece, -2).astype(f32), nothing, nothing], axis=0
    )
    retain2 = retain[None]
    first_gain2, second_gain2, state_gain2 = first_gain[None], second_gain[None], state_gain[None]

    def token_segments(number, trio):
        found = []
        if number > 0:
            found.append(("prev", token_heads, number - 1, width, 2 * width, number - 1))
        found.append(("own", token_heads, number, width, 2 * width, number))
        found.append(("free", trio, 0, width, 2 * width, None))
        return found

    def state_segments(number, trio):
        return [
            ("valid", token_heads, number, width, 2 * width, number),
            ("free", trio, 0, width, 2 * width, None),
        ]

    current = state_start[0]
    near_t = turn(idx, near, 0, 6 * width, "near_turn")
    state_low, trio = norm_project(after(idx, near_t), current, state_gain2, near, 0, 3 * width, "state_proj")
    first_low, token_heads = norm_project(
        idx, tokens, first_gain2, near, 3 * width, 3 * width, "token_proj"
    )
    states, lows, trios = [], [], []
    state_out, state_logs, token_out, token_logs = [], [], [], []
    x1s, second_lows, hiddens, slopes, dense_sums = [], [], [], [], []
    state_pieces, token_pieces = [], []
    end = nblocks - 1

    def state_part(b):
        mixed, logs = attend(
            idx,
            (trios[b], 0, 0),
            state_segments(b, trios[b]),
            katt,
            None,
            heads,
            f"state_attend{b}",
        )
        state_out.append(mixed)
        state_logs.append(logs)
        state_pieces.append(row_moves(mixed) if b < nblocks - 1 else None)

    for b in range(nblocks):
        states.append(current)
        lows.append(state_low)
        trios.append(trio)
        last = b + 1 == nblocks
        if not last:
            state_part(b)
        mixed, logs = attend(
            idx, (token_heads, b, 0), token_segments(b, trio), katt, qatt, heads, f"token_attend{b}"
        )
        if b == 0:
            mid_pieces = row_pieces(mid_moved, mixed)
        token_out.append(mixed)
        token_logs.append(logs)
        token_pieces.append(row_moves(mixed))
        if not last:
            current, state_low, trio = state_update(
                idx,
                row_pieces(state_pieces[b], mixed),
                mid_pieces,
                current,
                retain2,
                state_gain2,
                near,
                3 * width,
                f"update{b}",
            )
            token_pieces[b] = row_pieces(token_pieces[b], trio)
    state_part(nblocks - 1)
    token_pieces[-1] = row_pieces(token_pieces[-1], state_out[-1])

    gus = [None] * nblocks
    gms, gas, losses, gps, gos, second_sums = [], [], [], [], [], []
    second_back = []
    for b in range(nblocks):
        x1, low = output_forward(
            idx, b, token_pieces[b], mid_pieces, tokens, second_gain2, f"out{b}"
        )
        x1s.append(x1)
        second_lows.append(low)
    down = turn(after(idx, state_out[-1], *second_lows), dense, hidden, hidden, "down_turn")
    order = idx
    for b in range(nblocks):
        h, slope, partial = dense_forward(order, second_lows[b], (dense, down), f"dense{b}")
        hiddens.append(h)
        slopes.append(slope)
        ties = []
        if b == 0:
            up_t = turn(after(idx, h), dense, 0, hidden, "up_turn")
            ties.append(up_t)
        dense_sums.append(RowSum(partial, f"dense_sum{b}", ties=ties))
        order = after(idx, dense_sums[b].chip)

    def state_back_part(b, gos_state, own, free, dtype):
        return attend_back(
            idx,
            (trios[b], 0, 0),
            state_segments(b, trios[b]),
            katt,
            None,
            heads,
            state_logs[b],
            gos_state,
            [own, free],
            [dtype, dtype],
            f"state_back{b}",
        )

    def token_back_part(b, own, free, dtype, upstream):
        segments = token_segments(b, trios[b])
        added = ([[]] if b > 0 else []) + [own, free]
        dtypes = ([f32] if b > 0 else []) + [dtype, dtype]
        found = attend_back(
            idx,
            (token_heads, b, 0),
            segments,
            katt,
            qatt,
            heads,
            token_logs[b],
            upstream,
            added,
            dtypes,
            f"token_back{b}",
        )
        return found[0], found[-4:], (found[1], found[2]) if b > 0 else None

    late_mid = after(mid, dense_sums[end].chip)
    gus[end], gos_state = last_update_back(idx, retain2, late_mid, NS, "last_back")
    state_found = state_back_part(end, gos_state, [], [], f32)
    ready = teacher_all
    for b in range(nblocks):
        hides = [hiddens[end]] if b == 0 else [gms[b - 1], state_found[0]]
        gm, ga, loss, partial = dense_backward(
            idx, b, dense_sums[b].result(*hides), x1s[b], ready, katt, slopes[b], (up_t, dense), f"back{b}"
        )
        gms.append(gm)
        gas.append(ga)
        losses.append(loss)
        if b < end:
            second_back.append(RowSum(partial, f"back_sum{b}"))
            ready = after(teacher_all, second_back[b].chip)
    dense_grads = weight_grads(
        idx,
        [
            [(low, 0, ga) for low, ga in zip(second_lows, gas)],
            [(gm, 0, h) for gm, h in zip(gms, hiddens)],
        ],
        "dense_grads",
    )
    filled = [dense_grads]
    ties = [dense_grads] + [back.far for back in second_back] if pairs else []
    second_back.append(RowSum(partial, f"back_sum{end}", ties=ties))
    dense_grads = lax.psum_scatter(dense_grads, "col", scatter_dimension=0, tiled=True)

    token_found = [None] * nblocks
    for b in range(nblocks):
        gp, go, gain_sum = output_backward(
            idx,
            second_back[b].result(*(filled if b == end else [gms[end]])),
            gms[b],
            x1s[b],
            second_gain2,
            mid,
            f"out_back{b}",
        )
        gps.append(gp)
        gos.append(go)
        second_sums.append(gain_sum)
        if b < end:
            token_found[b] = token_back_part(b, [], [], f32, go)
            filled.append(token_found[b][0])
    trio_grads = [None] * nblocks
    token_grads = [None] * nblocks
    first_sums = [None] * nblocks
    gain_sums = []
    grad_next = None
    gqs, gk, gv, gks, gvs = state_found
    gq, (gk, gv, gks, gvs), key_part = token_back_part(
        end, [(gk, gv)], [(gks, gvs)], bf16, gos[end]
    )
    state_pieces[-1] = row_moves(after(state_out[-1], gos[end]))
    gqs = after(gqs, state_pieces[-1][2])
    trio_grads[end] = (gqs, gks, gvs)
    token_grads[end] = (gq, gk, gv)
    for b in reversed(range(nblocks)):
        order = idx
        if b == 0:

            def state_group(k):
                return [(lows[c], 0, trio_grads[c][k]) for c in range(nblocks)]

            def token_group(k):
                return [(first_low, c, token_grads[c][k]) for c in range(nblocks)]

            write_group = [(gu, 0, out) for gu, out in zip(gus, state_out)]
            late_grads = weight_grads(
                idx,
                [state_group(k) for k in range(3)] + [token_group(1), token_group(2)],
                "late_grads",
            )
            order = after(idx, late_grads)
            rest_grads = Scattered(
                [token_group(0), [(gp, 0, out) for gp, out in zip(gps, token_out)], write_group],
                "rest_grads",
                late_grads,
            )
            rest_grads.send()
            late_grads = lax.psum_scatter(late_grads, "col", scatter_dimension=0, tiled=True)
        trio_sum = RowSum(
            project_back(order, trio_grads[b], near_t, 0, f"trio_back{b}"),
            f"trio_sum{b}",
        )
        hides = []
        if b == end:
            (final_state,) = state_update(
                idx,
                row_pieces(state_pieces[-1], gq),
                mid_pieces,
                current,
                retain2,
                None,
                None,
                0,
                "update_last",
            )
            hides.append(final_state)
        first_sums[b] = project_back(idx, token_grads[b], near_t, 3 * width, f"first_back{b}")
        hides.append(first_sums[b])
        first_sums[b] = RowSum(first_sums[b], f"first_sum{b}", b) if pairs else first_sums[b]
        if b > 0:
            grad_next, gain_sum, gus[b - 1], gos_state = state_back(
                idx,
                trio_sum.result(*hides),
                states[b],
                grad_next,
                retain2,
                state_gain2,
                mid,
                f"chain_back{b}",
            )
            gq, (gk, gv, gks, gvs), next_part = token_found[b - 1]
            gqs, gk, gv, gks, gvs = state_back_part(
                b - 1, gos_state, [(gk, gv), key_part], [(gks, gvs)], bf16
            )
            key_part = next_part
            trio_grads[b - 1] = (gqs, gks, gvs)
            token_grads[b - 1] = (gq, gk, gv)
        else:
            grad_next, gain_sum = state_back(
                after(idx, rest_grads.own) if lines else idx,
                trio_sum.result(*hides),
                states[b],
                grad_next,
                retain2,
                state_gain2,
                None,
                "chain_back0",
            )
        gain_sums.append(gain_sum)

    if pairs:
        own_rows = [first.chip for first in first_sums]
        arrived = [first.far for first in first_sums]
        input_grad, first_sum = input_rows(
            idx, own_rows, arrived, gps, block_input[0], first_gain2, "input_rows"
        )
        first_sum = first_sum[0]
    else:
        both = jnp.concatenate(first_sums)
        grad_first = lax.psum_scatter(both, "row", scatter_dimension=0, tiled=True).astype(f32)
        own_gx1 = lax.dynamic_slice_in_dim(
            jnp.concatenate(gps), row_index * local_rows, local_rows
        ).astype(f32)
        unit, inverse = unit_rows(block_input[0].astype(f32))
        input_grad = own_gx1 + unit_back(grad_first, unit, inverse, first_gain2)
        first_sum = jnp.sum(grad_first * unit, axis=0)

    share = 1.0 / row_devices
    sums = jnp.stack(
        [
            sum(losses)[0] * share,
            first_sum,
            sum(second_sums)[0] * share,
            sum(gain_sums)[0] * share,
        ]
    )
    if lines:
        sums = after(sums, *rest_grads.far)
    summed = all_sum(sums)
    total_loss = jnp.sum(summed[0]) / (2.0 * total_tokens)

    upper_grad, lower_grad = unpack_grads(
        dense_grads, [hidden, hidden], [False, True], "unpack_dense"
    )
    late = unpack_grads(late_grads, [width] * 5, [False] * 5, "unpack_late")
    rest = rest_grads.result([False, True, True])

    return (
        total_loss,
        final_state[None],
        input_grad[None],
        grad_next[None],
        rest[0],
        late[3],
        late[4],
        rest[1],
        upper_grad,
        lower_grad,
        late[0],
        late[1],
        late[2],
        rest[2],
        summed[1],
        summed[2],
        summed[3],
    )


def solution(mesh):
    in_specs = (
        P("col", "row", None),
        P("col", None, None),
        P("col", "row", None),
        P(),
        P("col", None),
        P("col", None),
        P(),
        P("col", "row"),
        P("col", "row"),
        P("col", "row"),
        P("row", "col"),
        P("col", None),
        P(None, "col"),
        P("col", "row"),
        P("col", "row"),
        P("col", "row"),
        P(None, "col"),
        P(),
        P(),
        P(),
    )
    out_specs = (
        P(),
        P("col", None, None),
        P("col", "row", None),
        P("col", None, None),
        P("col", "row"),
        P("col", "row"),
        P("col", "row"),
        P("row", "col"),
        P("col", "row"),
        P("row", "col"),
        P("col", "row"),
        P("col", "row"),
        P("col", "row"),
        P("row", "col"),
        P(),
        P(),
        P(),
    )
    return jax.shard_map(
        per_device, mesh=mesh, in_specs=in_specs, out_specs=out_specs, check_vma=False
    )
```

```python
import functools

import jax
import jax.numpy as jnp
from jax import lax
from jax.experimental import pallas as pl
from jax.experimental.pallas import tpu as pltpu
from jax.sharding import PartitionSpec as P

HEAD = 128
BLOCK = 512
HALF = 256
NS = 512
PIECE = 256
COST = 8
TILE = 256

epsilon = 1e-06
masked_value = -1e30
score_scale = HEAD ** (-0.5)
log2_scale = score_scale * 1.4426950408889634
f32 = jnp.float32
bf16 = jnp.bfloat16


def dot_nn(a, b):
    return lax.dot_general(a, b, (((1,), (0,)), ((), ())), preferred_element_type=f32)


def dot_nt(a, b):
    return lax.dot_general(a, b, (((1,), (1,)), ((), ())), preferred_element_type=f32)


def dot_tn(a, b):
    return lax.dot_general(a, b, (((0,), (0,)), ((), ())), preferred_element_type=f32)


def cost(flops, arrays):
    return pl.CostEstimate(flops=flops // COST, bytes_accessed=1024, transcendentals=0)


def after(x, *earlier):
    return lax.optimization_barrier((x,) + earlier)[0]


def shaped(shape, dtype):
    return jax.ShapeDtypeStruct(shape, dtype)


def launch(body, idx, inputs, outputs, scratch=(), flops=0, vmem=12, name=None):
    return pl.pallas_call(
        body,
        in_specs=[pl.BlockSpec(memory_space=pltpu.SMEM)]
        + [pl.BlockSpec(memory_space=pltpu.VMEM)] * len(inputs),
        out_specs=[pl.BlockSpec(memory_space=pltpu.VMEM)] * len(outputs),
        out_shape=list(outputs),
        scratch_shapes=list(scratch),
        compiler_params=pltpu.CompilerParams(vmem_limit_bytes=vmem << 20),
        cost_estimate=cost(flops, inputs),
        name=name,
    )(idx, *inputs)


def rows_of(i, base=0, size=HALF):
    return pl.ds(pl.multiple_of(base + i * size, size), size)


def tile_start(i, s):
    steps = HALF // TILE
    return lax.rem(i // steps + s[1], 2) * HALF + lax.rem(i, steps) * TILE


def span(start, base=0):
    return pl.ds(pl.multiple_of(base + start, TILE), TILE)


def unit_rows(x):
    inverse = lax.rsqrt(jnp.mean(x * x, axis=-1, keepdims=True) + epsilon)
    return x * inverse, inverse


def unit_back(up, unit, inverse, gain):
    scaled = up * gain
    inner = jnp.mean(scaled * unit, axis=-1, keepdims=True)
    return inverse * (scaled - unit * inner)


def norm_project(idx, values, gain, weights, column, width, name):
    rows, features = values.shape

    def body(s, x_ref, g_ref, w_ref, n_ref, p_ref):
        @pl.loop(0, rows // TILE)
        def _(i):
            at = span(i * TILE)
            unit, unused = unit_rows(x_ref[at, :].astype(f32))
            normed = (unit * g_ref[...]).astype(bf16)
            n_ref[at, :] = normed
            p_ref[at, :] = dot_nn(normed, w_ref[:, column : column + width]).astype(bf16)

    return launch(
        body,
        idx,
        [values, gain, weights],
        [shaped((rows, features), bf16), shaped((rows, width), bf16)],
        flops=2 * rows * features * width,
        name=name,
    )


def masked_scores(kind, keys, queries, katt, qatt):
    scores = dot_nt(keys, queries)
    if kind == "free":
        return scores
    if kind == "valid":
        return jnp.where(katt[:, 2:3] > 0.0, scores, masked_value)
    places = lax.broadcasted_iota(jnp.int32, scores.shape, 0)
    asking = lax.broadcasted_iota(jnp.int32, scores.shape, 1)
    same = katt[:, 0:1] == qatt[0:1, :]
    if kind == "prev":
        allowed = same & (places > asking)
    else:
        allowed = same & ((places <= asking) | (katt[:, 1:2] == qatt[1:2, :]))
    return jnp.where(allowed, scores, masked_value)


def attention_inputs(queries, segments, katt, qatt):
    arrays = []

    def place(array):
        for k, known in enumerate(arrays):
            if known is array:
                return k
        arrays.append(array)
        return len(arrays) - 1

    use_q = place(queries[0])
    use_k = [place(segment[1]) for segment in segments]
    use_att = place(katt)
    use_qatt = place(qatt) if qatt is not None else None
    return arrays, use_q, use_k, use_att, use_qatt


def read_attention(refs, uses, queries, segments, head):
    use_q, use_k, use_att, use_qatt = uses
    unused, q_row, q_col = queries

    def take(ref, row, col):
        lanes = pl.ds(pl.multiple_of(col + head * HEAD, HEAD), HEAD)
        return ref[row * BLOCK : (row + 1) * BLOCK, lanes]

    q = take(refs[use_q], q_row, q_col)
    parts = []
    for (kind, unused, row, k_col, v_col, att), k in zip(segments, use_k):
        rows = None if att is None else refs[use_att][att * BLOCK : (att + 1) * BLOCK, :]
        parts.append((kind, take(refs[k], row, k_col), take(refs[k], row, v_col), rows))
    qa = None if use_qatt is None else refs[use_qatt][:, q_row * BLOCK : (q_row + 1) * BLOCK]
    return q, parts, qa


def attend(idx, queries, segments, katt, qatt, heads, name):
    arrays, *uses = attention_inputs(queries, segments, katt, qatt)
    count = len(arrays)

    def body(s, *refs):
        o_ref, l_ref = refs[count:]

        @pl.loop(0, heads)
        def _(head):
            q, parts, qa = read_attention(refs, uses, queries, segments, head)
            scores = [masked_scores(kind, k, q, ka, qa) for kind, k, v, ka in parts]
            largest = functools.reduce(
                jnp.maximum, [jnp.max(x, axis=0, keepdims=True) for x in scores]
            )
            total = jnp.zeros_like(largest)
            mixed = jnp.zeros((HEAD, BLOCK), f32)
            for x, (kind, k, v, ka) in zip(scores, parts):
                raised = jnp.exp2((x - largest) * log2_scale)
                total = total + jnp.sum(raised, axis=0, keepdims=True)
                mixed = mixed + dot_tn(v, raised.astype(bf16))
            lanes = pl.ds(pl.multiple_of(head * HEAD, HEAD), HEAD)
            o_ref[:, lanes] = jnp.transpose(mixed * (1.0 / total)).astype(bf16)
            l_ref[head] = largest * log2_scale + jnp.log2(total)

    keys = BLOCK * len(segments)
    return launch(
        body,
        idx,
        arrays,
        [shaped((BLOCK, heads * HEAD), bf16), shaped((heads, 1, BLOCK), f32)],
        flops=4 * heads * BLOCK * keys * HEAD * 2,
        name=name,
    )


def attend_back(idx, queries, segments, katt, qatt, heads, logs, upstream, added, dtypes, name):
    arrays, *uses = attention_inputs(queries, segments, katt, qatt)
    count = len(arrays)
    inputs = arrays + [logs, upstream]
    for pairs in added:
        for pair in pairs:
            inputs.extend(pair)
    wide = (BLOCK, heads * HEAD)
    outputs = [shaped(wide, bf16)]
    for dtype in dtypes:
        outputs.extend([shaped(wide, dtype)] * 2)

    def body(s, *refs):
        rest = list(refs[count:])
        l_ref, go_ref = rest.pop(0), rest.pop(0)
        sums = []
        for pairs in added:
            sums.append([(rest.pop(0), rest.pop(0)) for unused in pairs])
        gq_ref = rest.pop(0)
        outs = list(zip(rest[0::2], rest[1::2]))

        @pl.loop(0, heads)
        def _(head):
            q, parts, qa = read_attention(refs, uses, queries, segments, head)
            lanes = pl.ds(pl.multiple_of(head * HEAD, HEAD), HEAD)
            log_total = l_ref[head]
            go = go_ref[:, lanes]
            chances, grads = [], []
            inner = jnp.zeros((1, BLOCK), f32)
            for kind, k, v, ka in parts:
                x = masked_scores(kind, k, q, ka, qa)
                chance = jnp.exp2(x * log2_scale - log_total)
                grad = dot_nt(v, go)
                inner = inner + jnp.sum(chance * grad, axis=0, keepdims=True)
                chances.append(chance)
                grads.append(grad)
            gq = jnp.zeros((HEAD, BLOCK), f32)
            for (kind, k, v, ka), chance, grad, pairs, out in zip(
                parts, chances, grads, sums, outs
            ):
                gl = (chance * (grad - inner)).astype(bf16)
                gk = dot_nn(gl, q) * score_scale
                gv = dot_nn(chance.astype(bf16), go)
                gq = gq + dot_tn(k, gl)
                for more_k, more_v in pairs:
                    gk = gk + more_k[:, lanes]
                    gv = gv + more_v[:, lanes]
                out[0][:, lanes] = gk.astype(out[0].dtype)
                out[1][:, lanes] = gv.astype(out[1].dtype)
            gq_ref[:, lanes] = jnp.transpose(gq * score_scale).astype(bf16)

    keys = BLOCK * len(segments)
    return launch(
        body,
        idx,
        inputs,
        outputs,
        flops=10 * heads * BLOCK * keys * HEAD * 2,
        vmem=20,
        name=name,
    )


def state_update(idx, pieces, write_pieces, state, retain, gain, weights, width, name):
    rows, features = state.shape
    count = len(pieces)
    project = weights is not None

    def body(s, *refs):
        refs = list(refs)
        piece_refs = [refs.pop(0) for unused in range(count)]
        w_refs = [refs.pop(0) for unused in range(count)]
        s_ref, r_ref = refs[:2]
        refs = refs[2:]
        if project:
            g_ref, p_ref, out_ref, n_ref, t_ref = refs
        else:
            (out_ref,) = refs

        @pl.loop(0, rows // TILE)
        def _(i):
            at = span(i * TILE)
            terms = [
                dot_nn(o_ref[at, :], w_ref[: o_ref.shape[1], :])
                for o_ref, w_ref in zip(piece_refs, w_refs)
            ]
            while len(terms) > 1:
                terms = [a + b for a, b in zip(terms[0::2], terms[1::2])]
            update = terms[0]
            keep = r_ref[...]
            following = keep * s_ref[at, :].astype(f32) + (1.0 - keep) * update
            out_ref[at, :] = following
            if project:
                normed = (unit_rows(following)[0] * g_ref[...]).astype(bf16)
                n_ref[at, :] = normed
                t_ref[at, :] = dot_nn(normed, p_ref[:, :width]).astype(bf16)

    inputs = list(pieces) + list(write_pieces) + [state, retain]
    outputs = [shaped((rows, features), f32)]
    if project:
        inputs += [gain, weights]
        outputs += [shaped((rows, features), bf16), shaped((rows, width), bf16)]
    return launch(
        body,
        idx,
        inputs,
        outputs,
        flops=2 * rows * features * (features + (width if project else 0)),
        name=name,
    )


def take_sum(i, s, refs, total):
    chip_ref, mine_ref, theirs_ref = refs
    steps = HALF // TILE
    at, inner = span(tile_start(i, s)), span(lax.rem(i, steps) * TILE)

    @pl.when(i < steps)
    def _():
        total[...] = chip_ref[at, :].astype(f32) + mine_ref[inner, :].astype(f32)

    @pl.when(i >= steps)
    def _():
        total[...] = chip_ref[at, :].astype(f32) + theirs_ref[inner, :].astype(f32)

    return total[...]


def chip_sum(idx, partial, other, name):
    rows, features = partial.shape
    tall = 32

    def body(s, a_ref, b_ref, sum_ref, own_ref):
        @pl.loop(0, rows // tall)
        def _(i):
            at = rows_of(i, 0, tall)
            sum_ref[at, :] = (a_ref[at, :].astype(f32) + b_ref[at, :].astype(f32)).astype(bf16)

        @pl.loop(0, HALF // tall)
        def _(i):
            own_ref[rows_of(i, 0, tall), :] = sum_ref[pl.ds(pl.multiple_of(s[1] * HALF + i * tall, tall), tall), :]

    return launch(
        body,
        idx,
        [partial, other],
        [shaped((rows, features), bf16), shaped((HALF, features), bf16)],
        name=name,
    )


def add_rows(i, ref, value):
    value = jnp.sum(value, axis=0, keepdims=True)

    @pl.when(i == 0)
    def _():
        ref[...] = value

    @pl.when(i != 0)
    def _():
        ref[...] = ref[...] + value


def project_back(idx, grads, weights, column, name):
    rows, width = grads[0].shape
    features = weights.shape[1]

    def body(s, *refs):
        *g_refs, w_ref, out_ref = refs

        @pl.loop(0, rows // TILE)
        def _(i):
            at = span(i * TILE)
            out = jnp.zeros((TILE, features), f32)
            for k, ref in enumerate(g_refs):
                first = column + k * width
                out = out + dot_nn(ref[at, :], w_ref[first : first + width, :])
            out_ref[at, :] = out.astype(bf16)

    return launch(
        body,
        idx,
        list(grads) + [weights],
        [shaped((rows, features), bf16)],
        flops=2 * rows * features * width * len(grads),
        name=name,
    )[0]


def state_back(idx, sums, state, following, retain, gain, write_own, name):
    rows, features = state.shape
    before = write_own is not None
    width = write_own.shape[1] // 2 if before else 10

    def body(s, *refs):
        refs = list(refs)
        total = refs.pop()
        sum_refs = [refs.pop(0) for unused in range(len(sums))]
        s_ref, r_ref, g_ref = refs[:3]
        refs = refs[3:]
        following_ref = refs.pop(0) if following is not None else None
        if before:
            w_ref, gs_ref, gain_ref, gu_ref, gos_ref = refs
        else:
            gs_ref, gain_ref = refs

        @pl.loop(0, rows // TILE)
        def _(i):
            at = span(tile_start(i, s))
            up = take_sum(i, s, sum_refs, total)
            unit, inverse = unit_rows(s_ref[at, :].astype(f32))
            out = unit_back(up, unit, inverse, g_ref[...])
            if following is not None:
                out = r_ref[...] * following_ref[at, :] + out
            gs_ref[at, :] = out
            add_rows(i, gain_ref, up * unit)
            if before:
                gu = ((1.0 - r_ref[...]) * out).astype(bf16)
                gu_ref[at, :] = gu
                gos_ref[at, :] = dot_nn(gu, w_ref[:, :width]).astype(bf16)

    inputs = list(sums) + [state, retain, gain]
    outputs = [shaped((rows, features), f32), shaped((1, features), f32)]
    if following is not None:
        inputs.append(following)
    if before:
        inputs.append(write_own)
        outputs += [shaped((rows, features), bf16), shaped((rows, width), bf16)]
    return launch(
        body,
        idx,
        inputs,
        outputs,
        scratch=[pltpu.VMEM((TILE, features), f32)],
        flops=2 * rows * features * width,
        name=name,
    )


def last_update_back(idx, retain, write_own, rows, name):
    features, width = write_own.shape[0], write_own.shape[1] // 2

    def body(s, r_ref, w_ref, gu_ref, gos_ref):
        gu = ((1.0 - r_ref[...]) * jnp.zeros((rows, features), f32)).astype(bf16)
        gu_ref[...] = gu
        gos_ref[...] = dot_nn(gu, w_ref[:, :width]).astype(bf16)

    return launch(
        body,
        idx,
        [retain, write_own],
        [shaped((rows, features), bf16), shaped((rows, width), bf16)],
        name=name,
    )


def gelu_both(a):
    root, cubic = 0.7978845608028654, 0.044715
    squared = a * a
    bent = jnp.tanh(root * (a + cubic * (squared * a)))
    rising = 0.5 * (1.0 + bent)
    slope = rising + (0.5 * root) * a * (1.0 - bent * bent) * (1.0 + (3.0 * cubic) * squared)
    return a * rising, slope


def output_forward(idx, number, pieces, out_pieces, tokens, gain, name):
    features = tokens.shape[1]
    count = len(pieces)

    def body(s, *refs):
        o_refs, w_refs = refs[:count], refs[count : 2 * count]
        t_ref, g_ref, x1_ref, xn_ref = refs[2 * count :]

        @pl.loop(0, BLOCK // TILE)
        def _(i):
            at = span(i * TILE)
            x1 = t_ref[span(i * TILE, number * BLOCK), :].astype(f32)
            for o_ref, w_ref in zip(o_refs, w_refs):
                x1 = x1 + dot_nn(o_ref[at, :], w_ref[o_ref.shape[1] :, :])
            x1_ref[at, :] = x1
            xn_ref[at, :] = (unit_rows(x1)[0] * g_ref[...]).astype(bf16)

    return launch(
        body,
        idx,
        list(pieces) + list(out_pieces) + [tokens, gain],
        [shaped((BLOCK, features), f32), shaped((BLOCK, features), bf16)],
        flops=2 * BLOCK * features * features,
        name=name,
    )


def dense_forward(idx, normed, dense, name):
    features = normed.shape[1]
    hidden = dense[1].shape[0]

    def body(s, n_ref, up_ref, down_ref, h_ref, slope_ref, part_ref):
        @pl.loop(0, BLOCK // TILE)
        def _(i):
            at = span(i * TILE)
            h, slope = gelu_both(dot_nn(n_ref[at, :], up_ref[:, :hidden]))
            h = h.astype(bf16)
            h_ref[at, :] = h
            slope_ref[at, :] = slope.astype(bf16)
            part_ref[at, :] = dot_nn(h, down_ref[...]).astype(bf16)

    return launch(
        body,
        idx,
        [normed, *dense],
        [
            shaped((BLOCK, hidden), bf16),
            shaped((BLOCK, hidden), bf16),
            shaped((BLOCK, features), bf16),
        ],
        flops=4 * BLOCK * features * hidden,
        name=name,
    )


def dense_backward(idx, number, sums, x1, teacher, katt, slope, dense, name):
    features = x1.shape[1]
    up_t, both = dense
    hidden = up_t.shape[0]

    def body(s, *refs):
        refs = list(refs)
        total = refs.pop()
        sum_refs = [refs.pop(0) for unused in range(len(sums))]
        x_ref, t_ref, v_ref, slope_ref, up_ref, d_ref = refs[:6]
        gm_ref, ga_ref, loss_ref, part_ref = refs[6:]

        @pl.loop(0, BLOCK // TILE)
        def _(i):
            start = tile_start(i, s)
            at, far = span(start), span(start, number * BLOCK)
            errors = x_ref[at, :] + take_sum(i, s, sum_refs, total) - t_ref[far, :].astype(f32)
            gy = v_ref[far, 2:3] * errors
            add_rows(i, loss_ref, gy * errors)
            gm = gy.astype(bf16)
            gm_ref[at, :] = gm
            ga = (dot_nn(gm, d_ref[:, hidden:]) * slope_ref[at, :].astype(f32)).astype(bf16)
            ga_ref[at, :] = ga
            part_ref[at, :] = dot_nn(ga, up_ref[...]).astype(bf16)

    return launch(
        body,
        idx,
        list(sums) + [x1, teacher, katt, slope, up_t, both],
        [
            shaped((BLOCK, features), bf16),
            shaped((BLOCK, hidden), bf16),
            shaped((1, features), f32),
            shaped((BLOCK, features), bf16),
        ],
        scratch=[pltpu.VMEM((TILE, features), f32)],
        flops=4 * BLOCK * features * hidden,
        name=name,
    )


def output_backward(idx, sums, gy, x1, gain, out_own, name):
    features = x1.shape[1]
    width = out_own.shape[1] // 2

    def body(s, *refs):
        refs = list(refs)
        total = refs.pop()
        sum_refs = [refs.pop(0) for unused in range(len(sums))]
        gy_ref, x_ref, g_ref, w_ref, gp_ref, go_ref, gain_ref = refs

        @pl.loop(0, BLOCK // TILE)
        def _(i):
            at = span(tile_start(i, s))
            up = take_sum(i, s, sum_refs, total)
            unit, inverse = unit_rows(x_ref[at, :])
            gx = gy_ref[at, :].astype(f32) + unit_back(up, unit, inverse, g_ref[...])
            gp = gx.astype(bf16)
            gp_ref[at, :] = gp
            go_ref[at, :] = dot_nn(gp, w_ref[:, width:]).astype(bf16)
            add_rows(i, gain_ref, up * unit)

    return launch(
        body,
        idx,
        list(sums) + [gy, x1, gain, out_own],
        [
            shaped((BLOCK, features), bf16),
            shaped((BLOCK, width), bf16),
            shaped((1, features), f32),
        ],
        scratch=[pltpu.VMEM((TILE, features), f32)],
        flops=2 * BLOCK * features * width,
        name=name,
    )


def weight_grads(idx, groups, name, before=None, weight=40):
    features = groups[0][0][0].shape[1]
    inputs, specs, total, flops = [], [], 0, 0
    for parts in groups:
        for left, block, right in parts:
            rows = right.shape[0]
            inputs += [left, right]
            specs.append(pl.BlockSpec((rows, HALF), lambda i, block=block: (block, i)))
            specs.append(
                pl.BlockSpec(right.shape, lambda i: (0, 0), pipeline_mode=pl.Buffered(1))
            )
            flops += 2 * rows * features * right.shape[1]
        total += parts[0][2].shape[1]
    if before is not None:
        inputs.append(before)
        specs.append(pl.BlockSpec((HALF, total), lambda i: (i, 0)))

    def body(s, *refs):
        refs = list(refs)
        out_ref = refs.pop()
        before_ref = refs.pop() if before is not None else None
        at = 0
        for parts in groups:
            size = parts[0][2].shape[1]
            if before is None:
                out = jnp.zeros((HALF, size), f32)
            else:
                out = before_ref[:, at : at + size].astype(f32)
            for unused in parts:
                left, right = refs.pop(0), refs.pop(0)
                out = out + dot_tn(left[...], right[...])
            out_ref[:, at : at + size] = out.astype(bf16)
            at += size

    return pl.pallas_call(
        body,
        grid=(features // HALF,),
        in_specs=[pl.BlockSpec(memory_space=pltpu.SMEM)] + specs,
        out_specs=pl.BlockSpec((HALF, total), lambda i: (i, 0)),
        out_shape=pltpu.HBM((features, total), bf16),
        compiler_params=pltpu.CompilerParams(
            dimension_semantics=("arbitrary",), vmem_limit_bytes=20 << 20
        ),
        cost_estimate=cost(weight * flops, inputs),
        name=name,
    )(idx, *inputs)


def unpack_grads(packed, widths, flipped, name):
    rows = packed.shape[0]

    def body(p_ref, *out_refs):
        at = 0
        for size, flip, out_ref in zip(widths, flipped, out_refs):
            values = p_ref[:, at : at + size].astype(f32)
            out_ref[...] = jnp.transpose(values) if flip else values
            at += size

    return pl.pallas_call(
        body,
        in_specs=[pl.BlockSpec(memory_space=pltpu.VMEM)],
        out_specs=[pl.BlockSpec(memory_space=pltpu.VMEM)] * len(widths),
        out_shape=[
            shaped((size, rows) if flip else (rows, size), f32)
            for size, flip in zip(widths, flipped)
        ],
        compiler_params=pltpu.CompilerParams(vmem_limit_bytes=8 << 20),
        cost_estimate=cost(0, [packed]),
        name=name,
    )(packed)


def arrange_rows(idx, pieces, count, name):
    rows, features = pieces[0].shape
    rows = rows // count

    def body(s, *refs):
        ins, outs = refs[: len(pieces)], refs[len(pieces) :]
        for k, ref in enumerate(ins):
            for j, out_ref in enumerate(outs):
                out_ref[rows_of(s[0] ^ k, 0, rows), :] = ref[j * rows : (j + 1) * rows, :]

    return launch(
        body,
        idx,
        pieces,
        [shaped((rows * len(pieces), features), pieces[0].dtype)] * count,
        name=name,
    )


def turn(idx, values, first, count, name):
    rows = values.shape[0]
    wide = 256

    def body(s, v_ref, out_ref):
        @pl.loop(0, count // wide)
        def _(i):
            lanes = pl.ds(pl.multiple_of(first + i * wide, HEAD), wide)
            out_ref[rows_of(i, 0, wide), :] = jnp.transpose(v_ref[:, lanes])

    return launch(body, idx, [values], [shaped((count, rows), values.dtype)], name=name)[0]


def arrange_columns(idx, blocks, across, name):
    rows, width = blocks[0].shape
    depth = len(blocks)

    def body(s, *refs):
        out_ref = refs[-1]
        for k in range(depth):
            level = lax.rem(s[3] + depth - k, depth)
            out_ref[rows_of(2 * level + s[4], 0, rows), :] = refs[k][...]
            out_ref[rows_of(2 * level + 1 - s[4], 0, rows), :] = refs[depth + k][...]

    return launch(
        body,
        idx,
        list(blocks) + list(across),
        [shaped((2 * depth * rows, width), blocks[0].dtype)],
        name=name,
    )[0]


def split_grads(idx, groups, depth, name):
    features = groups[0][0][0].shape[1]
    rows = features // (2 * depth)
    total = sum(parts[0][2].shape[1] for parts in groups)
    inputs = []

    def place(array):
        for k, known in enumerate(inputs):
            if known is array:
                return k
        inputs.append(array)
        return len(inputs) - 1

    uses = [[(place(a), block, place(c)) for a, block, c in parts] for parts in groups]

    def body(s, *refs):
        *ins, theirs_ref, mine_ref, held = refs

        @pl.loop(0, depth)
        def _(i):
            lanes = pl.ds(pl.multiple_of(i * 2 * rows, 2 * rows), 2 * rows)
            at = 0
            for parts in uses:
                size = ins[parts[0][2]].shape[1]
                out = jnp.zeros((2 * rows, size), f32)
                for left, block, right in parts:
                    count = ins[right].shape[0]
                    tall = slice(block * count, (block + 1) * count)
                    out = out + dot_tn(ins[left][tall, lanes], ins[right][...])
                held[:, at : at + size] = out.astype(bf16)
                at += size
            mine_ref[rows_of(i, 0, rows), :] = held[rows_of(s[4], 0, rows), :]
            theirs_ref[rows_of(i, 0, rows), :] = held[rows_of(1 - s[4], 0, rows), :]

    return launch(
        body,
        idx,
        inputs,
        [shaped((depth * rows, total), bf16)] * 2,
        scratch=[pltpu.VMEM((2 * rows, total), bf16)],
        name=name,
    )


def pair_blocks(idx, mine, got, depth, name):
    rows, width = mine.shape[0] // depth, mine.shape[1]

    def body(s, mine_ref, got_ref, *out_refs):
        for k, ref in enumerate(out_refs):
            at = rows_of(lax.rem(s[3] + k, depth), 0, rows)
            ref[...] = (mine_ref[at, :].astype(f32) + got_ref[at, :].astype(f32)).astype(ref.dtype)

    return launch(
        body,
        idx,
        [mine, got],
        [shaped((rows, width), f32)] + [shaped((rows, width), bf16)] * (depth - 1),
        name=name,
    )


def line_sum(idx, own, others, widths, flipped, name):
    rows = own.shape[0]

    def body(s, own_ref, *refs):
        ins, outs = refs[: len(others)], refs[len(others) :]
        total = own_ref[...]
        for ref in ins:
            total = total + ref[...].astype(f32)
        at = 0
        for size, flip, out_ref in zip(widths, flipped, outs):
            values = total[:, at : at + size]
            out_ref[...] = jnp.transpose(values) if flip else values
            at += size

    return launch(
        body,
        idx,
        [own] + list(others),
        [
            shaped((size, rows) if flip else (rows, size), f32)
            for size, flip in zip(widths, flipped)
        ],
        name=name,
    )


def pack(idx, arrays, takes, shapes, name):
    flipped = [take for take in takes if take[-1]]

    def body(s, *refs):
        ins, outs = refs[: len(arrays)], refs[len(arrays) : len(arrays) + len(shapes)]
        *held, sems = refs[len(arrays) + len(shapes) :]
        copies, spare = [], list(held)
        for j, (k, row, col, rows, cols, out, place, flip) in enumerate(takes):
            at = pl.ds(0, rows) if row is None else rows_of(s[row], 0, rows)
            to = pl.ds(0, cols) if col is None else rows_of(s[col], 0, cols)
            if flip:
                target = spare.pop(0)
            else:
                target = outs[out].at[pl.ds(place[0], rows), pl.ds(place[1], cols)]
            copies.append(pltpu.make_async_copy(ins[k].at[at, to], target, sems.at[j]))
            copies[-1].start()
        spare = list(held)
        for copy, (k, row, col, rows, cols, out, place, flip) in zip(copies, takes):
            copy.wait()
            if flip:
                to = slice(place[1], place[1] + rows)
                outs[out][place[0] : place[0] + cols, to] = jnp.transpose(spare.pop(0)[...])

    return pl.pallas_call(
        body,
        in_specs=[pl.BlockSpec(memory_space=pltpu.SMEM)]
        + [pl.BlockSpec(memory_space=pl.ANY)] * len(arrays),
        out_specs=[pl.BlockSpec(memory_space=pltpu.VMEM)] * len(shapes),
        out_shape=[shaped(a, bf16) for a in shapes],
        scratch_shapes=[pltpu.VMEM((take[3], take[4]), bf16) for take in flipped]
        + [pltpu.SemaphoreType.DMA((len(takes),))],
        compiler_params=pltpu.CompilerParams(vmem_limit_bytes=8 << 20),
        cost_estimate=cost(0, arrays),
        name=name,
    )(idx, *[pltpu.with_memory_space_constraint(a, pltpu.HBM) for a in arrays])


def input_rows(idx, own, arrived, gps, tokens, gain, name):
    rows, features = tokens.shape
    count = len(gps)

    def body(s, *refs):
        own_refs, far_refs, gp_refs = refs[:count], refs[count : 2 * count], refs[2 * count : 3 * count]
        t_ref, g_ref, out_ref, gain_ref = refs[3 * count :]
        unit, inverse = unit_rows(t_ref[...].astype(f32))
        for b in range(count):

            @pl.when(s[2] // 2 == b)
            def _():
                at = rows_of(s[1])
                up = own_refs[b][at, :].astype(f32) + far_refs[b][...].astype(f32)
                base = gp_refs[b][rows_of(s[1]), :].astype(f32)
                out_ref[...] = base + unit_back(up, unit, inverse, g_ref[...])
                gain_ref[...] = jnp.sum(up * unit, axis=0, keepdims=True)

    return launch(
        body,
        idx,
        list(own) + list(arrived) + list(gps) + [tokens, gain],
        [shaped((rows, features), f32), shaped((1, features), f32)],
        name=name,
    )


def per_device(
    block_input,
    state_start,
    teacher,
    valid_mask,
    segment,
    image_offset,
    retain,
    to_query,
    to_key,
    to_value,
    to_output,
    to_hidden,
    to_model,
    state_query,
    state_key,
    state_value,
    state_write,
    first_gain,
    second_gain,
    state_gain,
):
    row_devices = lax.axis_size("row")
    col_devices = lax.axis_size("col")
    row_index = lax.axis_index("row")
    col_index = lax.axis_index("col")
    local_rows, features = block_input.shape[1:]
    length = local_rows * row_devices
    width = to_query.shape[1]
    heads = width // HEAD
    hidden = to_hidden.shape[1] // row_devices
    nblocks = length // BLOCK
    pairs = row_devices == 4 and 2 * local_rows == BLOCK
    lines = pairs and col_devices == 8
    core_pairs = [(k, k ^ 1) for k in range(row_devices)]
    chip_pairs = [(k, k ^ 2) for k in range(row_devices)] if pairs else None
    if pairs:
        idx = jnp.stack([row_index, row_index % 2, row_index, col_index // 2, col_index % 2])
    else:
        idx = jnp.stack([0, 1, row_index, 0, 0])
    idx = idx.astype(jnp.int32)

    def to_core(x):
        return lax.ppermute(x, "row", core_pairs)

    def to_chip(x):
        return lax.ppermute(x, "row", chip_pairs)

    def row_moves(x):
        if not pairs:
            stacked = lax.all_gather(x, "row", axis=0, tiled=False)
            return [stacked[k] for k in range(row_devices)]
        return [x, to_core(x), to_chip(x)]

    def row_pieces(moved, *ties):
        if not pairs:
            return moved
        x, near, far = moved
        return [x, near, far, to_core(after(far, *ties))]

    depth_z = col_devices // 2

    def along(v, step):
        levels = range(depth_z)
        moves = [(2 * z + y, 2 * ((z + step) % depth_z) + y) for z in levels for y in range(2)]
        return lax.ppermute(v, "col", moves)

    def across(v):
        return lax.ppermute(v, "col", [(k, k ^ 1) for k in range(col_devices)])

    class Columns:
        def __init__(self, x, name):
            self.name = name
            if lines:
                self.blocks = [x] + [along(x, k) for k in range(1, depth_z)]
                self.crossed = [across(x)]
            else:
                self.whole = lax.all_gather(x, "col", axis=0, tiled=True)

        def cross(self, k, *ties):
            if lines:
                self.crossed.append(across(after(self.blocks[k], *ties)))

        def landed(self, k):
            return [self.blocks[k], self.crossed[k - 1]] if lines else []

        def result(self, *ties):
            if lines:
                order = after(idx, *ties)
                return arrange_columns(order, self.blocks, self.crossed, self.name)
            return self.whole

    class Scattered:
        def __init__(self, groups, name, *ties):
            self.name, self.widths = name, [parts[0][2].shape[1] for parts in groups]
            if lines:
                order = after(idx, *ties) if ties else idx
                theirs, self.mine = split_grads(order, groups, depth_z, name)
                self.got = across(theirs)
            else:
                packed = weight_grads(idx, groups, name)
                self.whole = lax.psum_scatter(packed, "col", scatter_dimension=0, tiled=True)

        def send(self, *ties):
            if lines:
                mine = after(self.mine, *ties) if ties else self.mine
                self.own, *blocks = pair_blocks(idx, mine, self.got, depth_z, f"{self.name}_y")
                self.far = [along(block, k + 1) for k, block in enumerate(blocks)]

        def result(self, flipped):
            if lines:
                return line_sum(idx, self.own, self.far, self.widths, flipped, f"{self.name}_z")
            return unpack_grads(self.whole, self.widths, flipped, f"{self.name}_z")

    class RowSum:
        def __init__(self, partial, name, receiver=None, ties=()):
            if pairs:
                order = after(idx, *ties) if ties else idx
                self.chip, own = chip_sum(order, partial, to_core(partial), name)
                moves = [m for m in chip_pairs if receiver is None or m[1] // 2 == receiver]
                self.far = lax.ppermute(own, "row", moves)
            else:
                self.chip = lax.psum(partial, "row")

        def result(self, *ties):
            if pairs:
                return [self.chip, self.far, to_core(after(self.far, *ties))]
            none = jnp.zeros((HALF, features), bf16)
            return [self.chip, none, none]

    def all_sum(x):
        for axis, size in (("row", row_devices), ("col", col_devices)):
            step = 1
            while step < size:
                x = x + lax.ppermute(x, axis, [(k, k ^ step) for k in range(size)])
                step *= 2
        return x

    depth = to_query.shape[0]
    (near,) = pack(
        idx,
        [state_query, state_key, state_value, to_query, to_key, to_value],
        [(k, None, None, depth, width, 0, (0, k * width), False) for k in range(6)],
        [(depth, 6 * width)],
        "pack_near",
    )
    near = lax.all_gather(near, "col", axis=0, tiled=True)
    rows_in, mid, far_weights = pack(
        idx,
        [state_write, to_output, to_hidden, to_model, block_input[0], teacher[0]],
        [
            (4, None, None, local_rows, features, 0, (0, 0), False),
            (5, None, None, local_rows, features, 0, (local_rows, 0), False),
            (0, 2, None, width, depth, 1, (0, 0), True),
            (1, None, None, width, depth, 1, (0, width), True),
            (2, None, 2, depth, hidden, 2, (0, 0), False),
            (3, 2, None, hidden, depth, 2, (0, hidden), True),
        ],
        [(2 * local_rows, features), (depth, 2 * width), (depth, 2 * hidden)],
        "pack_rest",
    )
    rows_moved = row_moves(rows_in) if pairs else None
    mid = Columns(mid, "mid")
    for k in range(1, depth_z):
        mid.cross(k)
    mid = mid.result()
    mid_n = turn(idx, mid, 0, 2 * width, "mid_turn")
    held = [mid_n] + (rows_moved[2:] if pairs else [])
    dense = lax.all_gather(after(far_weights, *held), "col", axis=0, tiled=True)
    mid_moved = row_moves(mid_n)
    if pairs:
        tokens, teacher_all = arrange_rows(idx, row_pieces(rows_moved), 2, "tokens")
    else:
        tokens, teacher_all = [
            lax.all_gather(x[0], "row", axis=0, tiled=True) for x in (block_input, teacher)
        ]

    valid_row = lax.dynamic_index_in_dim(valid_mask, col_index, 0, keepdims=False)
    segment_row = segment[0]
    numbers = jnp.arange(nblocks, dtype=jnp.int32)
    places = jnp.arange(length, dtype=jnp.int32)
    starts = numbers * BLOCK + image_offset[0]
    inside = (places[:, None] >= starts[None, :]) & (places[:, None] < starts[None, :] + PIECE)
    piece = jnp.sum(jnp.where(inside, numbers[None, :] + 1, 0), axis=1) - 1
    valid_count = jnp.sum(valid_mask.astype(f32))
    total_tokens = f32(length * col_devices)
    weight_of_row = total_tokens / valid_count * valid_row.astype(f32)
    document = segment_row.astype(f32)
    nothing = jnp.zeros_like(document)
    katt = jnp.stack(
        [jnp.where(valid_row > 0, document, -1.0), piece.astype(f32), weight_of_row, nothing],
        axis=1,
    )
    qatt = jnp.stack(
        [document, jnp.where(piece >= 0, piece, -2).astype(f32), nothing, nothing], axis=0
    )
    retain2 = retain[None]
    first_gain2, second_gain2, state_gain2 = first_gain[None], second_gain[None], state_gain[None]

    def token_segments(number, trio):
        found = []
        if number > 0:
            found.append(("prev", token_heads, number - 1, width, 2 * width, number - 1))
        found.append(("own", token_heads, number, width, 2 * width, number))
        found.append(("free", trio, 0, width, 2 * width, None))
        return found

    def state_segments(number, trio):
        return [
            ("valid", token_heads, number, width, 2 * width, number),
            ("free", trio, 0, width, 2 * width, None),
        ]

    current = state_start[0]
    near_t = turn(idx, near, 0, 6 * width, "near_turn")
    state_low, trio = norm_project(after(idx, near_t), current, state_gain2, near, 0, 3 * width, "state_proj")
    first_low, token_heads = norm_project(
        idx, tokens, first_gain2, near, 3 * width, 3 * width, "token_proj"
    )
    states, lows, trios = [], [], []
    state_out, state_logs, token_out, token_logs = [], [], [], []
    x1s, second_lows, hiddens, slopes, dense_sums = [], [], [], [], []
    state_pieces, token_pieces = [], []
    end = nblocks - 1

    def state_part(b):
        mixed, logs = attend(
            idx,
            (trios[b], 0, 0),
            state_segments(b, trios[b]),
            katt,
            None,
            heads,
            f"state_attend{b}",
        )
        state_out.append(mixed)
        state_logs.append(logs)
        state_pieces.append(row_moves(mixed) if b < nblocks - 1 else None)

    for b in range(nblocks):
        states.append(current)
        lows.append(state_low)
        trios.append(trio)
        last = b + 1 == nblocks
        if not last:
            state_part(b)
        mixed, logs = attend(
            idx, (token_heads, b, 0), token_segments(b, trio), katt, qatt, heads, f"token_attend{b}"
        )
        if b == 0:
            mid_pieces = row_pieces(mid_moved, mixed)
        token_out.append(mixed)
        token_logs.append(logs)
        token_pieces.append(row_moves(mixed))
        if not last:
            current, state_low, trio = state_update(
                idx,
                row_pieces(state_pieces[b], mixed),
                mid_pieces,
                current,
                retain2,
                state_gain2,
                near,
                3 * width,
                f"update{b}",
            )
            token_pieces[b] = row_pieces(token_pieces[b], trio)
    state_part(nblocks - 1)
    token_pieces[-1] = row_pieces(token_pieces[-1], state_out[-1])

    def state_back_part(b, gos_state, own, free, dtype):
        return attend_back(
            idx,
            (trios[b], 0, 0),
            state_segments(b, trios[b]),
            katt,
            None,
            heads,
            state_logs[b],
            gos_state,
            [own, free],
            [dtype, dtype],
            f"state_back{b}",
        )

    def token_back_part(b, own, free, dtype, upstream):
        segments = token_segments(b, trios[b])
        added = ([[]] if b > 0 else []) + [own, free]
        dtypes = ([f32] if b > 0 else []) + [dtype, dtype]
        found = attend_back(
            idx,
            (token_heads, b, 0),
            segments,
            katt,
            qatt,
            heads,
            token_logs[b],
            upstream,
            added,
            dtypes,
            f"token_back{b}",
        )
        return found[0], found[-4:], (found[1], found[2]) if b > 0 else None

    gus = [None] * nblocks
    gms, gas, losses, gps, gos, second_sums = [], [], [], [], [], []
    second_back = []
    for b in range(nblocks):
        x1, low = output_forward(
            idx, b, token_pieces[b], mid_pieces, tokens, second_gain2, f"out{b}"
        )
        x1s.append(x1)
        second_lows.append(low)
    down = turn(after(idx, state_out[-1], *second_lows), dense, hidden, hidden, "down_turn")
    order = idx
    for b in range(nblocks):
        h, slope, partial = dense_forward(order, second_lows[b], (dense, down), f"dense{b}")
        hiddens.append(h)
        slopes.append(slope)
        ties = []
        if b == 0:
            up_t = turn(after(idx, h), dense, 0, hidden, "up_turn")
            ties.append(up_t)
        if b == end:
            late_mid = after(mid, h)
            gus[end], gos_state = last_update_back(idx, retain2, late_mid, NS, "last_back")
            state_found = state_back_part(end, gos_state, [], [], f32)
            ties.append(state_found[0])
        dense_sums.append(RowSum(partial, f"dense_sum{b}", ties=ties))
        order = after(idx, dense_sums[b].chip)

    early_grads, partials = [], []
    ready = teacher_all
    for b in range(nblocks):
        hides = [hiddens[end], state_found[0]] if b == 0 else [gms[b - 1]] + early_grads
        gm, ga, loss, partial = dense_backward(
            idx, b, dense_sums[b].result(*hides), x1s[b], ready, katt, slopes[b], (up_t, dense), f"back{b}"
        )
        gms.append(gm)
        gas.append(ga)
        losses.append(loss)
        if b < end:
            early_grads = [
                weight_grads(
                    idx,
                    [[(second_lows[b], 0, ga)], [(gm, 0, hiddens[b])]],
                    f"dense_grads{b}",
                    *early_grads,
                )
            ]
        partials.append(partial)
        if b > 0:
            second_back.append(RowSum(partials[b - 1], f"back_sum{b - 1}", ties=[gm]))
            ready = after(teacher_all, second_back[b - 1].chip)
    dense_grads = weight_grads(
        idx,
        [[(second_lows[end], 0, gas[end])], [(gms[end], 0, hiddens[end])]],
        "dense_grads",
        *early_grads,
    )
    filled = [dense_grads]
    ties = [dense_grads] + [back.far for back in second_back] if pairs else []
    second_back.append(RowSum(partial, f"back_sum{end}", ties=ties))
    dense_grads = lax.psum_scatter(dense_grads, "col", scatter_dimension=0, tiled=True)

    token_found = [None] * nblocks
    for b in range(nblocks):
        gp, go, gain_sum = output_backward(
            idx,
            second_back[b].result(*(filled if b == end else [gms[end]])),
            gms[b],
            x1s[b],
            second_gain2,
            mid,
            f"out_back{b}",
        )
        gps.append(gp)
        gos.append(go)
        second_sums.append(gain_sum)
        if b < end:
            token_found[b] = token_back_part(b, [], [], f32, go)
            filled.append(token_found[b][0])
    trio_grads = [None] * nblocks
    token_grads = [None] * nblocks
    first_sums = [None] * nblocks
    gain_sums = []
    grad_next = None
    gqs, gk, gv, gks, gvs = state_found
    gq, (gk, gv, gks, gvs), key_part = token_back_part(
        end, [(gk, gv)], [(gks, gvs)], bf16, gos[end]
    )
    state_pieces[-1] = row_moves(after(state_out[-1], gos[end]))
    gqs = after(gqs, state_pieces[-1][2])
    trio_grads[end] = (gqs, gks, gvs)
    token_grads[end] = (gq, gk, gv)
    for b in reversed(range(nblocks)):
        order = idx
        if b == 0:

            def state_group(k):
                return [(lows[c], 0, trio_grads[c][k]) for c in range(nblocks)]

            def token_group(k):
                return [(first_low, c, token_grads[c][k]) for c in range(nblocks)]

            write_group = [(gu, 0, out) for gu, out in zip(gus, state_out)]
            late_grads = weight_grads(
                idx,
                [state_group(k) for k in range(3)] + [token_group(1), token_group(2)],
                "late_grads",
                weight=130,
            )
            order = after(idx, late_grads)
            rest_grads = Scattered(
                [token_group(0), [(gp, 0, out) for gp, out in zip(gps, token_out)], write_group],
                "rest_grads",
                late_grads,
            )
            rest_grads.send()
            late_grads = lax.psum_scatter(late_grads, "col", scatter_dimension=0, tiled=True)
        trio_sum = RowSum(
            project_back(order, trio_grads[b], near_t, 0, f"trio_back{b}"),
            f"trio_sum{b}",
        )
        hides = []
        if b == end:
            (final_state,) = state_update(
                idx,
                row_pieces(state_pieces[-1], gq),
                mid_pieces,
                current,
                retain2,
                None,
                None,
                0,
                "update_last",
            )
            hides.append(final_state)
        first_sums[b] = project_back(idx, token_grads[b], near_t, 3 * width, f"first_back{b}")
        hides.append(first_sums[b])
        first_sums[b] = RowSum(first_sums[b], f"first_sum{b}", b) if pairs else first_sums[b]
        if b > 0:
            grad_next, gain_sum, gus[b - 1], gos_state = state_back(
                idx,
                trio_sum.result(*hides),
                states[b],
                grad_next,
                retain2,
                state_gain2,
                mid,
                f"chain_back{b}",
            )
            gq, (gk, gv, gks, gvs), next_part = token_found[b - 1]
            gqs, gk, gv, gks, gvs = state_back_part(
                b - 1, gos_state, [(gk, gv), key_part], [(gks, gvs)], bf16
            )
            key_part = next_part
            trio_grads[b - 1] = (gqs, gks, gvs)
            token_grads[b - 1] = (gq, gk, gv)
        else:
            grad_next, gain_sum = state_back(
                after(idx, rest_grads.own) if lines else idx,
                trio_sum.result(*hides),
                states[b],
                grad_next,
                retain2,
                state_gain2,
                None,
                "chain_back0",
            )
        gain_sums.append(gain_sum)

    if pairs:
        own_rows = [first.chip for first in first_sums]
        arrived = [first.far for first in first_sums]
        input_grad, first_sum = input_rows(
            idx, own_rows, arrived, gps, block_input[0], first_gain2, "input_rows"
        )
        first_sum = first_sum[0]
    else:
        both = jnp.concatenate(first_sums)
        grad_first = lax.psum_scatter(both, "row", scatter_dimension=0, tiled=True).astype(f32)
        own_gx1 = lax.dynamic_slice_in_dim(
            jnp.concatenate(gps), row_index * local_rows, local_rows
        ).astype(f32)
        unit, inverse = unit_rows(block_input[0].astype(f32))
        input_grad = own_gx1 + unit_back(grad_first, unit, inverse, first_gain2)
        first_sum = jnp.sum(grad_first * unit, axis=0)

    share = 1.0 / row_devices
    sums = jnp.stack(
        [
            sum(losses)[0] * share,
            first_sum,
            sum(second_sums)[0] * share,
            sum(gain_sums)[0] * share,
        ]
    )
    if lines:
        sums = after(sums, *rest_grads.far)
    summed = all_sum(sums)
    total_loss = jnp.sum(summed[0]) / (2.0 * total_tokens)

    upper_grad, lower_grad = unpack_grads(
        dense_grads, [hidden, hidden], [False, True], "unpack_dense"
    )
    late = unpack_grads(late_grads, [width] * 5, [False] * 5, "unpack_late")
    rest = rest_grads.result([False, True, True])

    return (
        total_loss,
        final_state[None],
        input_grad[None],
        grad_next[None],
        rest[0],
        late[3],
        late[4],
        rest[1],
        upper_grad,
        lower_grad,
        late[0],
        late[1],
        late[2],
        rest[2],
        summed[1],
        summed[2],
        summed[3],
    )


def solution(mesh):
    in_specs = (
        P("col", "row", None),
        P("col", None, None),
        P("col", "row", None),
        P(),
        P("col", None),
        P("col", None),
        P(),
        P("col", "row"),
        P("col", "row"),
        P("col", "row"),
        P("row", "col"),
        P("col", None),
        P(None, "col"),
        P("col", "row"),
        P("col", "row"),
        P("col", "row"),
        P(None, "col"),
        P(),
        P(),
        P(),
    )
    out_specs = (
        P(),
        P("col", None, None),
        P("col", "row", None),
        P("col", None, None),
        P("col", "row"),
        P("col", "row"),
        P("col", "row"),
        P("row", "col"),
        P("col", "row"),
        P("row", "col"),
        P("col", "row"),
        P("col", "row"),
        P("col", "row"),
        P("row", "col"),
        P(),
        P(),
        P(),
    )
    return jax.shard_map(
        per_device, mesh=mesh, in_specs=in_specs, out_specs=out_specs, check_vma=False
    )
```

```python
import functools

import jax
import jax.numpy as jnp
from jax import lax
from jax.experimental import pallas as pl
from jax.experimental.pallas import tpu as pltpu
from jax.sharding import PartitionSpec as P

HEAD = 128
BLOCK = 512
HALF = 256
NS = 512
PIECE = 256
COST = 8
TILE = 256

epsilon = 1e-06
masked_value = -1e30
score_scale = HEAD ** (-0.5)
log2_scale = score_scale * 1.4426950408889634
f32 = jnp.float32
bf16 = jnp.bfloat16


def dot_nn(a, b):
    return lax.dot_general(a, b, (((1,), (0,)), ((), ())), preferred_element_type=f32)


def dot_nt(a, b):
    return lax.dot_general(a, b, (((1,), (1,)), ((), ())), preferred_element_type=f32)


def dot_tn(a, b):
    return lax.dot_general(a, b, (((0,), (0,)), ((), ())), preferred_element_type=f32)


def cost(flops, arrays):
    return pl.CostEstimate(flops=flops // COST, bytes_accessed=1024, transcendentals=0)


def after(x, *earlier):
    return lax.optimization_barrier((x,) + earlier)[0]


def shaped(shape, dtype):
    return jax.ShapeDtypeStruct(shape, dtype)


def launch(body, idx, inputs, outputs, scratch=(), flops=0, vmem=8, name=None):
    return pl.pallas_call(
        body,
        in_specs=[pl.BlockSpec(memory_space=pltpu.SMEM)]
        + [pl.BlockSpec(memory_space=pltpu.VMEM)] * len(inputs),
        out_specs=[pl.BlockSpec(memory_space=pltpu.VMEM)] * len(outputs),
        out_shape=list(outputs),
        scratch_shapes=list(scratch),
        compiler_params=pltpu.CompilerParams(vmem_limit_bytes=vmem << 20),
        cost_estimate=cost(flops, inputs),
        name=name,
    )(idx, *inputs)


def rows_of(i, base=0, size=HALF):
    return pl.ds(pl.multiple_of(base + i * size, size), size)


def tile_start(i, s):
    steps = HALF // TILE
    return lax.rem(i // steps + s[1], 2) * HALF + lax.rem(i, steps) * TILE


def span(start, base=0):
    return pl.ds(pl.multiple_of(base + start, TILE), TILE)


def unit_rows(x):
    inverse = lax.rsqrt(jnp.mean(x * x, axis=-1, keepdims=True) + epsilon)
    return x * inverse, inverse


def unit_back(up, unit, inverse, gain):
    scaled = up * gain
    inner = jnp.mean(scaled * unit, axis=-1, keepdims=True)
    return inverse * (scaled - unit * inner)


def norm_project(idx, values, gain, weights, column, width, name):
    rows, features = values.shape

    def body(s, x_ref, g_ref, w_ref, n_ref, p_ref):
        @pl.loop(0, rows // TILE)
        def _(i):
            at = span(i * TILE)
            unit, unused = unit_rows(x_ref[at, :].astype(f32))
            normed = (unit * g_ref[...]).astype(bf16)
            n_ref[at, :] = normed
            p_ref[at, :] = dot_nn(normed, w_ref[:, column : column + width]).astype(bf16)

    return launch(
        body,
        idx,
        [values, gain, weights],
        [shaped((rows, features), bf16), shaped((rows, width), bf16)],
        flops=2 * rows * features * width,
        name=name,
    )


def masked_scores(kind, keys, queries, katt, qatt):
    scores = dot_nt(keys, queries)
    if kind == "free":
        return scores
    if kind == "valid":
        return jnp.where(katt[:, 2:3] > 0.0, scores, masked_value)
    places = lax.broadcasted_iota(jnp.int32, scores.shape, 0)
    asking = lax.broadcasted_iota(jnp.int32, scores.shape, 1)
    same = katt[:, 0:1] == qatt[0:1, :]
    if kind == "prev":
        allowed = same & (places > asking)
    else:
        allowed = same & ((places <= asking) | (katt[:, 1:2] == qatt[1:2, :]))
    return jnp.where(allowed, scores, masked_value)


def attention_inputs(queries, segments, katt, qatt):
    arrays = []

    def place(array):
        for k, known in enumerate(arrays):
            if known is array:
                return k
        arrays.append(array)
        return len(arrays) - 1

    use_q = place(queries[0])
    use_k = [place(segment[1]) for segment in segments]
    use_att = place(katt)
    use_qatt = place(qatt) if qatt is not None else None
    return arrays, use_q, use_k, use_att, use_qatt


def read_attention(refs, uses, queries, segments, head):
    use_q, use_k, use_att, use_qatt = uses
    unused, q_row, q_col = queries

    def take(ref, row, col):
        lanes = pl.ds(pl.multiple_of(col + head * HEAD, HEAD), HEAD)
        return ref[row * BLOCK : (row + 1) * BLOCK, lanes]

    q = take(refs[use_q], q_row, q_col)
    parts = []
    for (kind, unused, row, k_col, v_col, att), k in zip(segments, use_k):
        rows = None if att is None else refs[use_att][att * BLOCK : (att + 1) * BLOCK, :]
        parts.append((kind, take(refs[k], row, k_col), take(refs[k], row, v_col), rows))
    qa = None if use_qatt is None else refs[use_qatt][:, q_row * BLOCK : (q_row + 1) * BLOCK]
    return q, parts, qa


def attend(idx, queries, segments, katt, qatt, heads, name):
    arrays, *uses = attention_inputs(queries, segments, katt, qatt)
    count = len(arrays)

    def body(s, *refs):
        o_ref, l_ref = refs[count:]

        @pl.loop(0, heads)
        def _(head):
            q, parts, qa = read_attention(refs, uses, queries, segments, head)
            scores = [masked_scores(kind, k, q, ka, qa) for kind, k, v, ka in parts]
            largest = functools.reduce(
                jnp.maximum, [jnp.max(x, axis=0, keepdims=True) for x in scores]
            )
            total = jnp.zeros_like(largest)
            mixed = jnp.zeros((HEAD, BLOCK), f32)
            for x, (kind, k, v, ka) in zip(scores, parts):
                raised = jnp.exp2((x - largest) * log2_scale)
                total = total + jnp.sum(raised, axis=0, keepdims=True)
                mixed = mixed + dot_tn(v, raised.astype(bf16))
            lanes = pl.ds(pl.multiple_of(head * HEAD, HEAD), HEAD)
            o_ref[:, lanes] = jnp.transpose(mixed * (1.0 / total)).astype(bf16)
            l_ref[head] = largest * log2_scale + jnp.log2(total)

    keys = BLOCK * len(segments)
    return launch(
        body,
        idx,
        arrays,
        [shaped((BLOCK, heads * HEAD), bf16), shaped((heads, 1, BLOCK), f32)],
        flops=4 * heads * BLOCK * keys * HEAD * 2,
        name=name,
    )


def attend_back(idx, queries, segments, katt, qatt, heads, logs, upstream, added, dtypes, name):
    arrays, *uses = attention_inputs(queries, segments, katt, qatt)
    count = len(arrays)
    inputs = arrays + [logs, upstream]
    for pairs in added:
        for pair in pairs:
            inputs.extend(pair)
    wide = (BLOCK, heads * HEAD)
    outputs = [shaped(wide, bf16)]
    for dtype in dtypes:
        outputs.extend([shaped(wide, dtype)] * 2)

    def body(s, *refs):
        rest = list(refs[count:])
        l_ref, go_ref = rest.pop(0), rest.pop(0)
        sums = []
        for pairs in added:
            sums.append([(rest.pop(0), rest.pop(0)) for unused in pairs])
        gq_ref = rest.pop(0)
        outs = list(zip(rest[0::2], rest[1::2]))

        @pl.loop(0, heads)
        def _(head):
            q, parts, qa = read_attention(refs, uses, queries, segments, head)
            lanes = pl.ds(pl.multiple_of(head * HEAD, HEAD), HEAD)
            log_total = l_ref[head]
            go = go_ref[:, lanes]
            chances, grads = [], []
            inner = jnp.zeros((1, BLOCK), f32)
            for kind, k, v, ka in parts:
                x = masked_scores(kind, k, q, ka, qa)
                chance = jnp.exp2(x * log2_scale - log_total)
                grad = dot_nt(v, go)
                inner = inner + jnp.sum(chance * grad, axis=0, keepdims=True)
                chances.append(chance)
                grads.append(grad)
            gq = jnp.zeros((HEAD, BLOCK), f32)
            for (kind, k, v, ka), chance, grad, pairs, out in zip(
                parts, chances, grads, sums, outs
            ):
                gl = (chance * (grad - inner)).astype(bf16)
                gk = dot_nn(gl, q) * score_scale
                gv = dot_nn(chance.astype(bf16), go)
                gq = gq + dot_tn(k, gl)
                for more_k, more_v in pairs:
                    gk = gk + more_k[:, lanes]
                    gv = gv + more_v[:, lanes]
                out[0][:, lanes] = gk.astype(out[0].dtype)
                out[1][:, lanes] = gv.astype(out[1].dtype)
            gq_ref[:, lanes] = jnp.transpose(gq * score_scale).astype(bf16)

    keys = BLOCK * len(segments)
    return launch(
        body,
        idx,
        inputs,
        outputs,
        flops=10 * heads * BLOCK * keys * HEAD * 2,
        vmem=8,
        name=name,
    )


def state_update(idx, pieces, write_pieces, state, retain, gain, weights, width, name):
    rows, features = state.shape
    count = len(pieces)
    project = weights is not None

    def body(s, *refs):
        refs = list(refs)
        piece_refs = [refs.pop(0) for unused in range(count)]
        w_refs = [refs.pop(0) for unused in range(count)]
        s_ref, r_ref = refs[:2]
        refs = refs[2:]
        if project:
            g_ref, p_ref, out_ref, n_ref, t_ref = refs
        else:
            (out_ref,) = refs

        @pl.loop(0, rows // TILE)
        def _(i):
            at = span(i * TILE)
            terms = [
                dot_nn(o_ref[at, :], w_ref[: o_ref.shape[1], :])
                for o_ref, w_ref in zip(piece_refs, w_refs)
            ]
            while len(terms) > 1:
                terms = [a + b for a, b in zip(terms[0::2], terms[1::2])]
            update = terms[0]
            keep = r_ref[...]
            following = keep * s_ref[at, :].astype(f32) + (1.0 - keep) * update
            out_ref[at, :] = following
            if project:
                normed = (unit_rows(following)[0] * g_ref[...]).astype(bf16)
                n_ref[at, :] = normed
                t_ref[at, :] = dot_nn(normed, p_ref[:, :width]).astype(bf16)

    inputs = list(pieces) + list(write_pieces) + [state, retain]
    outputs = [shaped((rows, features), f32)]
    if project:
        inputs += [gain, weights]
        outputs += [shaped((rows, features), bf16), shaped((rows, width), bf16)]
    return launch(
        body,
        idx,
        inputs,
        outputs,
        flops=2 * rows * features * (features + (width if project else 0)),
        name=name,
    )


def take_sum(i, s, refs, total):
    chip_ref, mine_ref, theirs_ref = refs
    steps = HALF // TILE
    at, inner = span(tile_start(i, s)), span(lax.rem(i, steps) * TILE)

    @pl.when(i < steps)
    def _():
        total[...] = chip_ref[at, :].astype(f32) + mine_ref[inner, :].astype(f32)

    @pl.when(i >= steps)
    def _():
        total[...] = chip_ref[at, :].astype(f32) + theirs_ref[inner, :].astype(f32)

    return total[...]


def chip_sum(idx, partial, other, name):
    rows, features = partial.shape
    tall = 32

    def body(s, a_ref, b_ref, sum_ref, own_ref):
        @pl.loop(0, rows // tall)
        def _(i):
            at = rows_of(i, 0, tall)
            sum_ref[at, :] = (a_ref[at, :].astype(f32) + b_ref[at, :].astype(f32)).astype(bf16)

        @pl.loop(0, HALF // tall)
        def _(i):
            own_ref[rows_of(i, 0, tall), :] = sum_ref[pl.ds(pl.multiple_of(s[1] * HALF + i * tall, tall), tall), :]

    return launch(
        body,
        idx,
        [partial, other],
        [shaped((rows, features), bf16), shaped((HALF, features), bf16)],
        name=name,
    )


def add_rows(i, ref, value):
    value = jnp.sum(value, axis=0, keepdims=True)

    @pl.when(i == 0)
    def _():
        ref[...] = value

    @pl.when(i != 0)
    def _():
        ref[...] = ref[...] + value


def project_back(idx, grads, weights, column, name):
    rows, width = grads[0].shape
    features = weights.shape[1]

    def body(s, *refs):
        *g_refs, w_ref, out_ref = refs

        @pl.loop(0, rows // TILE)
        def _(i):
            at = span(i * TILE)
            out = jnp.zeros((TILE, features), f32)
            for k, ref in enumerate(g_refs):
                first = column + k * width
                out = out + dot_nn(ref[at, :], w_ref[first : first + width, :])
            out_ref[at, :] = out.astype(bf16)

    return launch(
        body,
        idx,
        list(grads) + [weights],
        [shaped((rows, features), bf16)],
        flops=2 * rows * features * width * len(grads),
        name=name,
    )[0]


def state_back(idx, sums, state, following, retain, gain, write_own, name):
    rows, features = state.shape
    before = write_own is not None
    width = write_own.shape[1] // 2 if before else 10

    def body(s, *refs):
        refs = list(refs)
        total = refs.pop()
        sum_refs = [refs.pop(0) for unused in range(len(sums))]
        s_ref, r_ref, g_ref = refs[:3]
        refs = refs[3:]
        following_ref = refs.pop(0) if following is not None else None
        if before:
            w_ref, gs_ref, gain_ref, gu_ref, gos_ref = refs
        else:
            gs_ref, gain_ref = refs

        @pl.loop(0, rows // TILE)
        def _(i):
            at = span(tile_start(i, s))
            up = take_sum(i, s, sum_refs, total)
            unit, inverse = unit_rows(s_ref[at, :].astype(f32))
            out = unit_back(up, unit, inverse, g_ref[...])
            if following is not None:
                out = r_ref[...] * following_ref[at, :] + out
            gs_ref[at, :] = out
            add_rows(i, gain_ref, up * unit)
            if before:
                gu = ((1.0 - r_ref[...]) * out).astype(bf16)
                gu_ref[at, :] = gu
                gos_ref[at, :] = dot_nn(gu, w_ref[:, :width]).astype(bf16)

    inputs = list(sums) + [state, retain, gain]
    outputs = [shaped((rows, features), f32), shaped((1, features), f32)]
    if following is not None:
        inputs.append(following)
    if before:
        inputs.append(write_own)
        outputs += [shaped((rows, features), bf16), shaped((rows, width), bf16)]
    return launch(
        body,
        idx,
        inputs,
        outputs,
        scratch=[pltpu.VMEM((TILE, features), f32)],
        flops=2 * rows * features * width,
        name=name,
    )


def last_update_back(idx, retain, write_own, rows, name):
    features, width = write_own.shape[0], write_own.shape[1] // 2

    def body(s, r_ref, w_ref, gu_ref, gos_ref):
        gu = ((1.0 - r_ref[...]) * jnp.zeros((rows, features), f32)).astype(bf16)
        gu_ref[...] = gu
        gos_ref[...] = dot_nn(gu, w_ref[:, :width]).astype(bf16)

    return launch(
        body,
        idx,
        [retain, write_own],
        [shaped((rows, features), bf16), shaped((rows, width), bf16)],
        name=name,
    )


def gelu_both(a):
    root, cubic = 0.7978845608028654, 0.044715
    squared = a * a
    bent = jnp.tanh(root * (a + cubic * (squared * a)))
    rising = 0.5 * (1.0 + bent)
    slope = rising + (0.5 * root) * a * (1.0 - bent * bent) * (1.0 + (3.0 * cubic) * squared)
    return a * rising, slope


def output_forward(idx, number, pieces, out_pieces, tokens, gain, name):
    features = tokens.shape[1]
    count = len(pieces)

    def body(s, *refs):
        o_refs, w_refs = refs[:count], refs[count : 2 * count]
        t_ref, g_ref, x1_ref, xn_ref = refs[2 * count :]

        @pl.loop(0, BLOCK // TILE)
        def _(i):
            at = span(i * TILE)
            x1 = t_ref[span(i * TILE, number * BLOCK), :].astype(f32)
            for o_ref, w_ref in zip(o_refs, w_refs):
                x1 = x1 + dot_nn(o_ref[at, :], w_ref[o_ref.shape[1] :, :])
            x1_ref[at, :] = x1
            xn_ref[at, :] = (unit_rows(x1)[0] * g_ref[...]).astype(bf16)

    return launch(
        body,
        idx,
        list(pieces) + list(out_pieces) + [tokens, gain],
        [shaped((BLOCK, features), f32), shaped((BLOCK, features), bf16)],
        flops=2 * BLOCK * features * features,
        name=name,
    )


def dense_forward(idx, normed, dense, name):
    features = normed.shape[1]
    hidden = dense[1].shape[0]

    def body(s, n_ref, up_ref, down_ref, h_ref, slope_ref, part_ref):
        @pl.loop(0, BLOCK // TILE)
        def _(i):
            at = span(i * TILE)
            h, slope = gelu_both(dot_nn(n_ref[at, :], up_ref[:, :hidden]))
            h = h.astype(bf16)
            h_ref[at, :] = h
            slope_ref[at, :] = slope.astype(bf16)
            part_ref[at, :] = dot_nn(h, down_ref[...]).astype(bf16)

    return launch(
        body,
        idx,
        [normed, *dense],
        [
            shaped((BLOCK, hidden), bf16),
            shaped((BLOCK, hidden), bf16),
            shaped((BLOCK, features), bf16),
        ],
        flops=4 * BLOCK * features * hidden,
        name=name,
    )


def dense_backward(idx, number, sums, x1, teacher, katt, slope, dense, name):
    features = x1.shape[1]
    up_t, both = dense
    hidden = up_t.shape[0]

    def body(s, *refs):
        refs = list(refs)
        total = refs.pop()
        sum_refs = [refs.pop(0) for unused in range(len(sums))]
        x_ref, t_ref, v_ref, slope_ref, up_ref, d_ref = refs[:6]
        gm_ref, ga_ref, loss_ref, part_ref = refs[6:]

        @pl.loop(0, BLOCK // TILE)
        def _(i):
            start = tile_start(i, s)
            at, far = span(start), span(start, number * BLOCK)
            errors = x_ref[at, :] + take_sum(i, s, sum_refs, total) - t_ref[far, :].astype(f32)
            gy = v_ref[far, 2:3] * errors
            add_rows(i, loss_ref, gy * errors)
            gm = gy.astype(bf16)
            gm_ref[at, :] = gm
            ga = (dot_nn(gm, d_ref[:, hidden:]) * slope_ref[at, :].astype(f32)).astype(bf16)
            ga_ref[at, :] = ga
            part_ref[at, :] = dot_nn(ga, up_ref[...]).astype(bf16)

    return launch(
        body,
        idx,
        list(sums) + [x1, teacher, katt, slope, up_t, both],
        [
            shaped((BLOCK, features), bf16),
            shaped((BLOCK, hidden), bf16),
            shaped((1, features), f32),
            shaped((BLOCK, features), bf16),
        ],
        scratch=[pltpu.VMEM((TILE, features), f32)],
        flops=4 * BLOCK * features * hidden,
        name=name,
    )


def output_backward(idx, sums, gy, x1, gain, out_own, name):
    features = x1.shape[1]
    width = out_own.shape[1] // 2

    def body(s, *refs):
        refs = list(refs)
        total = refs.pop()
        sum_refs = [refs.pop(0) for unused in range(len(sums))]
        gy_ref, x_ref, g_ref, w_ref, gp_ref, go_ref, gain_ref = refs

        @pl.loop(0, BLOCK // TILE)
        def _(i):
            at = span(tile_start(i, s))
            up = take_sum(i, s, sum_refs, total)
            unit, inverse = unit_rows(x_ref[at, :])
            gx = gy_ref[at, :].astype(f32) + unit_back(up, unit, inverse, g_ref[...])
            gp = gx.astype(bf16)
            gp_ref[at, :] = gp
            go_ref[at, :] = dot_nn(gp, w_ref[:, width:]).astype(bf16)
            add_rows(i, gain_ref, up * unit)

    return launch(
        body,
        idx,
        list(sums) + [gy, x1, gain, out_own],
        [
            shaped((BLOCK, features), bf16),
            shaped((BLOCK, width), bf16),
            shaped((1, features), f32),
        ],
        scratch=[pltpu.VMEM((TILE, features), f32)],
        flops=2 * BLOCK * features * width,
        name=name,
    )


def weight_grads(idx, groups, name, before=None, weight=40, vmem=8):
    features = groups[0][0][0].shape[1]
    inputs, specs, total, flops = [], [], 0, 0
    for parts in groups:
        for left, block, right in parts:
            rows = right.shape[0]
            inputs += [left, right]
            specs.append(pl.BlockSpec((rows, HALF), lambda i, block=block: (block, i)))
            specs.append(
                pl.BlockSpec(right.shape, lambda i: (0, 0), pipeline_mode=pl.Buffered(1))
            )
            flops += 2 * rows * features * right.shape[1]
        total += parts[0][2].shape[1]
    if before is not None:
        inputs.append(before)
        specs.append(pl.BlockSpec((HALF, total), lambda i: (i, 0)))

    def body(s, *refs):
        refs = list(refs)
        out_ref = refs.pop()
        before_ref = refs.pop() if before is not None else None
        at = 0
        for parts in groups:
            size = parts[0][2].shape[1]
            if before is None:
                out = jnp.zeros((HALF, size), f32)
            else:
                out = before_ref[:, at : at + size].astype(f32)
            for unused in parts:
                left, right = refs.pop(0), refs.pop(0)
                out = out + dot_tn(left[...], right[...])
            out_ref[:, at : at + size] = out.astype(bf16)
            at += size

    return pl.pallas_call(
        body,
        grid=(features // HALF,),
        in_specs=[pl.BlockSpec(memory_space=pltpu.SMEM)] + specs,
        out_specs=pl.BlockSpec((HALF, total), lambda i: (i, 0)),
        out_shape=pltpu.HBM((features, total), bf16),
        compiler_params=pltpu.CompilerParams(
            dimension_semantics=("arbitrary",), vmem_limit_bytes=vmem << 20
        ),
        cost_estimate=cost(weight * flops, inputs),
        name=name,
    )(idx, *inputs)


def unpack_grads(packed, widths, flipped, name):
    rows = packed.shape[0]

    def body(p_ref, *out_refs):
        at = 0
        for size, flip, out_ref in zip(widths, flipped, out_refs):
            values = p_ref[:, at : at + size].astype(f32)
            out_ref[...] = jnp.transpose(values) if flip else values
            at += size

    return pl.pallas_call(
        body,
        in_specs=[pl.BlockSpec(memory_space=pltpu.VMEM)],
        out_specs=[pl.BlockSpec(memory_space=pltpu.VMEM)] * len(widths),
        out_shape=[
            shaped((size, rows) if flip else (rows, size), f32)
            for size, flip in zip(widths, flipped)
        ],
        compiler_params=pltpu.CompilerParams(vmem_limit_bytes=8 << 20),
        cost_estimate=cost(0, [packed]),
        name=name,
    )(packed)


def arrange_rows(idx, pieces, count, name):
    rows, features = pieces[0].shape
    rows = rows // count

    def body(s, *refs):
        ins, outs = refs[: len(pieces)], refs[len(pieces) :]
        for k, ref in enumerate(ins):
            for j, out_ref in enumerate(outs):
                out_ref[rows_of(s[0] ^ k, 0, rows), :] = ref[j * rows : (j + 1) * rows, :]

    return launch(
        body,
        idx,
        pieces,
        [shaped((rows * len(pieces), features), pieces[0].dtype)] * count,
        name=name,
    )


def turn(idx, values, first, count, name):
    rows = values.shape[0]
    wide = 256

    def body(s, v_ref, out_ref):
        @pl.loop(0, count // wide)
        def _(i):
            lanes = pl.ds(pl.multiple_of(first + i * wide, HEAD), wide)
            out_ref[rows_of(i, 0, wide), :] = jnp.transpose(v_ref[:, lanes])

    return launch(body, idx, [values], [shaped((count, rows), values.dtype)], name=name)[0]


def arrange_columns(idx, blocks, across, name):
    rows, width = blocks[0].shape
    depth = len(blocks)

    def body(s, *refs):
        out_ref = refs[-1]
        for k in range(depth):
            level = lax.rem(s[3] + depth - k, depth)
            out_ref[rows_of(2 * level + s[4], 0, rows), :] = refs[k][...]
            out_ref[rows_of(2 * level + 1 - s[4], 0, rows), :] = refs[depth + k][...]

    return launch(
        body,
        idx,
        list(blocks) + list(across),
        [shaped((2 * depth * rows, width), blocks[0].dtype)],
        name=name,
    )[0]


def split_grads(idx, groups, depth, name):
    features = groups[0][0][0].shape[1]
    rows = features // (2 * depth)
    total = sum(parts[0][2].shape[1] for parts in groups)
    inputs = []

    def place(array):
        for k, known in enumerate(inputs):
            if known is array:
                return k
        inputs.append(array)
        return len(inputs) - 1

    uses = [[(place(a), block, place(c)) for a, block, c in parts] for parts in groups]

    def body(s, *refs):
        *ins, theirs_ref, mine_ref, held = refs

        @pl.loop(0, depth)
        def _(i):
            lanes = pl.ds(pl.multiple_of(i * 2 * rows, 2 * rows), 2 * rows)
            at = 0
            for parts in uses:
                size = ins[parts[0][2]].shape[1]
                out = jnp.zeros((2 * rows, size), f32)
                for left, block, right in parts:
                    count = ins[right].shape[0]
                    tall = slice(block * count, (block + 1) * count)
                    out = out + dot_tn(ins[left][tall, lanes], ins[right][...])
                held[:, at : at + size] = out.astype(bf16)
                at += size
            mine_ref[rows_of(i, 0, rows), :] = held[rows_of(s[4], 0, rows), :]
            theirs_ref[rows_of(i, 0, rows), :] = held[rows_of(1 - s[4], 0, rows), :]

    return launch(
        body,
        idx,
        inputs,
        [shaped((depth * rows, total), bf16)] * 2,
        scratch=[pltpu.VMEM((2 * rows, total), bf16)],
        name=name,
    )


def pair_blocks(idx, mine, got, depth, name):
    rows, width = mine.shape[0] // depth, mine.shape[1]

    def body(s, mine_ref, got_ref, *out_refs):
        for k, ref in enumerate(out_refs):
            at = rows_of(lax.rem(s[3] + k, depth), 0, rows)
            ref[...] = (mine_ref[at, :].astype(f32) + got_ref[at, :].astype(f32)).astype(ref.dtype)

    return launch(
        body,
        idx,
        [mine, got],
        [shaped((rows, width), f32)] + [shaped((rows, width), bf16)] * (depth - 1),
        name=name,
    )


def line_sum(idx, own, others, widths, flipped, name):
    rows = own.shape[0]

    def body(s, own_ref, *refs):
        ins, outs = refs[: len(others)], refs[len(others) :]
        total = own_ref[...]
        for ref in ins:
            total = total + ref[...].astype(f32)
        at = 0
        for size, flip, out_ref in zip(widths, flipped, outs):
            values = total[:, at : at + size]
            out_ref[...] = jnp.transpose(values) if flip else values
            at += size

    return launch(
        body,
        idx,
        [own] + list(others),
        [
            shaped((size, rows) if flip else (rows, size), f32)
            for size, flip in zip(widths, flipped)
        ],
        name=name,
    )


def pack(idx, arrays, takes, shapes, name):
    flipped = [take for take in takes if take[-1]]

    def body(s, *refs):
        ins, outs = refs[: len(arrays)], refs[len(arrays) : len(arrays) + len(shapes)]
        *held, sems = refs[len(arrays) + len(shapes) :]
        copies, spare = [], list(held)
        for j, (k, row, col, rows, cols, out, place, flip) in enumerate(takes):
            at = pl.ds(0, rows) if row is None else rows_of(s[row], 0, rows)
            to = pl.ds(0, cols) if col is None else rows_of(s[col], 0, cols)
            if flip:
                target = spare.pop(0)
            else:
                target = outs[out].at[pl.ds(place[0], rows), pl.ds(place[1], cols)]
            copies.append(pltpu.make_async_copy(ins[k].at[at, to], target, sems.at[j]))
            copies[-1].start()
        spare = list(held)
        for copy, (k, row, col, rows, cols, out, place, flip) in zip(copies, takes):
            copy.wait()
            if flip:
                to = slice(place[1], place[1] + rows)
                outs[out][place[0] : place[0] + cols, to] = jnp.transpose(spare.pop(0)[...])

    return pl.pallas_call(
        body,
        in_specs=[pl.BlockSpec(memory_space=pltpu.SMEM)]
        + [pl.BlockSpec(memory_space=pl.ANY)] * len(arrays),
        out_specs=[pl.BlockSpec(memory_space=pltpu.VMEM)] * len(shapes),
        out_shape=[shaped(a, bf16) for a in shapes],
        scratch_shapes=[pltpu.VMEM((take[3], take[4]), bf16) for take in flipped]
        + [pltpu.SemaphoreType.DMA((len(takes),))],
        compiler_params=pltpu.CompilerParams(vmem_limit_bytes=8 << 20),
        cost_estimate=cost(0, arrays),
        name=name,
    )(idx, *[pltpu.with_memory_space_constraint(a, pltpu.HBM) for a in arrays])


def input_rows(idx, own, arrived, gps, tokens, gain, name):
    rows, features = tokens.shape
    count = len(gps)

    def body(s, *refs):
        own_refs, far_refs, gp_refs = refs[:count], refs[count : 2 * count], refs[2 * count : 3 * count]
        t_ref, g_ref, out_ref, gain_ref = refs[3 * count :]
        unit, inverse = unit_rows(t_ref[...].astype(f32))
        for b in range(count):

            @pl.when(s[2] // 2 == b)
            def _():
                at = rows_of(s[1])
                up = own_refs[b][at, :].astype(f32) + far_refs[b][...].astype(f32)
                base = gp_refs[b][rows_of(s[1]), :].astype(f32)
                out_ref[...] = base + unit_back(up, unit, inverse, g_ref[...])
                gain_ref[...] = jnp.sum(up * unit, axis=0, keepdims=True)

    return launch(
        body,
        idx,
        list(own) + list(arrived) + list(gps) + [tokens, gain],
        [shaped((rows, features), f32), shaped((1, features), f32)],
        name=name,
    )


def per_device(
    block_input,
    state_start,
    teacher,
    valid_mask,
    segment,
    image_offset,
    retain,
    to_query,
    to_key,
    to_value,
    to_output,
    to_hidden,
    to_model,
    state_query,
    state_key,
    state_value,
    state_write,
    first_gain,
    second_gain,
    state_gain,
):
    row_devices = lax.axis_size("row")
    col_devices = lax.axis_size("col")
    row_index = lax.axis_index("row")
    col_index = lax.axis_index("col")
    local_rows, features = block_input.shape[1:]
    length = local_rows * row_devices
    width = to_query.shape[1]
    heads = width // HEAD
    hidden = to_hidden.shape[1] // row_devices
    nblocks = length // BLOCK
    pairs = row_devices == 4 and 2 * local_rows == BLOCK
    lines = pairs and col_devices == 8
    core_pairs = [(k, k ^ 1) for k in range(row_devices)]
    chip_pairs = [(k, k ^ 2) for k in range(row_devices)] if pairs else None
    if pairs:
        idx = jnp.stack([row_index, row_index % 2, row_index, col_index // 2, col_index % 2])
    else:
        idx = jnp.stack([0, 1, row_index, 0, 0])
    idx = idx.astype(jnp.int32)

    def to_core(x):
        return lax.ppermute(x, "row", core_pairs)

    def to_chip(x):
        return lax.ppermute(x, "row", chip_pairs)

    def row_moves(x):
        if not pairs:
            stacked = lax.all_gather(x, "row", axis=0, tiled=False)
            return [stacked[k] for k in range(row_devices)]
        return [x, to_core(x), to_chip(x)]

    def row_pieces(moved, *ties):
        if not pairs:
            return moved
        x, near, far = moved
        return [x, near, far, to_core(after(far, *ties))]

    depth_z = col_devices // 2

    def along(v, step):
        levels = range(depth_z)
        moves = [(2 * z + y, 2 * ((z + step) % depth_z) + y) for z in levels for y in range(2)]
        return lax.ppermute(v, "col", moves)

    def across(v):
        return lax.ppermute(v, "col", [(k, k ^ 1) for k in range(col_devices)])

    class Columns:
        def __init__(self, x, name):
            self.name = name
            if lines:
                self.blocks = [x] + [along(x, k) for k in range(1, depth_z)]
                self.crossed = [across(x)]
            else:
                self.whole = lax.all_gather(x, "col", axis=0, tiled=True)

        def cross(self, k, *ties):
            if lines:
                self.crossed.append(across(after(self.blocks[k], *ties)))

        def landed(self, k):
            return [self.blocks[k], self.crossed[k - 1]] if lines else []

        def result(self, *ties):
            if lines:
                order = after(idx, *ties)
                return arrange_columns(order, self.blocks, self.crossed, self.name)
            return self.whole

    class Scattered:
        def __init__(self, groups, name, *ties):
            self.name, self.widths = name, [parts[0][2].shape[1] for parts in groups]
            if lines:
                order = after(idx, *ties) if ties else idx
                theirs, self.mine = split_grads(order, groups, depth_z, name)
                self.got = across(theirs)
            else:
                packed = weight_grads(idx, groups, name)
                self.whole = lax.psum_scatter(packed, "col", scatter_dimension=0, tiled=True)

        def send(self, *ties):
            if lines:
                mine = after(self.mine, *ties) if ties else self.mine
                self.own, *blocks = pair_blocks(idx, mine, self.got, depth_z, f"{self.name}_y")
                self.far = [along(block, k + 1) for k, block in enumerate(blocks)]

        def result(self, flipped):
            if lines:
                return line_sum(idx, self.own, self.far, self.widths, flipped, f"{self.name}_z")
            return unpack_grads(self.whole, self.widths, flipped, f"{self.name}_z")

    class RowSum:
        def __init__(self, partial, name, receiver=None, ties=(), near=None):
            if pairs:
                order = after(idx, *ties) if ties else idx
                near = to_core(partial) if near is None else near
                self.chip, own = chip_sum(order, partial, near, name)
                moves = [m for m in chip_pairs if receiver is None or m[1] // 2 == receiver]
                self.far = lax.ppermute(own, "row", moves)
            else:
                self.chip = lax.psum(partial, "row")

        def result(self, *ties):
            if pairs:
                return [self.chip, self.far, to_core(after(self.far, *ties))]
            none = jnp.zeros((HALF, features), bf16)
            return [self.chip, none, none]

    def all_sum(x, *held):
        hops = 0
        for axis, size in (("row", row_devices), ("col", col_devices)):
            step = 1
            while step < size:
                if hops == 2 and held:
                    x = after(x, *held)
                x = x + lax.ppermute(x, axis, [(k, k ^ step) for k in range(size)])
                step *= 2
                hops += 1
        return x

    depth = to_query.shape[0]
    (near,) = pack(
        idx,
        [state_query, state_key, state_value, to_query, to_key, to_value],
        [(k, None, None, depth, width, 0, (0, k * width), False) for k in range(6)],
        [(depth, 6 * width)],
        "pack_near",
    )
    near = lax.all_gather(near, "col", axis=0, tiled=True)
    rows_in, mid, far_weights = pack(
        idx,
        [state_write, to_output, to_hidden, to_model, block_input[0], teacher[0]],
        [
            (4, None, None, local_rows, features, 0, (0, 0), False),
            (5, None, None, local_rows, features, 0, (local_rows, 0), False),
            (0, 2, None, width, depth, 1, (0, 0), True),
            (1, None, None, width, depth, 1, (0, width), True),
            (2, None, 2, depth, hidden, 2, (0, 0), False),
            (3, 2, None, hidden, depth, 2, (0, hidden), True),
        ],
        [(2 * local_rows, features), (depth, 2 * width), (depth, 2 * hidden)],
        "pack_rest",
    )
    rows_moved = row_moves(rows_in) if pairs else None
    mid = Columns(mid, "mid")
    for k in range(1, depth_z):
        mid.cross(k)
    mid = mid.result()
    mid_n = turn(idx, mid, 0, 2 * width, "mid_turn")
    held = [mid_n] + (rows_moved[2:] if pairs else [])
    dense = lax.all_gather(after(far_weights, *held), "col", axis=0, tiled=True)
    mid_moved = row_moves(mid_n)
    if pairs:
        tokens, teacher_all = arrange_rows(idx, row_pieces(rows_moved), 2, "tokens")
    else:
        tokens, teacher_all = [
            lax.all_gather(x[0], "row", axis=0, tiled=True) for x in (block_input, teacher)
        ]

    valid_row = lax.dynamic_index_in_dim(valid_mask, col_index, 0, keepdims=False)
    segment_row = segment[0]
    numbers = jnp.arange(nblocks, dtype=jnp.int32)
    places = jnp.arange(length, dtype=jnp.int32)
    starts = numbers * BLOCK + image_offset[0]
    inside = (places[:, None] >= starts[None, :]) & (places[:, None] < starts[None, :] + PIECE)
    piece = jnp.sum(jnp.where(inside, numbers[None, :] + 1, 0), axis=1) - 1
    valid_count = jnp.sum(valid_mask.astype(f32))
    total_tokens = f32(length * col_devices)
    weight_of_row = total_tokens / valid_count * valid_row.astype(f32)
    document = segment_row.astype(f32)
    nothing = jnp.zeros_like(document)
    katt = jnp.stack(
        [jnp.where(valid_row > 0, document, -1.0), piece.astype(f32), weight_of_row, nothing],
        axis=1,
    )
    qatt = jnp.stack(
        [document, jnp.where(piece >= 0, piece, -2).astype(f32), nothing, nothing], axis=0
    )
    retain2 = retain[None]
    first_gain2, second_gain2, state_gain2 = first_gain[None], second_gain[None], state_gain[None]

    def token_segments(number, trio):
        found = []
        if number > 0:
            found.append(("prev", token_heads, number - 1, width, 2 * width, number - 1))
        found.append(("own", token_heads, number, width, 2 * width, number))
        found.append(("free", trio, 0, width, 2 * width, None))
        return found

    def state_segments(number, trio):
        return [
            ("valid", token_heads, number, width, 2 * width, number),
            ("free", trio, 0, width, 2 * width, None),
        ]

    current = state_start[0]
    near_t = turn(idx, near, 0, 6 * width, "near_turn")
    state_low, trio = norm_project(after(idx, near_t), current, state_gain2, near, 0, 3 * width, "state_proj")
    first_low, token_heads = norm_project(
        idx, tokens, first_gain2, near, 3 * width, 3 * width, "token_proj"
    )
    states, lows, trios = [], [], []
    state_out, state_logs, token_out, token_logs = [], [], [], []
    x1s, second_lows, hiddens, slopes, dense_sums = [], [], [], [], []
    state_pieces, token_pieces = [], []
    end = nblocks - 1

    def state_part(b):
        mixed, logs = attend(
            idx,
            (trios[b], 0, 0),
            state_segments(b, trios[b]),
            katt,
            None,
            heads,
            f"state_attend{b}",
        )
        state_out.append(mixed)
        state_logs.append(logs)
        state_pieces.append(row_moves(mixed) if b < nblocks - 1 else None)

    for b in range(nblocks):
        states.append(current)
        lows.append(state_low)
        trios.append(trio)
        last = b + 1 == nblocks
        if not last:
            state_part(b)
        mixed, logs = attend(
            idx, (token_heads, b, 0), token_segments(b, trio), katt, qatt, heads, f"token_attend{b}"
        )
        if b == 0:
            mid_pieces = row_pieces(mid_moved, mixed)
        token_out.append(mixed)
        token_logs.append(logs)
        token_pieces.append(row_moves(mixed))
        if not last:
            current, state_low, trio = state_update(
                idx,
                row_pieces(state_pieces[b], mixed),
                mid_pieces,
                current,
                retain2,
                state_gain2,
                near,
                3 * width,
                f"update{b}",
            )
            token_pieces[b] = row_pieces(token_pieces[b], trio)
    state_part(nblocks - 1)
    token_pieces[-1] = row_pieces(token_pieces[-1], state_out[-1])

    def state_back_part(b, gos_state, own, free, dtype):
        return attend_back(
            idx,
            (trios[b], 0, 0),
            state_segments(b, trios[b]),
            katt,
            None,
            heads,
            state_logs[b],
            gos_state,
            [own, free],
            [dtype, dtype],
            f"state_back{b}",
        )

    def token_back_part(b, own, free, dtype, upstream):
        segments = token_segments(b, trios[b])
        added = ([[]] if b > 0 else []) + [own, free]
        dtypes = ([f32] if b > 0 else []) + [dtype, dtype]
        found = attend_back(
            idx,
            (token_heads, b, 0),
            segments,
            katt,
            qatt,
            heads,
            token_logs[b],
            upstream,
            added,
            dtypes,
            f"token_back{b}",
        )
        return found[0], found[-4:], (found[1], found[2]) if b > 0 else None

    gus = [None] * nblocks
    gms, gas, losses, gps, gos, second_sums = [], [], [], [], [], []
    second_back = []
    for b in range(nblocks):
        x1, low = output_forward(
            idx, b, token_pieces[b], mid_pieces, tokens, second_gain2, f"out{b}"
        )
        x1s.append(x1)
        second_lows.append(low)
    down = turn(after(idx, state_out[-1], *second_lows), dense, hidden, hidden, "down_turn")
    order = idx
    for b in range(nblocks):
        h, slope, partial = dense_forward(order, second_lows[b], (dense, down), f"dense{b}")
        hiddens.append(h)
        slopes.append(slope)
        ties = []
        if b == 0:
            up_t = turn(after(idx, h), dense, 0, hidden, "up_turn")
            ties.append(up_t)
        if b == end:
            late_mid = after(mid, h)
            gus[end], gos_state = last_update_back(idx, retain2, late_mid, NS, "last_back")
            state_found = state_back_part(end, gos_state, [], [], f32)
            ties.append(state_found[0])
        dense_sums.append(RowSum(partial, f"dense_sum{b}", ties=ties))
        order = after(idx, dense_sums[b].chip)

    early_grads, partials = [], []
    ready = teacher_all
    for b in range(nblocks):
        hides = [hiddens[end], state_found[0]] if b == 0 else [gms[b - 1]] + early_grads
        gm, ga, loss, partial = dense_backward(
            idx, b, dense_sums[b].result(*hides), x1s[b], ready, katt, slopes[b], (up_t, dense), f"back{b}"
        )
        gms.append(gm)
        gas.append(ga)
        losses.append(loss)
        if b < end:
            early_grads = [
                weight_grads(
                    idx,
                    [[(second_lows[b], 0, ga)], [(gm, 0, hiddens[b])]],
                    f"dense_grads{b}",
                    *early_grads,
                )
            ]
        partials.append((partial, to_core(partial) if pairs and b < end else None))
        ready = after(teacher_all, partials[b][1]) if pairs and b < end else teacher_all
        if b > 0:
            part, near_part = partials[b - 1]
            second_back.append(
                RowSum(part, f"back_sum{b - 1}", ties=[gm], near=near_part)
            )
    dense_grads = weight_grads(
        idx,
        [[(second_lows[end], 0, gas[end])], [(gms[end], 0, hiddens[end])]],
        "dense_grads",
        *early_grads,
    )
    filled = [dense_grads]
    ties = [dense_grads] + [back.far for back in second_back] if pairs else []
    second_back.append(RowSum(partial, f"back_sum{end}", ties=ties))
    dense_grads = lax.psum_scatter(dense_grads, "col", scatter_dimension=0, tiled=True)

    token_found = [None] * nblocks
    for b in range(nblocks):
        gp, go, gain_sum = output_backward(
            idx,
            second_back[b].result(*(filled if b == end else [gms[end]])),
            gms[b],
            x1s[b],
            second_gain2,
            mid,
            f"out_back{b}",
        )
        gps.append(gp)
        gos.append(go)
        second_sums.append(gain_sum)
        if b < end:
            token_found[b] = token_back_part(b, [], [], f32, go)
            filled.append(token_found[b][0])
    trio_grads = [None] * nblocks
    token_grads = [None] * nblocks
    first_sums = [None] * nblocks
    gain_sums = []
    grad_next = None
    gqs, gk, gv, gks, gvs = state_found
    gq, (gk, gv, gks, gvs), key_part = token_back_part(
        end, [(gk, gv)], [(gks, gvs)], bf16, gos[end]
    )
    state_pieces[-1] = row_moves(after(state_out[-1], gos[end]))
    gqs = after(gqs, state_pieces[-1][2])
    trio_grads[end] = (gqs, gks, gvs)
    token_grads[end] = (gq, gk, gv)
    for b in reversed(range(nblocks)):
        order = idx
        if b == 0:

            def state_group(k):
                return [(lows[c], 0, trio_grads[c][k]) for c in range(nblocks)]

            def token_group(k):
                return [(first_low, c, token_grads[c][k]) for c in range(nblocks)]

            write_group = [(gu, 0, out) for gu, out in zip(gus, state_out)]
            late_grads = weight_grads(
                idx,
                [state_group(k) for k in range(3)] + [token_group(1), token_group(2)],
                "late_grads",
                weight=130,
                vmem=12,
            )
            order = after(idx, late_grads)
            rest_grads = Scattered(
                [token_group(0), [(gp, 0, out) for gp, out in zip(gps, token_out)], write_group],
                "rest_grads",
                late_grads,
            )
            late_grads = lax.psum_scatter(late_grads, "col", scatter_dimension=0, tiled=True)
        trio_sum = RowSum(
            project_back(order, trio_grads[b], near_t, 0, f"trio_back{b}"),
            f"trio_sum{b}",
        )
        hides = []
        if b == end:
            (final_state,) = state_update(
                idx,
                row_pieces(state_pieces[-1], gq),
                mid_pieces,
                current,
                retain2,
                None,
                None,
                0,
                "update_last",
            )
            hides.append(final_state)
        first_sums[b] = project_back(idx, token_grads[b], near_t, 3 * width, f"first_back{b}")
        hides.append(first_sums[b])
        first_sums[b] = RowSum(first_sums[b], f"first_sum{b}", b) if pairs else first_sums[b]
        if b > 0:
            grad_next, gain_sum, gus[b - 1], gos_state = state_back(
                idx,
                trio_sum.result(*hides),
                states[b],
                grad_next,
                retain2,
                state_gain2,
                mid,
                f"chain_back{b}",
            )
            gq, (gk, gv, gks, gvs), next_part = token_found[b - 1]
            gqs, gk, gv, gks, gvs = state_back_part(
                b - 1, gos_state, [(gk, gv), key_part], [(gks, gvs)], bf16
            )
            key_part = next_part
            trio_grads[b - 1] = (gqs, gks, gvs)
            token_grads[b - 1] = (gq, gk, gv)
        else:
            grad_next, gain_sum = state_back(
                idx,
                trio_sum.result(*hides),
                states[b],
                grad_next,
                retain2,
                state_gain2,
                None,
                "chain_back0",
            )
        gain_sums.append(gain_sum)

    rest_grads.send(grad_next)

    if pairs:
        own_rows = [first.chip for first in first_sums]
        arrived = [first.far for first in first_sums]
        input_grad, first_sum = input_rows(
            idx, own_rows, arrived, gps, block_input[0], first_gain2, "input_rows"
        )
        first_sum = first_sum[0]
    else:
        both = jnp.concatenate(first_sums)
        grad_first = lax.psum_scatter(both, "row", scatter_dimension=0, tiled=True).astype(f32)
        own_gx1 = lax.dynamic_slice_in_dim(
            jnp.concatenate(gps), row_index * local_rows, local_rows
        ).astype(f32)
        unit, inverse = unit_rows(block_input[0].astype(f32))
        input_grad = own_gx1 + unit_back(grad_first, unit, inverse, first_gain2)
        first_sum = jnp.sum(grad_first * unit, axis=0)

    share = 1.0 / row_devices
    sums = jnp.stack(
        [
            sum(losses)[0] * share,
            first_sum,
            sum(second_sums)[0] * share,
            sum(gain_sums)[0] * share,
        ]
    )
    if lines:
        sums = after(sums, rest_grads.own)
    summed = all_sum(sums, *(rest_grads.far if lines else []))
    total_loss = jnp.sum(summed[0]) / (2.0 * total_tokens)

    upper_grad, lower_grad = unpack_grads(
        dense_grads, [hidden, hidden], [False, True], "unpack_dense"
    )
    late = unpack_grads(late_grads, [width] * 5, [False] * 5, "unpack_late")
    rest = rest_grads.result([False, True, True])

    return (
        total_loss,
        final_state[None],
        input_grad[None],
        grad_next[None],
        rest[0],
        late[3],
        late[4],
        rest[1],
        upper_grad,
        lower_grad,
        late[0],
        late[1],
        late[2],
        rest[2],
        summed[1],
        summed[2],
        summed[3],
    )


def solution(mesh):
    in_specs = (
        P("col", "row", None),
        P("col", None, None),
        P("col", "row", None),
        P(),
        P("col", None),
        P("col", None),
        P(),
        P("col", "row"),
        P("col", "row"),
        P("col", "row"),
        P("row", "col"),
        P("col", None),
        P(None, "col"),
        P("col", "row"),
        P("col", "row"),
        P("col", "row"),
        P(None, "col"),
        P(),
        P(),
        P(),
    )
    out_specs = (
        P(),
        P("col", None, None),
        P("col", "row", None),
        P("col", None, None),
        P("col", "row"),
        P("col", "row"),
        P("col", "row"),
        P("row", "col"),
        P("col", "row"),
        P("row", "col"),
        P("col", "row"),
        P("col", "row"),
        P("col", "row"),
        P("row", "col"),
        P(),
        P(),
        P(),
    )
    return jax.shard_map(
        per_device, mesh=mesh, in_specs=in_specs, out_specs=out_specs, check_vma=False
    )
```

```python
import functools

import jax
import jax.numpy as jnp
from jax import lax
from jax.experimental import pallas as pl
from jax.experimental.pallas import tpu as pltpu
from jax.sharding import PartitionSpec as P

HEAD = 128
BLOCK = 512
HALF = 256
NS = 512
PIECE = 256
COST = 8
TILE = 256

epsilon = 1e-06
masked_value = -1e30
score_scale = HEAD ** (-0.5)
log2_scale = score_scale * 1.4426950408889634
f32 = jnp.float32
bf16 = jnp.bfloat16


def dot_nn(a, b):
    return lax.dot_general(a, b, (((1,), (0,)), ((), ())), preferred_element_type=f32)


def dot_nt(a, b):
    return lax.dot_general(a, b, (((1,), (1,)), ((), ())), preferred_element_type=f32)


def dot_tn(a, b):
    return lax.dot_general(a, b, (((0,), (0,)), ((), ())), preferred_element_type=f32)


def cost(flops, arrays):
    return pl.CostEstimate(flops=flops // COST, bytes_accessed=1024, transcendentals=0)


def after(x, *earlier):
    return lax.optimization_barrier((x,) + earlier)[0]


def shaped(shape, dtype):
    return jax.ShapeDtypeStruct(shape, dtype)


def launch(body, idx, inputs, outputs, scratch=(), flops=0, vmem=8, name=None):
    return pl.pallas_call(
        body,
        in_specs=[pl.BlockSpec(memory_space=pltpu.SMEM)]
        + [pl.BlockSpec(memory_space=pltpu.VMEM)] * len(inputs),
        out_specs=[pl.BlockSpec(memory_space=pltpu.VMEM)] * len(outputs),
        out_shape=list(outputs),
        scratch_shapes=list(scratch),
        compiler_params=pltpu.CompilerParams(vmem_limit_bytes=vmem << 20),
        cost_estimate=cost(flops, inputs),
        name=name,
    )(idx, *inputs)


def rows_of(i, base=0, size=HALF):
    return pl.ds(pl.multiple_of(base + i * size, size), size)


def tile_start(i, s):
    steps = HALF // TILE
    return lax.rem(i // steps + s[1], 2) * HALF + lax.rem(i, steps) * TILE


def span(start, base=0):
    return pl.ds(pl.multiple_of(base + start, TILE), TILE)


def unit_rows(x):
    inverse = lax.rsqrt(jnp.mean(x * x, axis=-1, keepdims=True) + epsilon)
    return x * inverse, inverse


def unit_back(up, unit, inverse, gain):
    scaled = up * gain
    inner = jnp.mean(scaled * unit, axis=-1, keepdims=True)
    return inverse * (scaled - unit * inner)


def norm_project(idx, values, gain, weights, column, width, name):
    rows, features = values.shape

    def body(s, x_ref, g_ref, w_ref, n_ref, p_ref):
        @pl.loop(0, rows // TILE)
        def _(i):
            at = span(i * TILE)
            unit, unused = unit_rows(x_ref[at, :].astype(f32))
            normed = (unit * g_ref[...]).astype(bf16)
            n_ref[at, :] = normed
            p_ref[at, :] = dot_nn(normed, w_ref[:, column : column + width]).astype(bf16)

    return launch(
        body,
        idx,
        [values, gain, weights],
        [shaped((rows, features), bf16), shaped((rows, width), bf16)],
        flops=2 * rows * features * width,
        name=name,
    )


def masked_scores(kind, keys, queries, katt, qatt):
    scores = dot_nt(keys, queries)
    if kind == "free":
        return scores
    if kind == "valid":
        return jnp.where(katt[:, 2:3] > 0.0, scores, masked_value)
    places = lax.broadcasted_iota(jnp.int32, scores.shape, 0)
    asking = lax.broadcasted_iota(jnp.int32, scores.shape, 1)
    same = katt[:, 0:1] == qatt[0:1, :]
    if kind == "prev":
        allowed = same & (places > asking)
    else:
        allowed = same & ((places <= asking) | (katt[:, 1:2] == qatt[1:2, :]))
    return jnp.where(allowed, scores, masked_value)


def attention_inputs(queries, segments, katt, qatt):
    arrays = []

    def place(array):
        for k, known in enumerate(arrays):
            if known is array:
                return k
        arrays.append(array)
        return len(arrays) - 1

    use_q = place(queries[0])
    use_k = [place(segment[1]) for segment in segments]
    use_att = place(katt)
    use_qatt = place(qatt) if qatt is not None else None
    return arrays, use_q, use_k, use_att, use_qatt


def read_attention(refs, uses, queries, segments, head):
    use_q, use_k, use_att, use_qatt = uses
    unused, q_row, q_col = queries

    def take(ref, row, col):
        lanes = pl.ds(pl.multiple_of(col + head * HEAD, HEAD), HEAD)
        return ref[row * BLOCK : (row + 1) * BLOCK, lanes]

    q = take(refs[use_q], q_row, q_col)
    parts = []
    for (kind, unused, row, k_col, v_col, att), k in zip(segments, use_k):
        rows = None if att is None else refs[use_att][att * BLOCK : (att + 1) * BLOCK, :]
        parts.append((kind, take(refs[k], row, k_col), take(refs[k], row, v_col), rows))
    qa = None if use_qatt is None else refs[use_qatt][:, q_row * BLOCK : (q_row + 1) * BLOCK]
    return q, parts, qa


def attend(idx, queries, segments, katt, qatt, heads, name):
    arrays, *uses = attention_inputs(queries, segments, katt, qatt)
    count = len(arrays)

    def body(s, *refs):
        o_ref, l_ref = refs[count:]

        @pl.loop(0, heads)
        def _(head):
            q, parts, qa = read_attention(refs, uses, queries, segments, head)
            scores = [masked_scores(kind, k, q, ka, qa) for kind, k, v, ka in parts]
            largest = functools.reduce(
                jnp.maximum, [jnp.max(x, axis=0, keepdims=True) for x in scores]
            )
            total = jnp.zeros_like(largest)
            mixed = jnp.zeros((HEAD, BLOCK), f32)
            for x, (kind, k, v, ka) in zip(scores, parts):
                raised = jnp.exp2((x - largest) * log2_scale)
                total = total + jnp.sum(raised, axis=0, keepdims=True)
                mixed = mixed + dot_tn(v, raised.astype(bf16))
            lanes = pl.ds(pl.multiple_of(head * HEAD, HEAD), HEAD)
            o_ref[:, lanes] = jnp.transpose(mixed * (1.0 / total)).astype(bf16)
            l_ref[head] = largest * log2_scale + jnp.log2(total)

    keys = BLOCK * len(segments)
    return launch(
        body,
        idx,
        arrays,
        [shaped((BLOCK, heads * HEAD), bf16), shaped((heads, 1, BLOCK), f32)],
        flops=4 * heads * BLOCK * keys * HEAD * 2,
        name=name,
    )


def attend_back(idx, queries, segments, katt, qatt, heads, logs, upstream, added, dtypes, name):
    arrays, *uses = attention_inputs(queries, segments, katt, qatt)
    count = len(arrays)
    inputs = arrays + [logs, upstream]
    for pairs in added:
        for pair in pairs:
            inputs.extend(pair)
    wide = (BLOCK, heads * HEAD)
    outputs = [shaped(wide, bf16)]
    for dtype in dtypes:
        outputs.extend([shaped(wide, dtype)] * 2)

    def body(s, *refs):
        rest = list(refs[count:])
        l_ref, go_ref = rest.pop(0), rest.pop(0)
        sums = []
        for pairs in added:
            sums.append([(rest.pop(0), rest.pop(0)) for unused in pairs])
        gq_ref = rest.pop(0)
        outs = list(zip(rest[0::2], rest[1::2]))

        @pl.loop(0, heads)
        def _(head):
            q, parts, qa = read_attention(refs, uses, queries, segments, head)
            lanes = pl.ds(pl.multiple_of(head * HEAD, HEAD), HEAD)
            log_total = l_ref[head]
            go = go_ref[:, lanes]
            chances, grads = [], []
            inner = jnp.zeros((1, BLOCK), f32)
            for kind, k, v, ka in parts:
                x = masked_scores(kind, k, q, ka, qa)
                chance = jnp.exp2(x * log2_scale - log_total)
                grad = dot_nt(v, go)
                inner = inner + jnp.sum(chance * grad, axis=0, keepdims=True)
                chances.append(chance)
                grads.append(grad)
            gq = jnp.zeros((HEAD, BLOCK), f32)
            for (kind, k, v, ka), chance, grad, pairs, out in zip(
                parts, chances, grads, sums, outs
            ):
                gl = (chance * (grad - inner)).astype(bf16)
                gk = dot_nn(gl, q) * score_scale
                gv = dot_nn(chance.astype(bf16), go)
                gq = gq + dot_tn(k, gl)
                for more_k, more_v in pairs:
                    gk = gk + more_k[:, lanes]
                    gv = gv + more_v[:, lanes]
                out[0][:, lanes] = gk.astype(out[0].dtype)
                out[1][:, lanes] = gv.astype(out[1].dtype)
            gq_ref[:, lanes] = jnp.transpose(gq * score_scale).astype(bf16)

    keys = BLOCK * len(segments)
    return launch(
        body,
        idx,
        inputs,
        outputs,
        flops=10 * heads * BLOCK * keys * HEAD * 2,
        vmem=8,
        name=name,
    )


def state_update(idx, pieces, write_pieces, state, retain, gain, weights, width, name):
    rows, features = state.shape
    count = len(pieces)
    project = weights is not None

    def body(s, *refs):
        refs = list(refs)
        piece_refs = [refs.pop(0) for unused in range(count)]
        w_refs = [refs.pop(0) for unused in range(count)]
        s_ref, r_ref = refs[:2]
        refs = refs[2:]
        if project:
            g_ref, p_ref, out_ref, n_ref, t_ref = refs
        else:
            (out_ref,) = refs

        @pl.loop(0, rows // TILE)
        def _(i):
            at = span(i * TILE)
            terms = [
                dot_nn(o_ref[at, :], w_ref[: o_ref.shape[1], :])
                for o_ref, w_ref in zip(piece_refs, w_refs)
            ]
            while len(terms) > 1:
                terms = [a + b for a, b in zip(terms[0::2], terms[1::2])]
            update = terms[0]
            keep = r_ref[...]
            following = keep * s_ref[at, :].astype(f32) + (1.0 - keep) * update
            out_ref[at, :] = following
            if project:
                normed = (unit_rows(following)[0] * g_ref[...]).astype(bf16)
                n_ref[at, :] = normed
                t_ref[at, :] = dot_nn(normed, p_ref[:, :width]).astype(bf16)

    inputs = list(pieces) + list(write_pieces) + [state, retain]
    outputs = [shaped((rows, features), f32)]
    if project:
        inputs += [gain, weights]
        outputs += [shaped((rows, features), bf16), shaped((rows, width), bf16)]
    return launch(
        body,
        idx,
        inputs,
        outputs,
        flops=2 * rows * features * (features + (width if project else 0)),
        name=name,
    )


def take_sum(i, s, refs, total):
    chip_ref, mine_ref, theirs_ref = refs
    steps = HALF // TILE
    at, inner = span(tile_start(i, s)), span(lax.rem(i, steps) * TILE)

    @pl.when(i < steps)
    def _():
        total[...] = chip_ref[at, :].astype(f32) + mine_ref[inner, :].astype(f32)

    @pl.when(i >= steps)
    def _():
        total[...] = chip_ref[at, :].astype(f32) + theirs_ref[inner, :].astype(f32)

    return total[...]


def chip_sum(idx, partial, other, name):
    rows, features = partial.shape
    tall = 32

    def body(s, a_ref, b_ref, sum_ref, own_ref):
        @pl.loop(0, rows // tall)
        def _(i):
            at = rows_of(i, 0, tall)
            sum_ref[at, :] = (a_ref[at, :].astype(f32) + b_ref[at, :].astype(f32)).astype(bf16)

        @pl.loop(0, HALF // tall)
        def _(i):
            own_ref[rows_of(i, 0, tall), :] = sum_ref[pl.ds(pl.multiple_of(s[1] * HALF + i * tall, tall), tall), :]

    return launch(
        body,
        idx,
        [partial, other],
        [shaped((rows, features), bf16), shaped((HALF, features), bf16)],
        name=name,
    )


def add_rows(i, ref, value):
    value = jnp.sum(value, axis=0, keepdims=True)

    @pl.when(i == 0)
    def _():
        ref[...] = value

    @pl.when(i != 0)
    def _():
        ref[...] = ref[...] + value


def project_back(idx, grads, weights, column, name):
    rows, width = grads[0].shape
    features = weights.shape[1]

    def body(s, *refs):
        *g_refs, w_ref, out_ref = refs

        @pl.loop(0, rows // TILE)
        def _(i):
            at = span(i * TILE)
            out = jnp.zeros((TILE, features), f32)
            for k, ref in enumerate(g_refs):
                first = column + k * width
                out = out + dot_nn(ref[at, :], w_ref[first : first + width, :])
            out_ref[at, :] = out.astype(bf16)

    return launch(
        body,
        idx,
        list(grads) + [weights],
        [shaped((rows, features), bf16)],
        flops=2 * rows * features * width * len(grads),
        name=name,
    )[0]


def state_back(idx, sums, state, following, retain, gain, write_own, name):
    rows, features = state.shape
    before = write_own is not None
    width = write_own.shape[1] // 2 if before else 10

    def body(s, *refs):
        refs = list(refs)
        total = refs.pop()
        sum_refs = [refs.pop(0) for unused in range(len(sums))]
        s_ref, r_ref, g_ref = refs[:3]
        refs = refs[3:]
        following_ref = refs.pop(0) if following is not None else None
        if before:
            w_ref, gs_ref, gain_ref, gu_ref, gos_ref = refs
        else:
            gs_ref, gain_ref = refs

        @pl.loop(0, rows // TILE)
        def _(i):
            at = span(tile_start(i, s))
            up = take_sum(i, s, sum_refs, total)
            unit, inverse = unit_rows(s_ref[at, :].astype(f32))
            out = unit_back(up, unit, inverse, g_ref[...])
            if following is not None:
                out = r_ref[...] * following_ref[at, :] + out
            gs_ref[at, :] = out
            add_rows(i, gain_ref, up * unit)
            if before:
                gu = ((1.0 - r_ref[...]) * out).astype(bf16)
                gu_ref[at, :] = gu
                gos_ref[at, :] = dot_nn(gu, w_ref[:, :width]).astype(bf16)

    inputs = list(sums) + [state, retain, gain]
    outputs = [shaped((rows, features), f32), shaped((1, features), f32)]
    if following is not None:
        inputs.append(following)
    if before:
        inputs.append(write_own)
        outputs += [shaped((rows, features), bf16), shaped((rows, width), bf16)]
    return launch(
        body,
        idx,
        inputs,
        outputs,
        scratch=[pltpu.VMEM((TILE, features), f32)],
        flops=2 * rows * features * width,
        name=name,
    )


def last_update_back(idx, retain, write_own, rows, name):
    features, width = write_own.shape[0], write_own.shape[1] // 2

    def body(s, r_ref, w_ref, gu_ref, gos_ref):
        gu = ((1.0 - r_ref[...]) * jnp.zeros((rows, features), f32)).astype(bf16)
        gu_ref[...] = gu
        gos_ref[...] = dot_nn(gu, w_ref[:, :width]).astype(bf16)

    return launch(
        body,
        idx,
        [retain, write_own],
        [shaped((rows, features), bf16), shaped((rows, width), bf16)],
        name=name,
    )


def gelu_both(a):
    root, cubic = 0.7978845608028654, 0.044715
    squared = a * a
    bent = jnp.tanh(root * (a + cubic * (squared * a)))
    rising = 0.5 * (1.0 + bent)
    slope = rising + (0.5 * root) * a * (1.0 - bent * bent) * (1.0 + (3.0 * cubic) * squared)
    return a * rising, slope


def output_forward(idx, number, pieces, out_pieces, tokens, gain, name):
    features = tokens.shape[1]
    count = len(pieces)

    def body(s, *refs):
        o_refs, w_refs = refs[:count], refs[count : 2 * count]
        t_ref, g_ref, x1_ref, xn_ref = refs[2 * count :]

        @pl.loop(0, BLOCK // TILE)
        def _(i):
            at = span(i * TILE)
            x1 = t_ref[span(i * TILE, number * BLOCK), :].astype(f32)
            for o_ref, w_ref in zip(o_refs, w_refs):
                x1 = x1 + dot_nn(o_ref[at, :], w_ref[o_ref.shape[1] :, :])
            x1_ref[at, :] = x1
            xn_ref[at, :] = (unit_rows(x1)[0] * g_ref[...]).astype(bf16)

    return launch(
        body,
        idx,
        list(pieces) + list(out_pieces) + [tokens, gain],
        [shaped((BLOCK, features), f32), shaped((BLOCK, features), bf16)],
        flops=2 * BLOCK * features * features,
        name=name,
    )


def dense_forward(idx, normed, dense, name):
    features = normed.shape[1]
    hidden = dense[1].shape[0]

    def body(s, n_ref, up_ref, down_ref, h_ref, slope_ref, part_ref):
        @pl.loop(0, BLOCK // TILE)
        def _(i):
            at = span(i * TILE)
            h, slope = gelu_both(dot_nn(n_ref[at, :], up_ref[:, :hidden]))
            h = h.astype(bf16)
            h_ref[at, :] = h
            slope_ref[at, :] = slope.astype(bf16)
            part_ref[at, :] = dot_nn(h, down_ref[...]).astype(bf16)

    return launch(
        body,
        idx,
        [normed, *dense],
        [
            shaped((BLOCK, hidden), bf16),
            shaped((BLOCK, hidden), bf16),
            shaped((BLOCK, features), bf16),
        ],
        flops=4 * BLOCK * features * hidden,
        name=name,
    )


def dense_part(idx, grads, up_t, name):
    rows, features = grads.shape[0], up_t.shape[1]

    def body(s, ga_ref, up_ref, part_ref):
        @pl.loop(0, rows // TILE)
        def _(i):
            at = span(i * TILE)
            part_ref[at, :] = dot_nn(ga_ref[at, :], up_ref[...]).astype(bf16)

    return launch(body, idx, [grads, up_t], [shaped((rows, features), bf16)], name=name)[0]


def dense_backward(idx, number, sums, x1, teacher, katt, slope, dense, name, with_part):
    features = x1.shape[1]
    up_t, both = dense
    hidden = up_t.shape[0]

    def body(s, *refs):
        refs = list(refs)
        total = refs.pop()
        sum_refs = [refs.pop(0) for unused in range(len(sums))]
        x_ref, t_ref, v_ref, slope_ref, up_ref, d_ref = refs[:6]
        gm_ref, ga_ref, loss_ref, *part_refs = refs[6:]

        @pl.loop(0, BLOCK // TILE)
        def _(i):
            start = tile_start(i, s)
            at, far = span(start), span(start, number * BLOCK)
            errors = x_ref[at, :] + take_sum(i, s, sum_refs, total) - t_ref[far, :].astype(f32)
            gy = v_ref[far, 2:3] * errors
            add_rows(i, loss_ref, gy * errors)
            gm = gy.astype(bf16)
            gm_ref[at, :] = gm
            ga = (dot_nn(gm, d_ref[:, hidden:]) * slope_ref[at, :].astype(f32)).astype(bf16)
            ga_ref[at, :] = ga
            for part_ref in part_refs:
                part_ref[at, :] = dot_nn(ga, up_ref[...]).astype(bf16)

    return launch(
        body,
        idx,
        list(sums) + [x1, teacher, katt, slope, up_t, both],
        [
            shaped((BLOCK, features), bf16),
            shaped((BLOCK, hidden), bf16),
            shaped((1, features), f32),
        ]
        + [shaped((BLOCK, features), bf16)] * with_part,
        scratch=[pltpu.VMEM((TILE, features), f32)],
        flops=4 * BLOCK * features * hidden,
        name=name,
    )


def output_backward(idx, sums, gy, x1, gain, out_own, name):
    features = x1.shape[1]
    width = out_own.shape[1] // 2

    def body(s, *refs):
        refs = list(refs)
        total = refs.pop()
        sum_refs = [refs.pop(0) for unused in range(len(sums))]
        gy_ref, x_ref, g_ref, w_ref, gp_ref, go_ref, gain_ref = refs

        @pl.loop(0, BLOCK // TILE)
        def _(i):
            at = span(tile_start(i, s))
            up = take_sum(i, s, sum_refs, total)
            unit, inverse = unit_rows(x_ref[at, :])
            gx = gy_ref[at, :].astype(f32) + unit_back(up, unit, inverse, g_ref[...])
            gp = gx.astype(bf16)
            gp_ref[at, :] = gp
            go_ref[at, :] = dot_nn(gp, w_ref[:, width:]).astype(bf16)
            add_rows(i, gain_ref, up * unit)

    return launch(
        body,
        idx,
        list(sums) + [gy, x1, gain, out_own],
        [
            shaped((BLOCK, features), bf16),
            shaped((BLOCK, width), bf16),
            shaped((1, features), f32),
        ],
        scratch=[pltpu.VMEM((TILE, features), f32)],
        flops=2 * BLOCK * features * width,
        name=name,
    )


def weight_grads(idx, groups, name, before=None, weight=40, vmem=8):
    features = groups[0][0][0].shape[1]
    inputs, specs, total, flops = [], [], 0, 0
    for parts in groups:
        for left, block, right in parts:
            rows = right.shape[0]
            inputs += [left, right]
            specs.append(pl.BlockSpec((rows, HALF), lambda i, block=block: (block, i)))
            specs.append(
                pl.BlockSpec(right.shape, lambda i: (0, 0), pipeline_mode=pl.Buffered(1))
            )
            flops += 2 * rows * features * right.shape[1]
        total += parts[0][2].shape[1]
    if before is not None:
        inputs.append(before)
        specs.append(pl.BlockSpec((HALF, total), lambda i: (i, 0)))

    def body(s, *refs):
        refs = list(refs)
        out_ref = refs.pop()
        before_ref = refs.pop() if before is not None else None
        at = 0
        for parts in groups:
            size = parts[0][2].shape[1]
            if before is None:
                out = jnp.zeros((HALF, size), f32)
            else:
                out = before_ref[:, at : at + size].astype(f32)
            for unused in parts:
                left, right = refs.pop(0), refs.pop(0)
                out = out + dot_tn(left[...], right[...])
            out_ref[:, at : at + size] = out.astype(bf16)
            at += size

    return pl.pallas_call(
        body,
        grid=(features // HALF,),
        in_specs=[pl.BlockSpec(memory_space=pltpu.SMEM)] + specs,
        out_specs=pl.BlockSpec((HALF, total), lambda i: (i, 0)),
        out_shape=pltpu.HBM((features, total), bf16),
        compiler_params=pltpu.CompilerParams(
            dimension_semantics=("arbitrary",), vmem_limit_bytes=vmem << 20
        ),
        cost_estimate=cost(weight * flops, inputs),
        name=name,
    )(idx, *inputs)


def unpack_grads(packed, widths, flipped, name):
    rows = packed.shape[0]

    def body(p_ref, *out_refs):
        at = 0
        for size, flip, out_ref in zip(widths, flipped, out_refs):
            values = p_ref[:, at : at + size].astype(f32)
            out_ref[...] = jnp.transpose(values) if flip else values
            at += size

    return pl.pallas_call(
        body,
        in_specs=[pl.BlockSpec(memory_space=pltpu.VMEM)],
        out_specs=[pl.BlockSpec(memory_space=pltpu.VMEM)] * len(widths),
        out_shape=[
            shaped((size, rows) if flip else (rows, size), f32)
            for size, flip in zip(widths, flipped)
        ],
        compiler_params=pltpu.CompilerParams(vmem_limit_bytes=8 << 20),
        cost_estimate=cost(0, [packed]),
        name=name,
    )(packed)


def arrange_rows(idx, pieces, count, name):
    rows, features = pieces[0].shape
    rows = rows // count

    def body(s, *refs):
        ins, outs = refs[: len(pieces)], refs[len(pieces) :]
        for k, ref in enumerate(ins):
            for j, out_ref in enumerate(outs):
                out_ref[rows_of(s[0] ^ k, 0, rows), :] = ref[j * rows : (j + 1) * rows, :]

    return launch(
        body,
        idx,
        pieces,
        [shaped((rows * len(pieces), features), pieces[0].dtype)] * count,
        name=name,
    )


def turn(idx, values, first, count, name):
    rows = values.shape[0]
    wide = 256

    def body(s, v_ref, out_ref):
        @pl.loop(0, count // wide)
        def _(i):
            lanes = pl.ds(pl.multiple_of(first + i * wide, HEAD), wide)
            out_ref[rows_of(i, 0, wide), :] = jnp.transpose(v_ref[:, lanes])

    return launch(body, idx, [values], [shaped((count, rows), values.dtype)], name=name)[0]


def arrange_columns(idx, blocks, across, name):
    rows, width = blocks[0].shape
    depth = len(blocks)

    def body(s, *refs):
        out_ref = refs[-1]
        for k in range(depth):
            level = lax.rem(s[3] + depth - k, depth)
            out_ref[rows_of(2 * level + s[4], 0, rows), :] = refs[k][...]
            out_ref[rows_of(2 * level + 1 - s[4], 0, rows), :] = refs[depth + k][...]

    return launch(
        body,
        idx,
        list(blocks) + list(across),
        [shaped((2 * depth * rows, width), blocks[0].dtype)],
        name=name,
    )[0]


def split_grads(idx, groups, depth, name):
    features = groups[0][0][0].shape[1]
    rows = features // (2 * depth)
    total = sum(parts[0][2].shape[1] for parts in groups)
    inputs = []

    def place(array):
        for k, known in enumerate(inputs):
            if known is array:
                return k
        inputs.append(array)
        return len(inputs) - 1

    uses = [[(place(a), block, place(c)) for a, block, c in parts] for parts in groups]

    def body(s, *refs):
        *ins, theirs_ref, mine_ref, held = refs

        @pl.loop(0, depth)
        def _(i):
            lanes = pl.ds(pl.multiple_of(i * 2 * rows, 2 * rows), 2 * rows)
            at = 0
            for parts in uses:
                size = ins[parts[0][2]].shape[1]
                out = jnp.zeros((2 * rows, size), f32)
                for left, block, right in parts:
                    count = ins[right].shape[0]
                    tall = slice(block * count, (block + 1) * count)
                    out = out + dot_tn(ins[left][tall, lanes], ins[right][...])
                held[:, at : at + size] = out.astype(bf16)
                at += size
            mine_ref[rows_of(i, 0, rows), :] = held[rows_of(s[4], 0, rows), :]
            theirs_ref[rows_of(i, 0, rows), :] = held[rows_of(1 - s[4], 0, rows), :]

    return launch(
        body,
        idx,
        inputs,
        [shaped((depth * rows, total), bf16)] * 2,
        scratch=[pltpu.VMEM((2 * rows, total), bf16)],
        name=name,
    )


def pair_blocks(idx, mine, got, depth, name):
    rows, width = mine.shape[0] // depth, mine.shape[1]

    def body(s, mine_ref, got_ref, *out_refs):
        for k, ref in enumerate(out_refs):
            at = rows_of(lax.rem(s[3] + k, depth), 0, rows)
            ref[...] = (mine_ref[at, :].astype(f32) + got_ref[at, :].astype(f32)).astype(ref.dtype)

    return launch(
        body,
        idx,
        [mine, got],
        [shaped((rows, width), f32)] + [shaped((rows, width), bf16)] * (depth - 1),
        name=name,
    )


def line_sum(idx, own, others, widths, flipped, name):
    rows = own.shape[0]

    def body(s, own_ref, *refs):
        ins, outs = refs[: len(others)], refs[len(others) :]
        total = own_ref[...]
        for ref in ins:
            total = total + ref[...].astype(f32)
        at = 0
        for size, flip, out_ref in zip(widths, flipped, outs):
            values = total[:, at : at + size]
            out_ref[...] = jnp.transpose(values) if flip else values
            at += size

    return launch(
        body,
        idx,
        [own] + list(others),
        [
            shaped((size, rows) if flip else (rows, size), f32)
            for size, flip in zip(widths, flipped)
        ],
        name=name,
    )


def pack(idx, arrays, takes, shapes, name):
    flipped = [take for take in takes if take[-1]]

    def body(s, *refs):
        ins, outs = refs[: len(arrays)], refs[len(arrays) : len(arrays) + len(shapes)]
        *held, sems = refs[len(arrays) + len(shapes) :]
        copies, spare = [], list(held)
        for j, (k, row, col, rows, cols, out, place, flip) in enumerate(takes):
            at = pl.ds(0, rows) if row is None else rows_of(s[row], 0, rows)
            to = pl.ds(0, cols) if col is None else rows_of(s[col], 0, cols)
            if flip:
                target = spare.pop(0)
            else:
                target = outs[out].at[pl.ds(place[0], rows), pl.ds(place[1], cols)]
            copies.append(pltpu.make_async_copy(ins[k].at[at, to], target, sems.at[j]))
            copies[-1].start()
        spare = list(held)
        for copy, (k, row, col, rows, cols, out, place, flip) in zip(copies, takes):
            copy.wait()
            if flip:
                to = slice(place[1], place[1] + rows)
                outs[out][place[0] : place[0] + cols, to] = jnp.transpose(spare.pop(0)[...])

    return pl.pallas_call(
        body,
        in_specs=[pl.BlockSpec(memory_space=pltpu.SMEM)]
        + [pl.BlockSpec(memory_space=pl.ANY)] * len(arrays),
        out_specs=[pl.BlockSpec(memory_space=pltpu.VMEM)] * len(shapes),
        out_shape=[shaped(a, bf16) for a in shapes],
        scratch_shapes=[pltpu.VMEM((take[3], take[4]), bf16) for take in flipped]
        + [pltpu.SemaphoreType.DMA((len(takes),))],
        compiler_params=pltpu.CompilerParams(vmem_limit_bytes=8 << 20),
        cost_estimate=cost(0, arrays),
        name=name,
    )(idx, *[pltpu.with_memory_space_constraint(a, pltpu.HBM) for a in arrays])


def input_rows(idx, own, arrived, gps, tokens, gain, name):
    rows, features = tokens.shape
    count = len(gps)

    def body(s, *refs):
        own_refs, far_refs, gp_refs = refs[:count], refs[count : 2 * count], refs[2 * count : 3 * count]
        t_ref, g_ref, out_ref, gain_ref = refs[3 * count :]
        unit, inverse = unit_rows(t_ref[...].astype(f32))
        for b in range(count):

            @pl.when(s[2] // 2 == b)
            def _():
                at = rows_of(s[1])
                up = own_refs[b][at, :].astype(f32) + far_refs[b][...].astype(f32)
                base = gp_refs[b][rows_of(s[1]), :].astype(f32)
                out_ref[...] = base + unit_back(up, unit, inverse, g_ref[...])
                gain_ref[...] = jnp.sum(up * unit, axis=0, keepdims=True)

    return launch(
        body,
        idx,
        list(own) + list(arrived) + list(gps) + [tokens, gain],
        [shaped((rows, features), f32), shaped((1, features), f32)],
        name=name,
    )


def per_device(
    block_input,
    state_start,
    teacher,
    valid_mask,
    segment,
    image_offset,
    retain,
    to_query,
    to_key,
    to_value,
    to_output,
    to_hidden,
    to_model,
    state_query,
    state_key,
    state_value,
    state_write,
    first_gain,
    second_gain,
    state_gain,
):
    row_devices = lax.axis_size("row")
    col_devices = lax.axis_size("col")
    row_index = lax.axis_index("row")
    col_index = lax.axis_index("col")
    local_rows, features = block_input.shape[1:]
    length = local_rows * row_devices
    width = to_query.shape[1]
    heads = width // HEAD
    hidden = to_hidden.shape[1] // row_devices
    nblocks = length // BLOCK
    pairs = row_devices == 4 and 2 * local_rows == BLOCK
    lines = pairs and col_devices == 8
    core_pairs = [(k, k ^ 1) for k in range(row_devices)]
    chip_pairs = [(k, k ^ 2) for k in range(row_devices)] if pairs else None
    if pairs:
        idx = jnp.stack([row_index, row_index % 2, row_index, col_index // 2, col_index % 2])
    else:
        idx = jnp.stack([0, 1, row_index, 0, 0])
    idx = idx.astype(jnp.int32)

    def to_core(x):
        return lax.ppermute(x, "row", core_pairs)

    def to_chip(x):
        return lax.ppermute(x, "row", chip_pairs)

    def row_moves(x):
        if not pairs:
            stacked = lax.all_gather(x, "row", axis=0, tiled=False)
            return [stacked[k] for k in range(row_devices)]
        return [x, to_core(x), to_chip(x)]

    def row_pieces(moved, *ties):
        if not pairs:
            return moved
        x, near, far = moved
        return [x, near, far, to_core(after(far, *ties))]

    depth_z = col_devices // 2

    def along(v, step):
        levels = range(depth_z)
        moves = [(2 * z + y, 2 * ((z + step) % depth_z) + y) for z in levels for y in range(2)]
        return lax.ppermute(v, "col", moves)

    def across(v):
        return lax.ppermute(v, "col", [(k, k ^ 1) for k in range(col_devices)])

    class Columns:
        def __init__(self, x, name):
            self.name = name
            if lines:
                self.blocks = [x] + [along(x, k) for k in range(1, depth_z)]
                self.crossed = [across(x)]
            else:
                self.whole = lax.all_gather(x, "col", axis=0, tiled=True)

        def cross(self, k, *ties):
            if lines:
                self.crossed.append(across(after(self.blocks[k], *ties)))

        def landed(self, k):
            return [self.blocks[k], self.crossed[k - 1]] if lines else []

        def result(self, *ties):
            if lines:
                order = after(idx, *ties)
                return arrange_columns(order, self.blocks, self.crossed, self.name)
            return self.whole

    class Scattered:
        def __init__(self, groups, name, *ties):
            self.name, self.widths = name, [parts[0][2].shape[1] for parts in groups]
            if lines:
                order = after(idx, *ties) if ties else idx
                theirs, self.mine = split_grads(order, groups, depth_z, name)
                self.got = across(theirs)
            else:
                packed = weight_grads(idx, groups, name)
                self.whole = lax.psum_scatter(packed, "col", scatter_dimension=0, tiled=True)

        def send(self, *ties):
            if lines:
                mine = after(self.mine, *ties) if ties else self.mine
                self.own, *blocks = pair_blocks(idx, mine, self.got, depth_z, f"{self.name}_y")
                self.far = [along(block, k + 1) for k, block in enumerate(blocks)]

        def result(self, flipped):
            if lines:
                return line_sum(idx, self.own, self.far, self.widths, flipped, f"{self.name}_z")
            return unpack_grads(self.whole, self.widths, flipped, f"{self.name}_z")

    class RowSum:
        def __init__(self, partial, name, receiver=None, ties=(), near=None):
            if pairs:
                order = after(idx, *ties) if ties else idx
                near = to_core(partial) if near is None else near
                self.chip, own = chip_sum(order, partial, near, name)
                moves = [m for m in chip_pairs if receiver is None or m[1] // 2 == receiver]
                self.far = lax.ppermute(own, "row", moves)
            else:
                self.chip = lax.psum(partial, "row")

        def result(self, *ties):
            if pairs:
                return [self.chip, self.far, to_core(after(self.far, *ties))]
            none = jnp.zeros((HALF, features), bf16)
            return [self.chip, none, none]

    def all_sum(x, *held):
        hops = 0
        for axis, size in (("row", row_devices), ("col", col_devices)):
            step = 1
            while step < size:
                if hops == 2 and held:
                    x = after(x, *held)
                x = x + lax.ppermute(x, axis, [(k, k ^ step) for k in range(size)])
                step *= 2
                hops += 1
        return x

    depth = to_query.shape[0]
    (near,) = pack(
        idx,
        [state_query, state_key, state_value, to_query, to_key, to_value],
        [(k, None, None, depth, width, 0, (0, k * width), False) for k in range(6)],
        [(depth, 6 * width)],
        "pack_near",
    )
    near = lax.all_gather(near, "col", axis=0, tiled=True)
    rows_in, mid, far_weights = pack(
        idx,
        [state_write, to_output, to_hidden, to_model, block_input[0], teacher[0]],
        [
            (4, None, None, local_rows, features, 0, (0, 0), False),
            (5, None, None, local_rows, features, 0, (local_rows, 0), False),
            (0, 2, None, width, depth, 1, (0, 0), True),
            (1, None, None, width, depth, 1, (0, width), True),
            (2, None, 2, depth, hidden, 2, (0, 0), False),
            (3, 2, None, hidden, depth, 2, (0, hidden), True),
        ],
        [(2 * local_rows, features), (depth, 2 * width), (depth, 2 * hidden)],
        "pack_rest",
    )
    rows_moved = row_moves(rows_in) if pairs else None
    mid = Columns(mid, "mid")
    for k in range(1, depth_z):
        mid.cross(k)
    mid = mid.result()
    mid_n = turn(idx, mid, 0, 2 * width, "mid_turn")
    held = [mid_n] + (rows_moved[2:] if pairs else [])
    dense = lax.all_gather(after(far_weights, *held), "col", axis=0, tiled=True)
    mid_moved = row_moves(mid_n)
    if pairs:
        tokens, teacher_all = arrange_rows(idx, row_pieces(rows_moved), 2, "tokens")
    else:
        tokens, teacher_all = [
            lax.all_gather(x[0], "row", axis=0, tiled=True) for x in (block_input, teacher)
        ]

    valid_row = lax.dynamic_index_in_dim(valid_mask, col_index, 0, keepdims=False)
    segment_row = segment[0]
    numbers = jnp.arange(nblocks, dtype=jnp.int32)
    places = jnp.arange(length, dtype=jnp.int32)
    starts = numbers * BLOCK + image_offset[0]
    inside = (places[:, None] >= starts[None, :]) & (places[:, None] < starts[None, :] + PIECE)
    piece = jnp.sum(jnp.where(inside, numbers[None, :] + 1, 0), axis=1) - 1
    valid_count = jnp.sum(valid_mask.astype(f32))
    total_tokens = f32(length * col_devices)
    weight_of_row = total_tokens / valid_count * valid_row.astype(f32)
    document = segment_row.astype(f32)
    nothing = jnp.zeros_like(document)
    katt = jnp.stack(
        [jnp.where(valid_row > 0, document, -1.0), piece.astype(f32), weight_of_row, nothing],
        axis=1,
    )
    qatt = jnp.stack(
        [document, jnp.where(piece >= 0, piece, -2).astype(f32), nothing, nothing], axis=0
    )
    retain2 = retain[None]
    first_gain2, second_gain2, state_gain2 = first_gain[None], second_gain[None], state_gain[None]

    def token_segments(number, trio):
        found = []
        if number > 0:
            found.append(("prev", token_heads, number - 1, width, 2 * width, number - 1))
        found.append(("own", token_heads, number, width, 2 * width, number))
        found.append(("free", trio, 0, width, 2 * width, None))
        return found

    def state_segments(number, trio):
        return [
            ("valid", token_heads, number, width, 2 * width, number),
            ("free", trio, 0, width, 2 * width, None),
        ]

    current = state_start[0]
    near_t = turn(idx, near, 0, 6 * width, "near_turn")
    state_low, trio = norm_project(after(idx, near_t), current, state_gain2, near, 0, 3 * width, "state_proj")
    first_low, token_heads = norm_project(
        idx, tokens, first_gain2, near, 3 * width, 3 * width, "token_proj"
    )
    states, lows, trios = [], [], []
    state_out, state_logs, token_out, token_logs = [], [], [], []
    x1s, second_lows, hiddens, slopes, dense_sums = [], [], [], [], []
    state_pieces, token_pieces = [], []
    end = nblocks - 1

    def state_part(b):
        mixed, logs = attend(
            idx,
            (trios[b], 0, 0),
            state_segments(b, trios[b]),
            katt,
            None,
            heads,
            f"state_attend{b}",
        )
        state_out.append(mixed)
        state_logs.append(logs)
        state_pieces.append(row_moves(mixed) if b < nblocks - 1 else None)

    for b in range(nblocks):
        states.append(current)
        lows.append(state_low)
        trios.append(trio)
        last = b + 1 == nblocks
        if not last:
            state_part(b)
        mixed, logs = attend(
            idx, (token_heads, b, 0), token_segments(b, trio), katt, qatt, heads, f"token_attend{b}"
        )
        if b == 0:
            mid_pieces = row_pieces(mid_moved, mixed)
        token_out.append(mixed)
        token_logs.append(logs)
        token_pieces.append(row_moves(mixed))
        if not last:
            current, state_low, trio = state_update(
                idx,
                row_pieces(state_pieces[b], mixed),
                mid_pieces,
                current,
                retain2,
                state_gain2,
                near,
                3 * width,
                f"update{b}",
            )
            token_pieces[b] = row_pieces(token_pieces[b], trio)
    state_part(nblocks - 1)
    token_pieces[-1] = row_pieces(token_pieces[-1], state_out[-1])

    def state_back_part(b, gos_state, own, free, dtype):
        return attend_back(
            idx,
            (trios[b], 0, 0),
            state_segments(b, trios[b]),
            katt,
            None,
            heads,
            state_logs[b],
            gos_state,
            [own, free],
            [dtype, dtype],
            f"state_back{b}",
        )

    def token_back_part(b, own, free, dtype, upstream):
        segments = token_segments(b, trios[b])
        added = ([[]] if b > 0 else []) + [own, free]
        dtypes = ([f32] if b > 0 else []) + [dtype, dtype]
        found = attend_back(
            idx,
            (token_heads, b, 0),
            segments,
            katt,
            qatt,
            heads,
            token_logs[b],
            upstream,
            added,
            dtypes,
            f"token_back{b}",
        )
        return found[0], found[-4:], (found[1], found[2]) if b > 0 else None

    gus = [None] * nblocks
    gms, gas, losses, gps, gos, second_sums = [], [], [], [], [], []
    second_back = []
    for b in range(nblocks):
        x1, low = output_forward(
            idx, b, token_pieces[b], mid_pieces, tokens, second_gain2, f"out{b}"
        )
        x1s.append(x1)
        second_lows.append(low)
    down = turn(after(idx, state_out[-1], *second_lows), dense, hidden, hidden, "down_turn")
    order = idx
    for b in range(nblocks):
        h, slope, partial = dense_forward(order, second_lows[b], (dense, down), f"dense{b}")
        hiddens.append(h)
        slopes.append(slope)
        ties = []
        if b == 0:
            up_t = turn(after(idx, h), dense, 0, hidden, "up_turn")
            ties.append(up_t)
        if b == end:
            late_mid = after(mid, h)
            gus[end], gos_state = last_update_back(idx, retain2, late_mid, NS, "last_back")
            state_found = state_back_part(end, gos_state, [], [], f32)
            ties.append(state_found[0])
        dense_sums.append(RowSum(partial, f"dense_sum{b}", ties=ties))
        order = after(idx, dense_sums[b].chip)

    early_grads, partials = [], []
    ready = teacher_all
    for b in range(nblocks):
        hides = [hiddens[end], state_found[0]] if b == 0 else [gms[b - 1]] + early_grads
        gm, ga, loss, *partial = dense_backward(
            idx,
            b,
            dense_sums[b].result(*hides),
            x1s[b],
            ready,
            katt,
            slopes[b],
            (up_t, dense),
            f"back{b}",
            b < end,
        )
        partial = partial[0] if b < end else None
        gms.append(gm)
        gas.append(ga)
        losses.append(loss)
        if b < end:
            early_grads = [
                weight_grads(
                    idx,
                    [[(second_lows[b], 0, ga)], [(gm, 0, hiddens[b])]],
                    f"dense_grads{b}",
                    *early_grads,
                )
            ]
        partials.append((partial, to_core(partial) if pairs and b < end else None))
        ready = after(teacher_all, partials[b][1]) if pairs and b < end else teacher_all
        if b > 0:
            part, near_part = partials[b - 1]
            second_back.append(
                RowSum(part, f"back_sum{b - 1}", ties=[gm], near=near_part)
            )
    dense_grads = weight_grads(
        idx,
        [[(second_lows[end], 0, gas[end])], [(gms[end], 0, hiddens[end])]],
        "dense_grads",
        *early_grads,
    )
    filled = [dense_grads]
    ties = [dense_grads] + [back.far for back in second_back] if pairs else []
    held = [back.chip for back in second_back] if pairs else []
    partial = dense_part(after(idx, dense_grads, *held), gas[end], up_t, "back_part")
    second_back.append(RowSum(partial, f"back_sum{end}", ties=ties))
    dense_grads = lax.psum_scatter(dense_grads, "col", scatter_dimension=0, tiled=True)

    token_found = [None] * nblocks
    for b in range(nblocks):
        gp, go, gain_sum = output_backward(
            idx,
            second_back[b].result(*(filled if b == end else [gms[end]])),
            gms[b],
            x1s[b],
            second_gain2,
            mid,
            f"out_back{b}",
        )
        gps.append(gp)
        gos.append(go)
        second_sums.append(gain_sum)
        if b < end:
            token_found[b] = token_back_part(b, [], [], f32, go)
            filled.append(token_found[b][0])
    trio_grads = [None] * nblocks
    token_grads = [None] * nblocks
    first_sums = [None] * nblocks
    gain_sums = []
    grad_next = None
    gqs, gk, gv, gks, gvs = state_found
    gq, (gk, gv, gks, gvs), key_part = token_back_part(
        end, [(gk, gv)], [(gks, gvs)], bf16, gos[end]
    )
    state_pieces[-1] = row_moves(after(state_out[-1], gos[end]))
    gqs = after(gqs, state_pieces[-1][2])
    trio_grads[end] = (gqs, gks, gvs)
    token_grads[end] = (gq, gk, gv)
    for b in reversed(range(nblocks)):
        order = idx
        if b == 0:

            def state_group(k):
                return [(lows[c], 0, trio_grads[c][k]) for c in range(nblocks)]

            def token_group(k):
                return [(first_low, c, token_grads[c][k]) for c in range(nblocks)]

            write_group = [(gu, 0, out) for gu, out in zip(gus, state_out)]
            late_grads = weight_grads(
                idx,
                [state_group(k) for k in range(3)] + [token_group(1), token_group(2)],
                "late_grads",
                weight=115,
                vmem=12,
            )
            order = after(idx, late_grads)
            rest_grads = Scattered(
                [token_group(0), [(gp, 0, out) for gp, out in zip(gps, token_out)], write_group],
                "rest_grads",
                late_grads,
            )
            late_grads = lax.psum_scatter(late_grads, "col", scatter_dimension=0, tiled=True)
        trio_sum = RowSum(
            project_back(order, trio_grads[b], near_t, 0, f"trio_back{b}"),
            f"trio_sum{b}",
        )
        hides = []
        if b == end:
            (final_state,) = state_update(
                idx,
                row_pieces(state_pieces[-1], gq),
                mid_pieces,
                current,
                retain2,
                None,
                None,
                0,
                "update_last",
            )
            hides.append(final_state)
        first_sums[b] = project_back(idx, token_grads[b], near_t, 3 * width, f"first_back{b}")
        hides.append(first_sums[b])
        first_sums[b] = RowSum(first_sums[b], f"first_sum{b}", b) if pairs else first_sums[b]
        if b > 0:
            grad_next, gain_sum, gus[b - 1], gos_state = state_back(
                idx,
                trio_sum.result(*hides),
                states[b],
                grad_next,
                retain2,
                state_gain2,
                mid,
                f"chain_back{b}",
            )
            gq, (gk, gv, gks, gvs), next_part = token_found[b - 1]
            gqs, gk, gv, gks, gvs = state_back_part(
                b - 1, gos_state, [(gk, gv), key_part], [(gks, gvs)], bf16
            )
            key_part = next_part
            trio_grads[b - 1] = (gqs, gks, gvs)
            token_grads[b - 1] = (gq, gk, gv)
        else:
            grad_next, gain_sum = state_back(
                idx,
                trio_sum.result(*hides),
                states[b],
                grad_next,
                retain2,
                state_gain2,
                None,
                "chain_back0",
            )
        gain_sums.append(gain_sum)

    rest_grads.send(grad_next)

    upper_grad, lower_grad = unpack_grads(
        dense_grads, [hidden, hidden], [False, True], "unpack_dense"
    )
    order = after(idx, upper_grad)

    if pairs:
        own_rows = [first.chip for first in first_sums]
        arrived = [first.far for first in first_sums]
        input_grad, first_sum = input_rows(
            order, own_rows, arrived, gps, block_input[0], first_gain2, "input_rows"
        )
        first_sum = first_sum[0]
    else:
        both = jnp.concatenate(first_sums)
        grad_first = lax.psum_scatter(both, "row", scatter_dimension=0, tiled=True).astype(f32)
        own_gx1 = lax.dynamic_slice_in_dim(
            jnp.concatenate(gps), row_index * local_rows, local_rows
        ).astype(f32)
        unit, inverse = unit_rows(block_input[0].astype(f32))
        input_grad = own_gx1 + unit_back(grad_first, unit, inverse, first_gain2)
        first_sum = jnp.sum(grad_first * unit, axis=0)

    share = 1.0 / row_devices
    sums = jnp.stack(
        [
            sum(losses)[0] * share,
            first_sum,
            sum(second_sums)[0] * share,
            sum(gain_sums)[0] * share,
        ]
    )
    if lines:
        sums = after(sums, rest_grads.own)
    summed = all_sum(sums, *(rest_grads.far if lines else []))
    total_loss = jnp.sum(summed[0]) / (2.0 * total_tokens)

    late = unpack_grads(late_grads, [width] * 5, [False] * 5, "unpack_late")
    rest = rest_grads.result([False, True, True])

    return (
        total_loss,
        final_state[None],
        input_grad[None],
        grad_next[None],
        rest[0],
        late[3],
        late[4],
        rest[1],
        upper_grad,
        lower_grad,
        late[0],
        late[1],
        late[2],
        rest[2],
        summed[1],
        summed[2],
        summed[3],
    )


def solution(mesh):
    in_specs = (
        P("col", "row", None),
        P("col", None, None),
        P("col", "row", None),
        P(),
        P("col", None),
        P("col", None),
        P(),
        P("col", "row"),
        P("col", "row"),
        P("col", "row"),
        P("row", "col"),
        P("col", None),
        P(None, "col"),
        P("col", "row"),
        P("col", "row"),
        P("col", "row"),
        P(None, "col"),
        P(),
        P(),
        P(),
    )
    out_specs = (
        P(),
        P("col", None, None),
        P("col", "row", None),
        P("col", None, None),
        P("col", "row"),
        P("col", "row"),
        P("col", "row"),
        P("row", "col"),
        P("col", "row"),
        P("row", "col"),
        P("col", "row"),
        P("col", "row"),
        P("col", "row"),
        P("row", "col"),
        P(),
        P(),
        P(),
    )
    return jax.shard_map(
        per_device, mesh=mesh, in_specs=in_specs, out_specs=out_specs, check_vma=False
    )
```
